32 devices in a mesh: dp: 8 (over z, x), seq: 4 (over y, core).
Axes of the slice: x: 2, y: 2, z: 4, core: 2. Of those that a mesh axis runs over, the one named last changes fastest.
Arguments:
- clips_in: bfloat16 [32, 8, 196, 768], P('dp', 'seq'), may hold values from -6 to 6
- cotangent: bfloat16 [32, 8, 196, 768], P('dp', 'seq'), may hold values from -6 to 6
- clip_live: int32 [32], P('dp'), may hold values 0 or 1
- weights_in: bfloat16 [7680, 768], P(('dp', 'seq')), may hold values from -0.21875 to 0.21875
- weights_out: bfloat16 [5376, 768], P(('dp', 'seq')), may hold values from -0.75 to 0.75, as said below
- norm_gain: bfloat16 [3, 768], P(None, ('dp', 'seq')), may hold values from 0.25 to 1.75
- shift_rows: bfloat16 [10, 768], P(None, ('dp', 'seq')), may hold values from -1.796875 to 1.796875
- dense_shift: bfloat16 [768], P(('dp', 'seq')), may hold values from -1.796875 to 1.796875
Outputs:
- clips_out: bfloat16 [32, 8, 196, 768], P('dp', 'seq')
- grad_clips: float32 [32, 8, 196, 768], P('dp', 'seq')
- grad_in_rows: float32 [7680, 768], P(('dp', 'seq'))
- grad_out_rows: float32 [5376, 768], P(('dp', 'seq'))
- grad_gain: float32 [3, 768], P(None, ('dp', 'seq'))
- grad_shift: float32 [10, 768], P(None, ('dp', 'seq'))
- grad_dense_shift: float32 [768], P(('dp', 'seq'))
The draws below stay inside these ranges and needn't reach their ends.
Inputs may be any that keep to these rules, and one draw needn't show every extreme that they name: `clip_live`: 1 marks a clip slot that holds a clip, 0 an empty slot whose gradient is zero. `weights_out`: entries are scaled by their block's fan-in and lie within the stated bound.
All inputs are finite; a program needn't handle non-finite values. No bound on the sum of `clip_live` on one device may be relied on, other than what follows from the above.
Results may differ from the reference program's by a relative error of at most 0.023.
Values may be sent and summed in bfloat16 or wider, within the bound.
No kernel may reach another device: no remote copies, remote signals or barrier semaphores. Data moves between devices by JAX's collectives and lax.ppermute only.
A program may use at most 320 MiB of HBM per device.

```python
import math
import jax
import jax.numpy as jnp
from jax import lax

D = 768
HEADS = 12
HEAD_DIM = 64
FF = 3072
FRAMES = 8
PATCHES = 196
CLIPS = 32
IN_ROWS = 7680
SHIFT_ROWS = 10


def draw_weights_out(key, part):
    row_count = 3 * D + FF
    row_index = jnp.arange(row_count)[:, None]
    factor = jnp.where(row_index < D, 2.0 / math.sqrt(D), jnp.where(row_index < 2 * D, 1.0 / math.sqrt(D), jnp.where(row_index < 3 * D, 8.0 / math.sqrt(D), 1.5 / math.sqrt(FF))))
    sample = jax.random.normal(key, (row_count, D), jnp.float32)
    return jnp.clip(sample * factor, -0.75, 0.75).astype(jnp.bfloat16)


def plant(entries, stream_key, smallest, high):
    index_at = [jax.random.randint(jax.random.fold_in(stream_key, axis), (), 0, length) for axis, length in enumerate(entries.shape)]
    longest = entries.shape.index(max(entries.shape))
    neighbour = index_at[:longest] + [(index_at[longest] + 1) % entries.shape[longest]] + index_at[longest + 1:]
    return entries.at[tuple(index_at)].set(smallest).at[tuple(neighbour)].set(high)


def shard_levels(rng, dims, shards, smallest, top_value):
    loudness, own = 1.0, jax.random.fold_in(rng, 6)
    for position, parts in shards:
        steps = jnp.exp(jax.random.uniform(jax.random.fold_in(own, position), (parts,), jnp.float32, smallest / len(shards), top_value / len(shards)))
        loudness = loudness * jnp.repeat(steps, dims[position] // parts).reshape([-1 if axis == position else 1 for axis in range(len(dims))])
    return loudness


def gaussian(key, extent, deviation, bound, cuts=(), kind=jnp.bfloat16):
    array = jax.random.normal(key, extent, jnp.float32) * deviation
    if len(cuts) > 0:
        array = shard_levels(key, extent, cuts, -0.22, 0.18) * array
    return jnp.clip(array, min=-bound, max=bound).astype(kind)


def setup_inputs(seed: int = 0) -> dict:
    arg_keys = jax.random.split(jax.random.key(seed), 9)
    return {
        "clips_in": gaussian(arg_keys[0], (CLIPS, FRAMES, PATCHES, D), 1.0, 6.0, ((0, 8), (1, 4))),
        "cotangent": gaussian(arg_keys[1], (CLIPS, FRAMES, PATCHES, D), 1.0, 6.0, ((0, 8), (1, 4))),
        "clip_live": plant((jax.random.randint(arg_keys[2], (CLIPS,), 0, 4) < 3).astype(jnp.int32), jax.random.fold_in(arg_keys[2], 1), 0, 1),
        "weights_in": gaussian(arg_keys[3], (IN_ROWS, D), D ** -0.5, 0.21875, ((0, 32),)),
        "weights_out": draw_weights_out(jax.random.fold_in(arg_keys[8], 71), 0),
        "norm_gain": jnp.clip(1.0 + 0.15 * jax.random.normal(arg_keys[5], (3, D), jnp.float32), 0.25, 1.75).astype(jnp.bfloat16),
        "shift_rows": gaussian(arg_keys[6], (SHIFT_ROWS, D), 0.3, 1.796875, ((1, 32),)),
        "dense_shift": gaussian(arg_keys[7], (D,), 0.3, 1.796875, ((0, 32),)),
    }


@jax.custom_vjp
def low(v):
    return lax.optimization_barrier(v.astype(jnp.bfloat16)).astype(jnp.float32)

@jax.custom_vjp
def low_back(v):
    return v

def low_keep(v):
    return (low(v), None)

def low_pass(kept, grad):
    return (grad,)

def back_keep(v):
    return (v, None)

def back_low(kept, grad):
    return (low(grad),)
low.defvjp(low_keep, low_pass)
low_back.defvjp(back_keep, back_low)
EPSILON = 1e-06
PRECISE = lax.Precision.HIGHEST

def layer_norm(values, gains, shifts):
    centre = values - lax.optimization_barrier(jnp.mean(values, axis=-1, keepdims=True))
    spread = lax.optimization_barrier(jnp.mean(centre * centre, axis=-1, keepdims=True))
    return centre * lax.rsqrt(spread + EPSILON) * gains + shifts

def product(left, right):
    return jnp.dot(left, right, precision=PRECISE, preferred_element_type=jnp.float32)

def attend(project, score_spec, apply_spec):
    queries = project[:, :, 0]
    key_rows = project[:, :, 1]
    values = project[:, :, 2]
    scaling = project.shape[-1] ** (-0.5)
    scores = low_back(jnp.einsum(score_spec, queries, key_rows, precision=PRECISE) * scaling)
    weights = low(jax.nn.softmax(scores, axis=-1))
    return low_back(low(jnp.einsum(apply_spec, weights, values, precision=PRECISE)))

def layer(params, clip_now):
    weights_in, weights_out, gains, shifts, dense_bias = params
    model_width = clip_now.shape[-1]
    frames, patches = (clip_now.shape[0], clip_now.shape[1])
    flat_rows = clip_now.reshape(-1, model_width)
    temporal_in = low_back(flat_rows)
    normed_t = low(layer_norm(temporal_in, gains[0], shifts[0]))
    project_t = low_back(low(product(normed_t, weights_in[0:3 * model_width].T)))
    project_t = project_t.reshape(frames, patches, 3, HEADS, HEAD_DIM)
    mixed_t = attend(project_t, 'sbhd,tbhd->bhst', 'bhst,tbhd->sbhd').reshape(-1, model_width)
    projected_t = low_back(low(product(mixed_t, weights_out[0:model_width]) + shifts[3]))
    branch_t = low_back(low(product(projected_t, weights_out[model_width:2 * model_width]) + shifts[4]))
    after_t = flat_rows + branch_t
    normed_s = low(layer_norm(after_t, gains[1], shifts[1]))
    project_s = low_back(low(product(normed_s, weights_in[3 * model_width:6 * model_width].T)))
    project_s = project_s.reshape(frames, patches, 3, HEADS, HEAD_DIM)
    mixed_s = attend(project_s, 'bshd,bthd->bhst', 'bhst,bthd->bshd').reshape(-1, model_width)
    branch_s = low_back(product(mixed_s, weights_out[2 * model_width:3 * model_width]) + shifts[5])
    after_s = after_t + branch_s
    normed_m = low(layer_norm(after_s, gains[2], shifts[2]))
    hidden_pre = low_back(product(normed_m, weights_in[6 * model_width:].T) + shifts[6:].reshape(-1))
    hidden = low(jax.nn.gelu(hidden_pre, approximate=False))
    dense_out = low_back(product(hidden, weights_out[3 * model_width:]) + dense_bias)
    return (after_s + dense_out).reshape(clip_now.shape)

def reference(clips_in, cotangent, clip_live, weights_in, weights_out, norm_gain, shift_rows, dense_shift):
    params = (weights_in.astype(jnp.float32), weights_out.astype(jnp.float32), norm_gain.astype(jnp.float32), shift_rows.astype(jnp.float32), dense_shift.astype(jnp.float32))
    zero_grads = jax.tree.map(jnp.zeros_like, params)

    def clip_step(totals, inputs):
        clip_now, target_grad, live_flag = inputs
        output, pullback = jax.vjp(layer, params, clip_now.astype(jnp.float32))
        grad_params, grad_clip = pullback(target_grad.astype(jnp.float32) * live_flag.astype(jnp.float32))
        totals = jax.tree.map(jnp.add, totals, grad_params)
        return (totals, (output.astype(jnp.bfloat16), grad_clip))
    totals, (outputs, grad_clips) = lax.scan(clip_step, zero_grads, (clips_in, cotangent, clip_live))
    return (outputs, grad_clips, totals[0], totals[1], totals[2], totals[3], totals[4])
```

```python
from functools import partial

import jax
import jax.numpy as jnp
from jax import lax
from jax.experimental import pallas as pl
from jax.experimental.pallas import tpu as pltpu
from jax.sharding import PartitionSpec as P

HEADS = 12
HEAD_DIM = 64
EPSILON = 1e-06
PAIRS = HEADS // 2
LANES = 2 * HEAD_DIM
SUB = 16
NEG = -1e30
F32 = jnp.float32
BF16 = jnp.bfloat16


def nt(left, right):
    return lax.dot_general(left, right, (((1,), (1,)), ((), ())), preferred_element_type=F32)


def nn(left, right):
    return lax.dot_general(left, right, (((1,), (0,)), ((), ())), preferred_element_type=F32)


def tn(left, right):
    return lax.dot_general(left, right, (((0,), (0,)), ((), ())), preferred_element_type=F32)


def split_heads(pair):
    first = lax.broadcasted_iota(jnp.int32, pair.shape, 1) < HEAD_DIM
    zero = jnp.zeros_like(pair)
    return jnp.concatenate([jnp.where(first, pair, zero), jnp.where(first, zero, pair)], axis=0)


def join_heads(stacked):
    rows = stacked.shape[0] // 2
    first = lax.broadcasted_iota(jnp.int32, (rows, LANES), 1) < HEAD_DIM
    return jnp.where(first, stacked[:rows], stacked[rows:])


def pair_forward(queries, keys, values, keep):
    stacked = split_heads(queries * jnp.asarray(HEAD_DIM**-0.5, BF16))
    scores = jnp.where(keep, nt(stacked, keys), NEG)
    top = jnp.max(scores, axis=1, keepdims=True)
    weights = jnp.exp(scores - top)
    total = jnp.sum(weights, axis=1, keepdims=True)
    probs = (weights * (1.0 / total)).astype(BF16)
    return join_heads(nn(probs, values)).astype(BF16)


def pair_backward(queries, keys, values, grad, keep):
    scaling = HEAD_DIM**-0.5
    stacked = split_heads(queries * jnp.asarray(scaling, BF16))
    grads = split_heads(grad)
    scores = jnp.where(keep, nt(keys, stacked), NEG)
    top = jnp.max(scores, axis=0, keepdims=True)
    weights = jnp.exp(scores - top)
    total = jnp.sum(weights, axis=0, keepdims=True)
    probs = weights * (1.0 / total)
    grad_probs = nt(values, grads)
    mean = jnp.sum(probs * grad_probs, axis=0, keepdims=True)
    grad_scores = (probs * (grad_probs - mean)).astype(BF16)
    grad_values = nn(probs.astype(BF16), grads)
    grad_keys = nn(grad_scores, stacked)
    grad_queries = join_heads(tn(grad_scores, keys)) * scaling
    return (grad_queries.astype(BF16), grad_keys.astype(BF16), grad_values.astype(BF16))


def columns(kind, pair):
    start = (kind * PAIRS + pair) * LANES
    return slice(start, start + LANES)


def load(ref, cols):
    block = ref[..., cols]
    return block.reshape(-1, LANES)


def store(ref, cols, block):
    ref[..., cols] = block.reshape(ref.shape[:-1] + (LANES,))


def keep_mask(shape, key_axis, group, patches):
    key = lax.broadcasted_iota(jnp.int32, shape, key_axis)
    if group is None:
        return key < patches
    query = lax.broadcasted_iota(jnp.int32, shape, 1 - key_axis)
    return (key % group) == (query % group)


def forward_kernel(group, patches, project_ref, mixed_ref):
    rows = project_ref.size // project_ref.shape[-1]
    keep = keep_mask((2 * rows, rows), 1, group, patches)
    for pair in range(PAIRS):
        mixed = pair_forward(
            load(project_ref, columns(0, pair)),
            load(project_ref, columns(1, pair)),
            load(project_ref, columns(2, pair)),
            keep,
        )
        store(mixed_ref, columns(0, pair), mixed)


def backward_kernel(group, patches, project_ref, grad_ref, out_ref):
    rows = project_ref.size // project_ref.shape[-1]
    keep = keep_mask((rows, 2 * rows), 0, group, patches)
    for pair in range(PAIRS):
        results = pair_backward(
            load(project_ref, columns(0, pair)),
            load(project_ref, columns(1, pair)),
            load(project_ref, columns(2, pair)),
            load(grad_ref, columns(0, pair)),
            keep,
        )
        for kind, result in enumerate(results):
            store(out_ref, columns(kind, pair), result)


def attention_call(kernel, arrays, out_cols, temporal, patches):
    clips, frames, rows, _ = arrays[0].shape
    if temporal:
        group, steps, shape = SUB, rows // SUB, (1, frames, SUB)
        index = lambda c, i: (c, 0, i, 0)
    else:
        group, steps, shape = None, frames, (1, 1, rows)
        index = lambda c, i: (c, i, 0, 0)
    return pl.pallas_call(
        partial(kernel, group, patches),
        grid=(clips, steps),
        in_specs=[pl.BlockSpec(shape + (a.shape[-1],), index) for a in arrays],
        out_specs=pl.BlockSpec(shape + (out_cols,), index),
        out_shape=jax.ShapeDtypeStruct((clips, frames, rows, out_cols), BF16),
        compiler_params=pltpu.CompilerParams(dimension_semantics=("arbitrary", "arbitrary")),
    )(*arrays)


def norm_parts(values):
    centre = values - jnp.mean(values, axis=-1, keepdims=True)
    spread = jnp.mean(centre * centre, axis=-1, keepdims=True)
    scale = lax.rsqrt(spread + EPSILON)
    return (centre * scale, scale)


def layer_norm(values, gains, shifts):
    return (norm_parts(values)[0] * gains + shifts).astype(BF16)


def norm_backward(values, gains, grad):
    normed, scale = norm_parts(values)
    scaled = grad * gains
    first = jnp.mean(scaled, axis=-1, keepdims=True)
    second = jnp.mean(scaled * normed, axis=-1, keepdims=True)
    inner = (scaled - first - normed * second) * scale
    return (inner, jnp.sum(grad * normed, axis=0), jnp.sum(grad, axis=0))


def gelu_parts(values):
    cdf = 0.5 * (1.0 + lax.erf(values * (0.5**0.5)))
    density = jnp.exp(-0.5 * values * values) * 0.3989422804014327
    return (values * cdf, cdf + values * density)


def column_sum(rows):
    return jnp.sum(rows.astype(F32), axis=0)


def block(clip, target, weights_in, weights_out, gains, shifts, dense_bias, patches):
    shape = clip.shape
    width = shape[-1]
    grid = shape[:3]
    gains32, shifts32, dense32 = (gains.astype(F32), shifts.astype(F32), dense_bias.astype(F32))
    in_t, in_s, in_m = (
        weights_in[: 3 * width],
        weights_in[3 * width : 6 * width],
        weights_in[6 * width :],
    )
    out_t, out_f, out_s, out_m = (
        weights_out[:width],
        weights_out[width : 2 * width],
        weights_out[2 * width : 3 * width],
        weights_out[3 * width :],
    )
    start = clip.reshape(-1, width).astype(F32)
    normed_t = layer_norm(start, gains32[0], shifts32[0])
    project_t = nt(normed_t, in_t).astype(BF16).reshape(grid + (-1,))
    mixed_t = attention_call(forward_kernel, [project_t], width, True, patches).reshape(-1, width)
    projected_t = (nn(mixed_t, out_t) + shifts32[3]).astype(BF16)
    branch_t = (nn(projected_t, out_f) + shifts32[4]).astype(BF16)
    after_t = start + branch_t.astype(F32)
    normed_s = layer_norm(after_t, gains32[1], shifts32[1])
    project_s = nt(normed_s, in_s).astype(BF16).reshape(grid + (-1,))
    mixed_s = attention_call(forward_kernel, [project_s], width, False, patches).reshape(-1, width)
    after_s = after_t + (nn(mixed_s, out_s) + shifts32[5])
    normed_m = layer_norm(after_s, gains32[2], shifts32[2])
    hidden_pre = nt(normed_m, in_m) + shifts32[6:].reshape(-1)
    hidden32, slope32 = gelu_parts(hidden_pre)
    hidden, slope = (hidden32.astype(BF16), slope32.astype(BF16))
    output = (after_s + (nn(hidden, out_m) + dense32)).astype(BF16)

    grad_low = target.reshape(-1, width)
    grad_out = grad_low.astype(F32)
    d_out_m = tn(hidden, grad_low).astype(BF16)
    s_dense = column_sum(grad_low)
    grad_pre = (nt(grad_low, out_m) * slope.astype(F32)).astype(BF16)
    d_in_m = tn(grad_pre, normed_m).astype(BF16)
    s_hidden = column_sum(grad_pre).reshape(-1, width)
    part, g_m, b_m = norm_backward(after_s, gains32[2], nn(grad_pre, in_m))
    grad_s = grad_out + part
    grad_branch_s = grad_s.astype(BF16)
    d_out_s = tn(mixed_s, grad_branch_s).astype(BF16)
    s_space = column_sum(grad_branch_s)
    grad_mixed_s = nt(grad_branch_s, out_s).astype(BF16).reshape(shape)
    grad_project_s = attention_call(
        backward_kernel, [project_s, grad_mixed_s], 3 * width, False, patches
    ).reshape(-1, 3 * width)
    d_in_s = tn(grad_project_s, normed_s).astype(BF16)
    part, g_s, b_s = norm_backward(after_t, gains32[1], nn(grad_project_s, in_s))
    grad_t = grad_s + part
    grad_branch_t = grad_t.astype(BF16)
    d_out_f = tn(projected_t, grad_branch_t).astype(BF16)
    s_fc = column_sum(grad_branch_t)
    grad_projected = nt(grad_branch_t, out_f).astype(BF16)
    d_out_t = tn(mixed_t, grad_projected).astype(BF16)
    s_time = column_sum(grad_projected)
    grad_mixed_t = nt(grad_projected, out_t).astype(BF16).reshape(shape)
    grad_project_t = attention_call(
        backward_kernel, [project_t, grad_mixed_t], 3 * width, True, patches
    ).reshape(-1, 3 * width)
    d_in_t = tn(grad_project_t, normed_t).astype(BF16)
    part, g_t, b_t = norm_backward(start, gains32[0], nn(grad_project_t, in_t))
    grad_clip = (grad_t + part.astype(BF16).astype(F32)).astype(BF16)
    small = jnp.concatenate(
        [
            jnp.stack([g_t, g_s, g_m, b_t, b_s, b_m, s_time, s_fc, s_space], axis=0),
            s_hidden,
            s_dense[None, :],
        ],
        axis=0,
    )
    d_in = jnp.concatenate([d_in_t, d_in_s, d_in_m], axis=0)
    d_out = jnp.concatenate([d_out_t, d_out_f, d_out_s, d_out_m], axis=0)
    return (output.reshape(shape), grad_clip.reshape(shape), d_in, d_out, small)


def shards(clips_in, cotangent, clip_live, weights_in, weights_out, norm_gain, shift_rows, dense_shift):
    both = ("dp", "seq")
    devices = lax.axis_size(both)
    group = lax.axis_size("seq")
    count, _, patches, width = clips_in.shape
    own = count // group
    rows = -(-patches // SUB) * SUB
    gain_count = norm_gain.shape[0]
    shift_count = shift_rows.shape[0]

    def enter(x):
        x = lax.all_to_all(x, "seq", split_axis=0, concat_axis=1, tiled=True)
        return jnp.pad(x, ((0, 0), (0, 0), (0, rows - patches), (0, 0)))

    def leave(x):
        x = x[:, :, :patches]
        return lax.all_to_all(x, "seq", split_axis=1, concat_axis=0, tiled=True)

    full_in = lax.all_gather(weights_in, both, axis=0, tiled=True)
    full_out = lax.all_gather(weights_out, both, axis=0, tiled=True)
    packed = jnp.concatenate([norm_gain, shift_rows, dense_shift[None, :]], axis=0)
    slot = lax.dynamic_update_slice(
        jnp.zeros((devices,) + packed.shape, F32),
        packed.astype(F32)[None],
        (lax.axis_index(both), 0, 0),
    )
    full_small = lax.psum(slot, both).transpose(1, 0, 2).reshape(packed.shape[0], width).astype(BF16)
    live = lax.dynamic_slice(clip_live, (lax.axis_index("seq") * own,), (own,)).astype(BF16)
    output, grad_clip, d_in, d_out, small = block(
        enter(clips_in),
        enter(cotangent * 1) * live[:, None, None, None],
        full_in,
        full_out,
        full_small[:gain_count],
        full_small[gain_count : gain_count + shift_count],
        full_small[-1],
        patches,
    )
    summed_in = lax.psum_scatter(d_in, both, scatter_dimension=0, tiled=True).astype(F32)
    summed_out = lax.psum_scatter(d_out, both, scatter_dimension=0, tiled=True).astype(F32)
    summed_small = lax.psum(small, both)
    share = width // devices
    owned = lax.dynamic_slice(summed_small, (0, lax.axis_index(both) * share), (small.shape[0], share))
    return (
        leave(output),
        leave(grad_clip).astype(F32),
        summed_in,
        summed_out,
        owned[:gain_count],
        owned[gain_count : gain_count + shift_count],
        owned[-1],
    )


def solution(mesh):
    clip = P("dp", "seq", None, None)
    row = P(("dp", "seq"), None)
    col = P(None, ("dp", "seq"))
    flat = P(("dp", "seq"))
    return jax.shard_map(
        shards,
        mesh=mesh,
        in_specs=(clip, clip, P("dp"), row, row, col, col, flat),
        out_specs=(clip, clip, row, row, col, col, flat),
        check_vma=False,
    )
```

```python
from functools import partial

import jax
import jax.numpy as jnp
from jax import lax
from jax.experimental import pallas as pl
from jax.experimental.pallas import tpu as pltpu
from jax.sharding import PartitionSpec as P

HEADS = 12
HEAD_DIM = 64
EPSILON = 1e-06
PAIRS = HEADS // 2
LANES = 2 * HEAD_DIM
SUB = 16
NEG = -1e30
F32 = jnp.float32
BF16 = jnp.bfloat16


def nt(left, right):
    return lax.dot_general(left, right, (((1,), (1,)), ((), ())), preferred_element_type=F32)


def nn(left, right):
    return lax.dot_general(left, right, (((1,), (0,)), ((), ())), preferred_element_type=F32)


def tn(left, right):
    return lax.dot_general(left, right, (((0,), (0,)), ((), ())), preferred_element_type=F32)


def split_heads(pair):
    first = lax.broadcasted_iota(jnp.int32, pair.shape, 1) < HEAD_DIM
    zero = jnp.zeros_like(pair)
    return jnp.concatenate([jnp.where(first, pair, zero), jnp.where(first, zero, pair)], axis=0)


def join_heads(stacked):
    rows = stacked.shape[0] // 2
    first = lax.broadcasted_iota(jnp.int32, (rows, LANES), 1) < HEAD_DIM
    return jnp.where(first, stacked[:rows], stacked[rows:])


def pair_forward(queries, keys, values, keep):
    stacked = split_heads(queries * jnp.asarray(HEAD_DIM**-0.5, BF16))
    scores = jnp.where(keep, nt(stacked, keys), NEG)
    top = jnp.max(scores, axis=1, keepdims=True)
    weights = jnp.exp(scores - top)
    total = jnp.sum(weights, axis=1, keepdims=True)
    probs = (weights * (1.0 / total)).astype(BF16)
    return join_heads(nn(probs, values)).astype(BF16)


def pair_backward(queries, keys, values, grad, keep):
    scaling = HEAD_DIM**-0.5
    stacked = split_heads(queries * jnp.asarray(scaling, BF16))
    grads = split_heads(grad)
    scores = jnp.where(keep, nt(keys, stacked), NEG)
    top = jnp.max(scores, axis=0, keepdims=True)
    weights = jnp.exp(scores - top)
    total = jnp.sum(weights, axis=0, keepdims=True)
    probs = weights * (1.0 / total)
    grad_probs = nt(values, grads)
    mean = jnp.sum(probs * grad_probs, axis=0, keepdims=True)
    grad_scores = (probs * (grad_probs - mean)).astype(BF16)
    grad_values = nn(probs.astype(BF16), grads)
    grad_keys = nn(grad_scores, stacked)
    grad_queries = join_heads(tn(grad_scores, keys)) * scaling
    return (grad_queries.astype(BF16), grad_keys.astype(BF16), grad_values.astype(BF16))


def columns(kind, pair):
    start = (kind * PAIRS + pair) * LANES
    return slice(start, start + LANES)


def load(refs, kinds, kind, pair):
    place = 0
    while kind >= kinds[place]:
        kind -= kinds[place]
        place += 1
    return refs[place][..., columns(kind, pair)].reshape(-1, LANES)


def store(refs, kinds, kind, pair, block):
    place = 0
    while kind >= kinds[place]:
        kind -= kinds[place]
        place += 1
    ref = refs[place]
    ref[..., columns(kind, pair)] = block.reshape(ref.shape[:-1] + (LANES,))


def keep_mask(shape, key_axis, group, patches):
    key = lax.broadcasted_iota(jnp.int32, shape, key_axis)
    if group is None:
        return key < patches
    query = lax.broadcasted_iota(jnp.int32, shape, 1 - key_axis)
    return (key % group) == (query % group)


def forward_kernel(group, patches, kinds, *refs):
    project, mixed = (refs[: len(kinds)], refs[len(kinds) :])
    rows = project[0].size // project[0].shape[-1]
    keep = keep_mask((2 * rows, rows), 1, group, patches)
    for pair in range(PAIRS):
        block = pair_forward(*[load(project, kinds, kind, pair) for kind in range(3)], keep)
        store(mixed, (1,), 0, pair, block)


def backward_kernel(group, patches, kinds, *refs):
    count = len(kinds)
    project, grad, outs = (refs[:count], refs[count : count + 1], refs[count + 1 :])
    rows = project[0].size // project[0].shape[-1]
    keep = keep_mask((rows, 2 * rows), 0, group, patches)
    for pair in range(PAIRS):
        results = pair_backward(
            *[load(project, kinds, kind, pair) for kind in range(3)], load(grad, (1,), 0, pair), keep
        )
        for kind, result in enumerate(results):
            store(outs, kinds, kind, pair, result)


def attention_call(kernel, kinds, arrays, out_cols, temporal, patches):
    clips, frames, rows, _ = arrays[0].shape
    if temporal:
        group, steps, shape = SUB, rows // SUB, (1, frames, SUB)
        index = lambda c, i: (c, 0, i, 0)
    else:
        group, steps, shape = None, frames, (1, 1, rows)
        index = lambda c, i: (c, i, 0, 0)
    tokens = clips * frames * rows
    backward = kernel is backward_kernel
    return pl.pallas_call(
        partial(kernel, group, patches, kinds),
        grid=(clips, steps),
        in_specs=[pl.BlockSpec(shape + (a.shape[-1],), index) for a in arrays],
        out_specs=[pl.BlockSpec(shape + (cols,), index) for cols in out_cols],
        out_shape=[jax.ShapeDtypeStruct((clips, frames, rows, cols), BF16) for cols in out_cols],
        compiler_params=pltpu.CompilerParams(dimension_semantics=("arbitrary", "arbitrary")),
        cost_estimate=pl.CostEstimate(
            flops=tokens * (14_000_000 if backward else 9_000_000), bytes_accessed=0, transcendentals=0
        ),
    )(*arrays)


def place_kernel(sources, out_planes, counts, dest_ref, *refs):
    total = sum(counts)
    pieces, out = (refs[:total], refs[total])
    held, in_sem, out_sem = refs[total + 1 :]
    blocks = counts[0]
    incoming = []
    for entry, (group, plane) in enumerate(sources):
        for block in range(blocks):
            slot = entry * blocks + block
            copy = pltpu.make_async_copy(
                pieces[group * blocks + block].at[plane], held.at[slot], in_sem.at[slot]
            )
            copy.start()
            incoming.append(copy)
    outgoing = []
    for entry in range(out_planes):
        for block in range(blocks):
            slot = entry * blocks + block
            incoming[slot].wait()
            copy = pltpu.make_async_copy(held.at[slot], out.at[entry, dest_ref[block]], out_sem.at[slot])
            copy.start()
            outgoing.append(copy)
    for copy in outgoing:
        copy.wait()


def place(groups, sources, dest):
    blocks = len(groups[0])
    _, rows, width = groups[0][0].shape
    slots = len(sources) * blocks
    flat = [piece for group in groups for piece in group]
    anywhere = pl.BlockSpec(memory_space=pl.ANY)
    return pl.pallas_call(
        partial(place_kernel, tuple(sources), len(sources), tuple(len(g) for g in groups)),
        in_specs=[pl.BlockSpec(memory_space=pltpu.SMEM)] + [anywhere] * len(flat),
        out_specs=anywhere,
        out_shape=jax.ShapeDtypeStruct((len(sources), blocks, rows, width), BF16),
        scratch_shapes=[
            pltpu.VMEM((slots, rows, width), BF16),
            pltpu.SemaphoreType.DMA((slots,)),
            pltpu.SemaphoreType.DMA((slots,)),
        ],
        compiler_params=pltpu.CompilerParams(vmem_limit_bytes=slots * rows * width * 2 + (2 << 20)),
        cost_estimate=pl.CostEstimate(flops=0, bytes_accessed=4 * slots * rows * width, transcendentals=0),
    )(dest, *flat)


def split_kernel(spans, shape, core_ref, *refs):
    planes, squares, rows = shape
    parts = refs[: len(spans)]
    keep, send, held, in_sem, out_sem = refs[len(spans) :]
    core = core_ref[0]
    incoming = [[] for _ in range(planes * squares * 2)]
    count, row = (0, 0)
    for part, (first, length) in enumerate(spans):
        done = 0
        while done < length:
            slot, offset = divmod(row, rows)
            size = min(length - done, rows - offset)
            copy = pltpu.make_async_copy(
                parts[part].at[pl.ds(first + done, size)], held.at[slot, pl.ds(offset, size)], in_sem.at[count]
            )
            copy.start()
            incoming[slot].append(copy)
            count, row, done = (count + 1, row + size, done + size)
    outgoing = []
    for plane in range(planes):
        for square in range(squares):
            pair = (plane * squares + square) * 2
            for copy in incoming[pair] + incoming[pair + 1]:
                copy.wait()
            for which, (target, side) in enumerate(((send, 1 - core), (keep, core))):
                copy = pltpu.make_async_copy(
                    held.at[pair + side], target.at[square, plane], out_sem.at[pair + which]
                )
                copy.start()
                outgoing.append(copy)
    for copy in outgoing:
        copy.wait()


def split_cores(parts, planes, squares, rows, core):
    spans = tuple((first, length) for _, first, length in parts)
    arrays = [array for array, _, _ in parts]
    width = arrays[0].shape[1]
    slots = planes * squares * 2
    anywhere = pl.BlockSpec(memory_space=pl.ANY)
    half = jax.ShapeDtypeStruct((squares, planes, rows, width), BF16)
    return pl.pallas_call(
        partial(split_kernel, spans, (planes, squares, rows)),
        in_specs=[pl.BlockSpec(memory_space=pltpu.SMEM)] + [anywhere] * len(arrays),
        out_specs=[anywhere, anywhere],
        out_shape=[half, half],
        scratch_shapes=[
            pltpu.VMEM((slots, rows, width), BF16),
            pltpu.SemaphoreType.DMA((slots + len(parts),)),
            pltpu.SemaphoreType.DMA((slots,)),
        ],
        compiler_params=pltpu.CompilerParams(vmem_limit_bytes=slots * rows * width * 2 + (2 << 20)),
        cost_estimate=pl.CostEstimate(flops=0, bytes_accessed=4 * slots * rows * width, transcendentals=0),
    )(core, *arrays)


class Plan:
    def __init__(self, axes):
        self.axes = axes
        me = lax.axis_index(axes)
        self.plane, self.spot, self.square, self.core = (me // 8, me % 8, me % 8 // 2, me % 2)
        self.spots = jnp.bitwise_xor(jnp.arange(8, dtype=jnp.int32), self.spot)
        self.planes = (self.plane + 4 - jnp.arange(4, dtype=jnp.int32)) % 4
        self.core_ref = self.core.astype(jnp.int32).reshape(1)

    def flip(self, x, bits):
        return lax.ppermute(x, self.axes, [(d, d ^ bits) for d in range(32)])

    def shift(self, x, step):
        return lax.ppermute(x, self.axes, [(d, (d + 8 * step) % 32) for d in range(32)])

    def columns(self, shard):
        pieces = [shard[None]] + [self.shift(shard, step)[None] for step in (1, 2, 3)]
        return place([pieces], [(0, 0)], self.planes)[0]

    def spread(self, column):
        mine = [column] + [self.flip(column, bits) for bits in (2, 4, 6)]
        both = []
        for block in mine:
            both += [block, self.flip(block, 1)]
        return both

    def narrow(self, parts, rows):
        keep, send = split_cores(parts, 2, 4, rows, self.core_ref)
        other = self.flip(send, 1)
        total = None
        for bits in (2, 4, 6, 0):
            at = jnp.bitwise_xor(self.square, bits // 2)
            take = lambda a: lax.dynamic_index_in_dim(a, at, 0, keepdims=False).astype(F32)
            summed = (take(keep) + take(other)).astype(BF16)
            arrived = (summed if bits == 0 else self.flip(summed, bits)).astype(F32)
            total = arrived if total is None else total + arrived
        return total.astype(BF16)

    def finish(self, low, high):
        every = jnp.concatenate([low, high], axis=0)
        total = lax.dynamic_index_in_dim(every, self.plane, 0, keepdims=False).astype(F32)
        for step in (1, 2, 3):
            target = (self.plane + step) % 4
            block = lax.dynamic_index_in_dim(every, target, 0, keepdims=False)
            total = total + self.shift(block, step).astype(F32)
        return total

    def share_small(self, packed):
        count, share = packed.shape
        tiles = -(-count * share // (8 * LANES))
        flat = jnp.pad(packed.reshape(-1), (0, tiles * 8 * LANES - count * share)).reshape(1, tiles * 8, LANES)
        every = jnp.broadcast_to(flat, (32,) + flat.shape[1:])
        every = lax.all_to_all(every, self.axes, split_axis=0, concat_axis=0)
        every = every.reshape(32, -1)[:, : count * share].reshape(32, count, share)
        return every.transpose(1, 0, 2).reshape(count, 32 * share)

    def sum_small(self, small):
        count, width = small.shape
        share = width // 32
        tiles = -(-count * share // (8 * LANES))
        slots = small.reshape(count, 32, share).transpose(1, 0, 2).reshape(32, count * share)
        slots = jnp.pad(slots, ((0, 0), (0, tiles * 8 * LANES - count * share))).reshape(32, tiles * 8, LANES)
        slots = lax.all_to_all(slots, self.axes, split_axis=0, concat_axis=0)
        return jnp.sum(slots, axis=0).reshape(-1)[: count * share].reshape(count, share)


def norm_parts(values):
    centre = values - jnp.mean(values, axis=-1, keepdims=True)
    spread = jnp.mean(centre * centre, axis=-1, keepdims=True)
    scale = lax.rsqrt(spread + EPSILON)
    return (centre * scale, scale)


def layer_norm(values, gains, shifts):
    return (norm_parts(values)[0] * gains + shifts).astype(BF16)


def norm_backward(values, gains, grad):
    normed, scale = norm_parts(values)
    scaled = grad * gains
    first = jnp.mean(scaled, axis=-1, keepdims=True)
    second = jnp.mean(scaled * normed, axis=-1, keepdims=True)
    inner = (scaled - first - normed * second) * scale
    return (inner, jnp.sum(grad * normed, axis=0), jnp.sum(grad, axis=0))


def gelu_parts(values):
    cdf = 0.5 * (1.0 + lax.erf(values * (0.5**0.5)))
    density = jnp.exp(-0.5 * values * values) * 0.3989422804014327
    return (values * cdf, cdf + values * density)


def column_sum(rows):
    return jnp.sum(rows.astype(F32), axis=0)


def block(clip, target, weights, gains, shifts, dense_bias, patches):
    shape = clip.shape
    width = shape[-1]
    grid = shape[:3]
    gains32, shifts32, dense32 = (gains.astype(F32), shifts.astype(F32), dense_bias.astype(F32))
    in_t, in_qk, in_v, in_m, out_t, out_f, out_s, out_m = weights
    flat = lambda a: a.reshape(-1, a.shape[-1])
    start = clip.reshape(-1, width).astype(F32)
    normed_t = layer_norm(start, gains32[0], shifts32[0])
    project_t = nt(normed_t, in_t).astype(BF16).reshape(grid + (-1,))
    mixed_t = flat(attention_call(forward_kernel, (3,), [project_t], (width,), True, patches)[0])
    projected_t = (nn(mixed_t, out_t) + shifts32[3]).astype(BF16)
    branch_t = (nn(projected_t, out_f) + shifts32[4]).astype(BF16)
    after_t = start + branch_t.astype(F32)
    normed_s = layer_norm(after_t, gains32[1], shifts32[1])
    project_qk = nt(normed_s, in_qk).astype(BF16).reshape(grid + (-1,))
    project_v = nt(normed_s, in_v).astype(BF16).reshape(grid + (-1,))
    project_s = [project_qk, project_v]
    mixed_s = flat(attention_call(forward_kernel, (2, 1), project_s, (width,), False, patches)[0])
    after_s = after_t + (nn(mixed_s, out_s) + shifts32[5])
    normed_m = layer_norm(after_s, gains32[2], shifts32[2])
    hidden_pre = nt(normed_m, in_m) + shifts32[6:].reshape(-1)
    hidden32, slope32 = gelu_parts(hidden_pre)
    hidden, slope = (hidden32.astype(BF16), slope32.astype(BF16))
    output = (after_s + (nn(hidden, out_m) + dense32)).astype(BF16)

    grad_low = target.reshape(-1, width)
    grad_out = grad_low.astype(F32)
    d_out_m = tn(hidden, grad_low).astype(BF16)
    s_dense = column_sum(grad_low)
    grad_pre = (nt(grad_low, out_m) * slope.astype(F32)).astype(BF16)
    d_in_m = tn(grad_pre, normed_m).astype(BF16)
    s_hidden = column_sum(grad_pre).reshape(-1, width)
    part, g_m, b_m = norm_backward(after_s, gains32[2], nn(grad_pre, in_m))
    grad_s = grad_out + part
    grad_branch_s = grad_s.astype(BF16)
    d_out_s = tn(mixed_s, grad_branch_s).astype(BF16)
    s_space = column_sum(grad_branch_s)
    grad_mixed_s = nt(grad_branch_s, out_s).astype(BF16).reshape(shape)
    grad_qk, grad_v = attention_call(
        backward_kernel, (2, 1), project_s + [grad_mixed_s], (2 * width, width), False, patches
    )
    grad_qk, grad_v = (flat(grad_qk), flat(grad_v))
    d_in_qk = tn(grad_qk, normed_s).astype(BF16)
    d_in_v = tn(grad_v, normed_s).astype(BF16)
    part, g_s, b_s = norm_backward(after_t, gains32[1], nn(grad_qk, in_qk) + nn(grad_v, in_v))
    grad_t = grad_s + part
    grad_branch_t = grad_t.astype(BF16)
    d_out_f = tn(projected_t, grad_branch_t).astype(BF16)
    s_fc = column_sum(grad_branch_t)
    grad_projected = nt(grad_branch_t, out_f).astype(BF16)
    d_out_t = tn(mixed_t, grad_projected).astype(BF16)
    s_time = column_sum(grad_projected)
    grad_mixed_t = nt(grad_projected, out_t).astype(BF16).reshape(shape)
    grad_project_t = flat(
        attention_call(backward_kernel, (3,), [project_t, grad_mixed_t], (3 * width,), True, patches)[0]
    )
    d_in_t = tn(grad_project_t, normed_t).astype(BF16)
    part, g_t, b_t = norm_backward(start, gains32[0], nn(grad_project_t, in_t))
    grad_clip = (grad_t + part.astype(BF16).astype(F32)).astype(BF16)
    small = jnp.concatenate(
        [
            jnp.stack([g_t, g_s, g_m, b_t, b_s, b_m, s_time, s_fc, s_space], axis=0),
            s_hidden,
            s_dense[None, :],
        ],
        axis=0,
    )
    grads = (d_in_t, d_in_qk, d_in_v, d_in_m, d_out_t, d_out_f, d_out_s, d_out_m)
    return (output.reshape(shape), grad_clip.reshape(shape), grads, small)


def cut(array, sizes):
    pieces, row = ([], 0)
    for size in sizes:
        pieces.append(array[row : row + size])
        row += size
    return pieces


def shards(clips_in, cotangent, clip_live, weights_in, weights_out, norm_gain, shift_rows, dense_shift):
    both = ("dp", "seq")
    devices = lax.axis_size(both)
    group = lax.axis_size("seq")
    count, _, patches, width = clips_in.shape
    own = count // group
    rows = -(-patches // SUB) * SUB
    gain_count = norm_gain.shape[0]
    shift_count = shift_rows.shape[0]
    hidden = weights_out.shape[0] * devices - 3 * width
    planned = devices == 32 and group == 4 and width == 768 and hidden == 4 * width
    in_sizes = (3 * width, 2 * width, width, hidden)
    out_sizes = (width, width, width, hidden)

    def enter(x):
        x = lax.all_to_all(x, "seq", split_axis=0, concat_axis=1, tiled=True)
        return jnp.pad(x, ((0, 0), (0, 0), (0, rows - patches), (0, 0)))

    def leave(x):
        x = x[:, :, :patches]
        return lax.all_to_all(x, "seq", split_axis=1, concat_axis=0, tiled=True)

    packed = jnp.concatenate([norm_gain, shift_rows, dense_shift[None, :]], axis=0)
    if planned:
        plan = Plan(both)
        in_rows, out_rows = (weights_in.shape[0], weights_out.shape[0])
        column_in = plan.columns(weights_in)
        clip = enter(clips_in)
        full_small = plan.share_small(packed)
        in_low = plan.spread(column_in[:2])
        column_out = plan.columns(weights_out)
        out_low = plan.spread(column_out[:2])
        in_high = plan.spread(column_in[2:])
        out_high = plan.spread(column_out[2:])
        pair = [(0, 0), (0, 1)]
        low = place([in_low], pair, plan.spots).reshape(16 * in_rows, width)
        high = place([in_high], pair, plan.spots).reshape(16 * in_rows, width)
        early = place([out_low], pair, plan.spots).reshape(16 * out_rows, width)
        late = place([out_low, out_high], [(0, 1), (1, 0), (1, 1)], plan.spots).reshape(24 * out_rows, width)
        skip = 3 * width - 8 * out_rows
        weights = cut(low, in_sizes[:2]) + cut(high, in_sizes[2:]) + cut(early, out_sizes[:3]) + [late[skip:]]
    else:
        full_in = lax.all_gather(weights_in, both, axis=0, tiled=True)
        full_out = lax.all_gather(weights_out, both, axis=0, tiled=True)
        slot = lax.dynamic_update_slice(
            jnp.zeros((devices,) + packed.shape, F32),
            packed.astype(F32)[None],
            (lax.axis_index(both), 0, 0),
        )
        full_small = lax.psum(slot, both).transpose(1, 0, 2).reshape(packed.shape[0], width).astype(BF16)
        clip = enter(clips_in)
        weights = cut(full_in, in_sizes) + cut(full_out, out_sizes)
    live = lax.dynamic_slice(clip_live, (lax.axis_index("seq") * own,), (own,)).astype(BF16)
    output, grad_clip, grads, small = block(
        clip,
        enter(cotangent * 1) * live[:, None, None, None],
        weights,
        full_small[:gain_count],
        full_small[gain_count : gain_count + shift_count],
        full_small[-1],
        patches,
    )
    if planned:
        whole = lambda a: (a, 0, a.shape[0])
        d_in_t, d_in_qk, d_in_v, d_in_m, d_out_t, d_out_f, d_out_s, d_out_m = grads
        first = 16 * out_rows - 3 * width
        out_high = plan.narrow([(d_out_m, first, hidden - first)], out_rows)
        in_high = plan.narrow([whole(d_in_v), whole(d_in_m)], in_rows)
        out_low = plan.narrow([whole(d_out_t), whole(d_out_f), whole(d_out_s), (d_out_m, 0, first)], out_rows)
        summed_out = plan.finish(out_low, out_high)
        in_low = plan.narrow([whole(d_in_t), whole(d_in_qk)], in_rows)
        summed_in = plan.finish(in_low, in_high)
        owned = plan.sum_small(small)
    else:
        d_in, d_out = (jnp.concatenate(grads[:4], axis=0), jnp.concatenate(grads[4:], axis=0))
        summed_in = lax.psum_scatter(d_in, both, scatter_dimension=0, tiled=True).astype(F32)
        summed_out = lax.psum_scatter(d_out, both, scatter_dimension=0, tiled=True).astype(F32)
        summed_small = lax.psum(small, both)
        share = width // devices
        owned = lax.dynamic_slice(summed_small, (0, lax.axis_index(both) * share), (small.shape[0], share))
    return (
        leave(output),
        leave(grad_clip).astype(F32),
        summed_in,
        summed_out,
        owned[:gain_count],
        owned[gain_count : gain_count + shift_count],
        owned[-1],
    )


def solution(mesh):
    clip = P("dp", "seq", None, None)
    row = P(("dp", "seq"), None)
    col = P(None, ("dp", "seq"))
    flat = P(("dp", "seq"))
    return jax.shard_map(
        shards,
        mesh=mesh,
        in_specs=(clip, clip, P("dp"), row, row, col, col, flat),
        out_specs=(clip, clip, row, row, col, col, flat),
        check_vma=False,
    )
```

```python
from functools import partial

import jax
import jax.numpy as jnp
from jax import lax
from jax.experimental import pallas as pl
from jax.experimental.pallas import tpu as pltpu
from jax.sharding import PartitionSpec as P

HEADS = 12
HEAD_DIM = 64
EPSILON = 1e-06
PAIRS = HEADS // 2
LANES = 2 * HEAD_DIM
SUB = 16
NEG = -1e30
F32 = jnp.float32
BF16 = jnp.bfloat16


def nt(left, right):
    return lax.dot_general(left, right, (((1,), (1,)), ((), ())), preferred_element_type=F32)


def nn(left, right):
    return lax.dot_general(left, right, (((1,), (0,)), ((), ())), preferred_element_type=F32)


def tn(left, right):
    return lax.dot_general(left, right, (((0,), (0,)), ((), ())), preferred_element_type=F32)


def split_heads(pair):
    first = lax.broadcasted_iota(jnp.int32, pair.shape, 1) < HEAD_DIM
    zero = jnp.zeros_like(pair)
    return jnp.concatenate([jnp.where(first, pair, zero), jnp.where(first, zero, pair)], axis=0)


def join_heads(stacked):
    rows = stacked.shape[0] // 2
    first = lax.broadcasted_iota(jnp.int32, (rows, LANES), 1) < HEAD_DIM
    return jnp.where(first, stacked[:rows], stacked[rows:])


def pair_forward(queries, keys, values, keep):
    stacked = split_heads(queries * jnp.asarray(HEAD_DIM**-0.5, BF16))
    scores = jnp.where(keep, nt(stacked, keys), NEG)
    top = jnp.max(scores, axis=1, keepdims=True)
    weights = jnp.exp(scores - top)
    total = jnp.sum(weights, axis=1, keepdims=True)
    probs = (weights * (1.0 / total)).astype(BF16)
    return join_heads(nn(probs, values)).astype(BF16)


def pair_backward(queries, keys, values, grad, keep):
    scaling = HEAD_DIM**-0.5
    stacked = split_heads(queries * jnp.asarray(scaling, BF16))
    grads = split_heads(grad)
    scores = jnp.where(keep, nt(keys, stacked), NEG)
    top = jnp.max(scores, axis=0, keepdims=True)
    weights = jnp.exp(scores - top)
    total = jnp.sum(weights, axis=0, keepdims=True)
    probs = weights * (1.0 / total)
    grad_probs = nt(values, grads)
    mean = jnp.sum(probs * grad_probs, axis=0, keepdims=True)
    grad_scores = (probs * (grad_probs - mean)).astype(BF16)
    grad_values = nn(probs.astype(BF16), grads)
    grad_keys = nn(grad_scores, stacked)
    grad_queries = join_heads(tn(grad_scores, keys)) * scaling
    return (grad_queries.astype(BF16), grad_keys.astype(BF16), grad_values.astype(BF16))


def columns(kind, pair):
    start = (kind * PAIRS + pair) * LANES
    return slice(start, start + LANES)


def find(refs, kind, pair):
    cols = columns(kind, pair)
    for ref in refs:
        size = ref.shape[-1]
        if cols.start < size:
            return (ref, cols)
        cols = slice(cols.start - size, cols.stop - size)


def load(refs, kind, pair):
    ref, cols = find(refs, kind, pair)
    return ref[..., cols].reshape(-1, LANES)


def store(refs, kind, pair, block):
    ref, cols = find(refs, kind, pair)
    ref[..., cols] = block.reshape(ref.shape[:-1] + (LANES,))


def keep_mask(shape, key_axis, group, patches):
    key = lax.broadcasted_iota(jnp.int32, shape, key_axis)
    if group is None:
        return key < patches
    query = lax.broadcasted_iota(jnp.int32, shape, 1 - key_axis)
    return (key % group) == (query % group)


def forward_kernel(group, patches, count, *refs):
    project, mixed = (refs[:count], refs[count:])
    rows = project[0].size // project[0].shape[-1]
    keep = keep_mask((2 * rows, rows), 1, group, patches)
    for pair in range(PAIRS):
        block = pair_forward(*[load(project, kind, pair) for kind in range(3)], keep)
        store(mixed, 0, pair, block)


def backward_kernel(group, patches, count, *refs):
    project, grad, outs = (refs[:count], refs[count : count + 1], refs[count + 1 :])
    rows = project[0].size // project[0].shape[-1]
    keep = keep_mask((rows, 2 * rows), 0, group, patches)
    for pair in range(PAIRS):
        results = pair_backward(*[load(project, kind, pair) for kind in range(3)], load(grad, 0, pair), keep)
        for kind, result in enumerate(results):
            store(outs, kind, pair, result)


def attention_call(kernel, count, arrays, out_cols, temporal, patches):
    clips, frames, rows, _ = arrays[0].shape
    if temporal:
        group, steps, shape = SUB, rows // SUB, (1, frames, SUB)
        index = lambda c, i: (c, 0, i, 0)
    else:
        group, steps, shape = None, frames, (1, 1, rows)
        index = lambda c, i: (c, i, 0, 0)
    tokens = clips * frames * rows
    backward = kernel is backward_kernel
    return pl.pallas_call(
        partial(kernel, group, patches, count),
        grid=(clips, steps),
        in_specs=[pl.BlockSpec(shape + (a.shape[-1],), index) for a in arrays],
        out_specs=[pl.BlockSpec(shape + (cols,), index) for cols in out_cols],
        out_shape=[jax.ShapeDtypeStruct((clips, frames, rows, cols), BF16) for cols in out_cols],
        compiler_params=pltpu.CompilerParams(dimension_semantics=("arbitrary", "arbitrary")),
        cost_estimate=pl.CostEstimate(
            flops=tokens * (14_000_000 if backward else 9_000_000), bytes_accessed=0, transcendentals=0
        ),
    )(*arrays)


def place_kernel(outs_plan, blocks, groups, dest_ref, *refs):
    pieces, refs = (refs[: groups * blocks], refs[groups * blocks :])
    outs, refs = (refs[: len(outs_plan)], refs[len(outs_plan) :])
    held, in_sem, out_sem = (refs[:-2], refs[-2], refs[-1])
    moves, slot = ([], 0)
    for target, entries in enumerate(outs_plan):
        for entry, (group, row, rows) in enumerate(entries):
            for block in range(blocks):
                buffer = held[target].at[entry, block]
                source = pieces[group * blocks + block].at[pl.ds(row, rows)]
                fetch = pltpu.make_async_copy(source, buffer, in_sem.at[slot])
                fetch.start()
                write = pltpu.make_async_copy(buffer, outs[target].at[entry, dest_ref[block]], out_sem.at[slot])
                moves.append((fetch, write))
                slot += 1
    for fetch, write in moves:
        fetch.wait()
        write.start()
    for _, write in moves:
        write.wait()


def place(groups, outs_plan, dest):
    blocks = len(groups[0])
    width = groups[0][0].shape[1]
    shapes = [(len(entries), blocks, entries[0][2], width) for entries in outs_plan]
    slots = sum(len(entries) for entries in outs_plan) * blocks
    size = sum(2 * s[0] * s[1] * s[2] * s[3] for s in shapes)
    flat = [piece for group in groups for piece in group]
    anywhere = pl.BlockSpec(memory_space=pl.ANY)
    return pl.pallas_call(
        partial(place_kernel, tuple(tuple(e) for e in outs_plan), blocks, len(groups)),
        in_specs=[pl.BlockSpec(memory_space=pltpu.SMEM)] + [anywhere] * len(flat),
        out_specs=[anywhere] * len(shapes),
        out_shape=[jax.ShapeDtypeStruct(s, BF16) for s in shapes],
        scratch_shapes=[pltpu.VMEM(s, BF16) for s in shapes]
        + [pltpu.SemaphoreType.DMA((slots,)), pltpu.SemaphoreType.DMA((slots,))],
        compiler_params=pltpu.CompilerParams(vmem_limit_bytes=size + (2 << 20)),
        cost_estimate=pl.CostEstimate(flops=0, bytes_accessed=4 * size, transcendentals=0),
    )(dest, *flat)


def split_kernel(spans, plane_rows, squares, core_ref, *refs):
    parts, refs = (refs[: len(spans)], refs[len(spans) :])
    keep, send = refs[:2]
    held, in_sem, out_sem = (refs[2:-2], refs[-2], refs[-1])
    core = core_ref[0]
    incoming, count, part, done = ({}, 0, 0, 0)
    for plane, rows in enumerate(plane_rows):
        for slot in range(2 * squares):
            offset, incoming[plane, slot] = (0, [])
            while offset < rows:
                first, length = spans[part]
                size = min(length - done, rows - offset)
                copy = pltpu.make_async_copy(
                    parts[part].at[pl.ds(first + done, size)],
                    held[plane].at[slot, pl.ds(offset, size)],
                    in_sem.at[count],
                )
                copy.start()
                incoming[plane, slot].append(copy)
                count, offset, done = (count + 1, offset + size, done + size)
                if done == length:
                    part, done = (part + 1, 0)
    outgoing, row = ([], 0)
    for plane, rows in enumerate(plane_rows):
        for square in range(squares):
            for copy in incoming[plane, 2 * square] + incoming[plane, 2 * square + 1]:
                copy.wait()
            for target, side in ((send, 1 - core), (keep, core)):
                copy = pltpu.make_async_copy(
                    held[plane].at[2 * square + side], target.at[square, pl.ds(row, rows)], out_sem.at[len(outgoing)]
                )
                copy.start()
                outgoing.append(copy)
        row += rows
    for copy in outgoing:
        copy.wait()


def split_cores(parts, plane_rows, squares, core):
    spans = tuple((first, length) for _, first, length in parts)
    arrays = [array for array, _, _ in parts]
    width = arrays[0].shape[1]
    slots = len(plane_rows) * squares * 2
    size = 2 * squares * sum(plane_rows) * width * 2
    anywhere = pl.BlockSpec(memory_space=pl.ANY)
    half = jax.ShapeDtypeStruct((squares, sum(plane_rows), width), BF16)
    return pl.pallas_call(
        partial(split_kernel, spans, tuple(plane_rows), squares),
        in_specs=[pl.BlockSpec(memory_space=pltpu.SMEM)] + [anywhere] * len(arrays),
        out_specs=[anywhere, anywhere],
        out_shape=[half, half],
        scratch_shapes=[pltpu.VMEM((2 * squares, rows, width), BF16) for rows in plane_rows]
        + [pltpu.SemaphoreType.DMA((slots + len(parts),)), pltpu.SemaphoreType.DMA((slots,))],
        compiler_params=pltpu.CompilerParams(vmem_limit_bytes=size + (2 << 20)),
        cost_estimate=pl.CostEstimate(flops=0, bytes_accessed=4 * size, transcendentals=0),
    )(core, *arrays)


def tie(values, others):
    return lax.optimization_barrier((values, others))


class Whole:
    def __init__(self, axes, weights_in, weights_out, packed, width):
        self.axes, self.width = (axes, width)
        full_in = lax.all_gather(weights_in, axes, axis=0, tiled=True)
        full_out = lax.all_gather(weights_out, axes, axis=0, tiled=True)
        devices = lax.axis_size(axes)
        slot = lax.dynamic_update_slice(
            jnp.zeros((devices,) + packed.shape, F32), packed.astype(F32)[None], (lax.axis_index(axes), 0, 0)
        )
        self.small = lax.psum(slot, axes).transpose(1, 0, 2).reshape(packed.shape[0], width).astype(BF16)
        self.in_a, self.in_b = (full_in[: 5 * width // 2], full_in[5 * width // 2 : 3 * width])
        self.in_t, self.in_qk = (full_in[: 3 * width], full_in[3 * width : 5 * width])
        self.in_v, self.in_m = (full_in[5 * width : 6 * width], full_in[6 * width :])
        self.out_t, self.out_f = (full_out[:width], full_out[width : 2 * width])
        self.out_s, self.out_m = (full_out[2 * width : 3 * width], full_out[3 * width :])
        self.grads = {}

    def tick(self, name, *values):
        return values[0] if len(values) == 1 else values

    def total(self, small):
        g = self.grads
        d_in = jnp.concatenate([g["in_t"], g["in_qk"], g["in_v"], g["in_m"]], axis=0)
        d_out = jnp.concatenate([g["out_t"], g["out_f"], g["out_s"], g["out_m"]], axis=0)
        summed_in = lax.psum_scatter(d_in, self.axes, scatter_dimension=0, tiled=True).astype(F32)
        summed_out = lax.psum_scatter(d_out, self.axes, scatter_dimension=0, tiled=True).astype(F32)
        share = self.width // lax.axis_size(self.axes)
        at = (0, lax.axis_index(self.axes) * share)
        return (summed_in, summed_out, lax.dynamic_slice(lax.psum(small, self.axes), at, (small.shape[0], share)))


class Staged:
    def __init__(self, axes, weights_in, weights_out, packed, width):
        self.axes, self.width = (axes, width)
        me = lax.axis_index(axes)
        self.plane, self.spot, self.square, self.core = (me // 8, me % 8, me % 8 // 2, me % 2)
        self.spots = jnp.bitwise_xor(jnp.arange(8, dtype=jnp.int32), self.spot)
        self.planes = (self.plane + 4 - jnp.arange(4, dtype=jnp.int32)) % 4
        self.core_ref = self.core.astype(jnp.int32).reshape(1)
        self.rows_in, self.rows_out = (weights_in.shape[0], weights_out.shape[0])
        self.weights_out, self.count = (weights_out, packed.shape[0])
        self.grads = {}
        flat = packed.reshape(1, -1)
        tail = jnp.pad(flat, ((0, 7), (0, width - flat.shape[1])))
        self.column_in, self.column_small = self.columns(
            jnp.concatenate([weights_in, tail], axis=0), (self.rows_in, 8)
        )

    def flip(self, x, bits):
        return lax.ppermute(x, self.axes, [(d, d ^ bits) for d in range(32)])

    def shift(self, x, step):
        return lax.ppermute(x, self.axes, [(d, (d + 8 * step) % 32) for d in range(32)])

    def columns(self, shard, sizes):
        pieces = [shard] + [self.shift(shard, step) for step in (1, 2, 3)]
        plan, row = ([], 0)
        for size in sizes:
            plan.append([(0, row, size)])
            row += size
        return [out[0] for out in place([pieces], plan, self.planes)]

    def over(self, piece):
        return [piece] + [self.flip(piece, bits) for bits in (2, 4, 6)]

    def cores(self, pieces):
        both = []
        for piece in pieces:
            both += [piece, self.flip(piece, 1)]
        return both

    def lay(self, groups, entries):
        out = place(groups, [entries], self.spots)[0]
        return out.reshape(-1, self.width)

    def begin(self, clip):
        rows_in, rows_out, width = (self.rows_in, self.rows_out, self.width)
        smalls = self.column_small.reshape(-1, width)
        first = jnp.concatenate([self.column_in[0], smalls], axis=0)
        self.p1, self.p2, self.p3 = (self.column_in[k] for k in (1, 2, 3))
        weights_out, first = tie(self.weights_out, first)
        p0 = self.over(first)
        p0, (clip, self.p1) = tie(p0, (clip, self.p1))
        column = self.columns(weights_out, (rows_out,))[0]
        self.q01, self.q23 = (column[:2].reshape(-1, width), column[2:].reshape(-1, width))
        self.p1 = self.over(self.p1)
        self.p0 = self.cores(p0)
        low, small = place([self.p0], [[(0, 0, rows_in)], [(0, rows_in, 32)]], self.spots)
        self.in_a = low.reshape(-1, width)
        share = width // 32
        small = small.reshape(8, 4, 8, width)[:, :, 0, : self.count * share].reshape(8, 4, self.count, share)
        self.small = small.transpose(2, 1, 0, 3).reshape(self.count, width)
        return clip

    def tick(self, name, *values):
        single = len(values) == 1
        rows_in, rows_out, width = (self.rows_in, self.rows_out, self.width)
        g = self.grads
        whole = lambda key: (g[key], 0, g[key].shape[0])
        if name == "query_t":
            values, (self.p1, self.q01) = tie(values, (self.p1, self.q01))
            self.q01 = self.over(self.q01)
            self.p1 = self.cores(self.p1)
            low = self.lay([self.p0, self.p1], [(0, 0, rows_in), (1, 0, rows_in)])
            self.in_t, self.in_qk = (low[: 3 * width], low[3 * width :])
            self.in_b = self.in_t[5 * width // 2 :]
        elif name == "mixed_t":
            values, (self.q01, self.p2) = tie(values, (self.q01, self.p2))
            self.p2 = self.over(self.p2)
            self.q01 = self.cores(self.q01)
            early = self.lay([self.q01], [(0, 0, rows_out), (0, rows_out, rows_out)])
            self.out_t, self.out_f, self.out_s = (early[k * width : (k + 1) * width] for k in range(3))
        elif name == "query_s":
            values, (self.p2, self.p3) = tie(values, (self.p2, self.p3))
            self.p3 = self.over(self.p3)
            self.p2 = self.cores(self.p2)
            self.in_v = self.lay([self.p2], [(0, 0, rows_in)])[:width]
        elif name == "mixed_s":
            values, (self.p3, self.q23) = tie(values, (self.p3, self.q23))
            self.q23 = self.over(self.q23)
            self.p3 = self.cores(self.p3)
            high = self.lay([self.p2, self.p3], [(0, 0, rows_in), (1, 0, rows_in)])
            self.in_m = high[width:]
        elif name == "hidden":
            values, self.q23 = tie(values, self.q23)
            self.q23 = self.cores(self.q23)
            entries = [(0, rows_out, rows_out), (1, 0, rows_out), (1, rows_out, rows_out)]
            self.out_m = self.lay([self.q01, self.q23], entries)[3 * width - 8 * rows_out :]
        elif name == "grad_hidden":
            first, split = (16 * rows_out - 3 * width, 24 * rows_in - 6 * width)
            self.out_first = first
            d_out_m, d_in_m = (g["out_m"], g["in_m"])
            self.part_a = self.halve(
                [(d_out_m, first, d_out_m.shape[0] - first), (d_in_m, split, d_in_m.shape[0] - split)],
                (rows_out, rows_out, rows_in),
            )
        elif name == "grad_mixed_s":
            values, self.part_a = tie(values, self.part_a)
            self.part_a = self.across(*self.part_a)
        elif name == "grad_t":
            values, self.part_a = tie(values, self.part_a)
            self.part_a = self.gathered(self.part_a)
        elif name == "grad_projected":
            first, split = (self.out_first, 24 * rows_in - 6 * width)
            self.part_b = self.halve(
                [
                    whole("in_v"),
                    (g["in_m"], 0, split),
                    whole("out_t"),
                    whole("out_f"),
                    whole("out_s"),
                    (g["out_m"], 0, first),
                ],
                (rows_in, rows_out, rows_out),
            )
            kept, values = tie(self.part_b[0], values)
            self.part_b = (kept,) + self.part_b[1:]
        elif name == "grad_mixed_t":
            values, self.part_b = tie(values, self.part_b)
            self.part_b = self.across(*self.part_b)
        elif name == "grad_in_t":
            values, self.part_b = tie(values, self.part_b)
            self.part_b = self.gathered(self.part_b)
            self.part_c = self.halve([whole("in_t"), whole("in_qk")], (rows_in, rows_in))
        return values[0] if single else values

    def halve(self, parts, plane_rows):
        keep, send = split_cores(parts, plane_rows, 4, self.core_ref)
        return (keep, self.flip(send, 1))

    def across(self, keep, other):
        result = []
        for bits in (0, 2, 4, 6):
            at = jnp.bitwise_xor(self.square, bits // 2)
            take = lambda a: lax.dynamic_index_in_dim(a, at, 0, keepdims=False).astype(F32)
            summed = (take(keep) + take(other)).astype(BF16)
            result.append(summed if bits == 0 else self.flip(summed, bits))
        return result

    def gathered(self, arrived):
        total = arrived[0].astype(F32)
        for block in arrived[1:]:
            total = total + block.astype(F32)
        return total.astype(BF16)

    def along(self, planes):
        every = jnp.stack(planes, axis=0)
        total = lax.dynamic_index_in_dim(every, self.plane, 0, keepdims=False).astype(F32)
        for step in (1, 2, 3):
            block = lax.dynamic_index_in_dim(every, (self.plane + step) % 4, 0, keepdims=False)
            total = total + self.shift(block, step).astype(F32)
        return total

    def sum_small(self, small):
        count, width = small.shape
        share = width // 32
        tiles = -(-count * share // (8 * LANES))
        slots = small.reshape(count, 32, share).transpose(1, 0, 2).reshape(32, count * share)
        slots = jnp.pad(slots, ((0, 0), (0, tiles * 8 * LANES - count * share))).reshape(32, tiles * 8, LANES)
        slots = lax.all_to_all(slots, self.axes, split_axis=0, concat_axis=0)
        return jnp.sum(slots, axis=0).reshape(-1)[: count * share].reshape(count, share)

    def total(self, small):
        rows_in, rows_out = (self.rows_in, self.rows_out)
        a, b = (self.part_a, self.part_b)
        out_planes = [b[rows_in : rows_in + rows_out], b[rows_in + rows_out :], a[:rows_out], a[rows_out : 2 * rows_out]]
        arrived = self.across(*self.part_c)
        small, arrived[0] = tie(small, arrived[0])
        summed_out = self.along(out_planes)
        owned = self.sum_small(small)
        c = self.gathered(arrived)
        summed_in = self.along([c[:rows_in], c[rows_in:], b[:rows_in], a[2 * rows_out :]])
        return (summed_in, summed_out, owned)


def norm_parts(values):
    centre = values - jnp.mean(values, axis=-1, keepdims=True)
    spread = jnp.mean(centre * centre, axis=-1, keepdims=True)
    scale = lax.rsqrt(spread + EPSILON)
    return (centre * scale, scale)


def layer_norm(values, gains, shifts):
    return (norm_parts(values)[0] * gains + shifts).astype(BF16)


def norm_backward(values, gains, grad):
    normed, scale = norm_parts(values)
    scaled = grad * gains
    first = jnp.mean(scaled, axis=-1, keepdims=True)
    second = jnp.mean(scaled * normed, axis=-1, keepdims=True)
    inner = (scaled - first - normed * second) * scale
    return (inner, jnp.sum(grad * normed, axis=0), jnp.sum(grad, axis=0))


def gelu_parts(values):
    cdf = 0.5 * (1.0 + lax.erf(values * (0.5**0.5)))
    density = jnp.exp(-0.5 * values * values) * 0.3989422804014327
    return (values * cdf, cdf + values * density)


def column_sum(rows):
    return jnp.sum(rows.astype(F32), axis=0)


def block(clip, target, leave, feed, gain_count, patches):
    shape = clip.shape
    width = shape[-1]
    grid = shape[:3]
    small32 = feed.small.astype(F32)
    gains32, shifts32, dense32 = (small32[:gain_count], small32[gain_count:-1], small32[-1])
    flat = lambda a: a.reshape(-1, a.shape[-1])
    cube = lambda a: a.reshape(grid + (a.shape[-1],))
    grads = feed.grads
    start = clip.reshape(-1, width).astype(F32)
    normed_t = layer_norm(start, gains32[0], shifts32[0])
    project_a = nt(normed_t, feed.in_a).astype(BF16)
    project_a, normed_t = feed.tick("query_t", project_a, normed_t)
    project_b = nt(normed_t, feed.in_b).astype(BF16)
    project_t = [cube(project_a), cube(project_b)]
    mixed_t = attention_call(forward_kernel, 2, project_t, (width,), True, patches)[0]
    mixed_t = flat(feed.tick("mixed_t", mixed_t))
    projected_t = (nn(mixed_t, feed.out_t) + shifts32[3]).astype(BF16)
    branch_t = (nn(projected_t, feed.out_f) + shifts32[4]).astype(BF16)
    after_t = start + branch_t.astype(F32)
    normed_s = layer_norm(after_t, gains32[1], shifts32[1])
    project_qk = nt(normed_s, feed.in_qk).astype(BF16)
    project_qk, normed_s = feed.tick("query_s", project_qk, normed_s)
    project_v = nt(normed_s, feed.in_v).astype(BF16)
    project_s = [cube(project_qk), cube(project_v)]
    mixed_s = attention_call(forward_kernel, 2, project_s, (width,), False, patches)[0]
    mixed_s = flat(feed.tick("mixed_s", mixed_s))
    grad_low = flat(target(mixed_s))
    after_s = after_t + (nn(mixed_s, feed.out_s) + shifts32[5])
    normed_m = layer_norm(after_s, gains32[2], shifts32[2])
    hidden_pre = nt(normed_m, feed.in_m) + shifts32[6:].reshape(-1)
    hidden32, slope32 = gelu_parts(hidden_pre)
    hidden, slope = feed.tick("hidden", hidden32.astype(BF16), slope32.astype(BF16))
    output = (after_s + (nn(hidden, feed.out_m) + dense32)).astype(BF16)
    output = leave(output.reshape(shape))

    grad_out = grad_low.astype(F32)
    grads["out_m"] = tn(hidden, grad_low).astype(BF16)
    s_dense = column_sum(grad_low)
    grad_pre = (nt(grad_low, feed.out_m) * slope.astype(F32)).astype(BF16)
    grads["in_m"] = tn(grad_pre, normed_m).astype(BF16)
    grad_pre = feed.tick("grad_hidden", grad_pre)
    s_hidden = column_sum(grad_pre).reshape(-1, width)
    part, g_m, b_m = norm_backward(after_s, gains32[2], nn(grad_pre, feed.in_m))
    grad_s = grad_out + part
    grad_branch_s = grad_s.astype(BF16)
    grads["out_s"] = tn(mixed_s, grad_branch_s).astype(BF16)
    s_space = column_sum(grad_branch_s)
    grad_mixed_s = nt(grad_branch_s, feed.out_s).astype(BF16)
    grad_mixed_s, output = feed.tick("grad_mixed_s", grad_mixed_s, output)
    grad_qk, grad_v = attention_call(
        backward_kernel, 2, project_s + [cube(grad_mixed_s)], (2 * width, width), False, patches
    )
    grad_qk, grad_v = (flat(grad_qk), flat(grad_v))
    grads["in_qk"] = tn(grad_qk, normed_s).astype(BF16)
    grads["in_v"] = tn(grad_v, normed_s).astype(BF16)
    part, g_s, b_s = norm_backward(after_t, gains32[1], nn(grad_qk, feed.in_qk) + nn(grad_v, feed.in_v))
    grad_t = grad_s + part
    grad_branch_t = feed.tick("grad_t", grad_t.astype(BF16))
    grads["out_f"] = tn(projected_t, grad_branch_t).astype(BF16)
    s_fc = column_sum(grad_branch_t)
    grad_projected = nt(grad_branch_t, feed.out_f).astype(BF16)
    grads["out_t"] = tn(mixed_t, grad_projected).astype(BF16)
    grad_projected = feed.tick("grad_projected", grad_projected)
    s_time = column_sum(grad_projected)
    grad_mixed_t = feed.tick("grad_mixed_t", nt(grad_projected, feed.out_t).astype(BF16))
    grad_project_t = attention_call(
        backward_kernel, 2, project_t + [cube(grad_mixed_t)], (3 * width,), True, patches
    )[0]
    grad_project_t = flat(grad_project_t)
    grads["in_t"] = tn(grad_project_t, normed_t).astype(BF16)
    grad_project_t = feed.tick("grad_in_t", grad_project_t)
    part, g_t, b_t = norm_backward(start, gains32[0], nn(grad_project_t, feed.in_t))
    grad_clip = (grad_t + part.astype(BF16).astype(F32)).astype(BF16)
    small = jnp.concatenate(
        [
            jnp.stack([g_t, g_s, g_m, b_t, b_s, b_m, s_time, s_fc, s_space], axis=0),
            s_hidden,
            s_dense[None, :],
        ],
        axis=0,
    )
    return (output, leave(grad_clip.reshape(shape)).astype(F32)) + feed.total(small)


def shards(clips_in, cotangent, clip_live, weights_in, weights_out, norm_gain, shift_rows, dense_shift):
    both = ("dp", "seq")
    group = lax.axis_size("seq")
    count, _, patches, width = clips_in.shape
    own = count // group
    rows = -(-patches // SUB) * SUB
    gain_count = norm_gain.shape[0]
    shift_count = shift_rows.shape[0]
    staged = lax.axis_size(both) == 32 and group == 4 and weights_in.shape[0] == 240 and weights_out.shape[0] == 168

    def enter(x):
        x = lax.all_to_all(x, "seq", split_axis=0, concat_axis=1, tiled=True)
        return jnp.pad(x, ((0, 0), (0, 0), (0, rows - patches), (0, 0)))

    def leave(x):
        x = x[:, :, :patches]
        return lax.all_to_all(x, "seq", split_axis=1, concat_axis=0, tiled=True)

    packed = jnp.concatenate([norm_gain, shift_rows, dense_shift[None, :]], axis=0)
    feed = (Staged if staged else Whole)(both, weights_in, weights_out, packed, width)
    clip = enter(clips_in)
    if staged:
        clip = feed.begin(clip)
    live = lax.dynamic_slice(clip_live, (lax.axis_index("seq") * own,), (own,)).astype(BF16)

    def target(after):
        gradient = cotangent * 1
        if staged:
            gradient = tie(gradient, after)[0]
        return enter(gradient) * live[:, None, None, None]

    output, grad_clip, summed_in, summed_out, owned = block(clip, target, leave, feed, gain_count, patches)
    return (
        output,
        grad_clip,
        summed_in,
        summed_out,
        owned[:gain_count],
        owned[gain_count : gain_count + shift_count],
        owned[-1],
    )


def solution(mesh):
    clip = P("dp", "seq", None, None)
    row = P(("dp", "seq"), None)
    col = P(None, ("dp", "seq"))
    flat = P(("dp", "seq"))
    return jax.shard_map(
        shards,
        mesh=mesh,
        in_specs=(clip, clip, P("dp"), row, row, col, col, flat),
        out_specs=(clip, clip, row, row, col, col, flat),
        check_vma=False,
    )
```

```python
from functools import partial

import jax
import jax.numpy as jnp
from jax import lax
from jax.experimental import pallas as pl
from jax.experimental.pallas import tpu as pltpu
from jax.sharding import PartitionSpec as P

HEADS = 12
HEAD_DIM = 64
EPSILON = 1e-06
PAIRS = HEADS // 2
LANES = 2 * HEAD_DIM
SUB = 16
NEG = -1e30
F32 = jnp.float32
BF16 = jnp.bfloat16


def nt(left, right):
    return lax.dot_general(left, right, (((1,), (1,)), ((), ())), preferred_element_type=F32)


def nn(left, right):
    return lax.dot_general(left, right, (((1,), (0,)), ((), ())), preferred_element_type=F32)


def tn(left, right):
    return lax.dot_general(left, right, (((0,), (0,)), ((), ())), preferred_element_type=F32)


def split_heads(pair):
    first = lax.broadcasted_iota(jnp.int32, pair.shape, 1) < HEAD_DIM
    zero = jnp.zeros_like(pair)
    return jnp.concatenate([jnp.where(first, pair, zero), jnp.where(first, zero, pair)], axis=0)


def join_heads(stacked):
    rows = stacked.shape[0] // 2
    first = lax.broadcasted_iota(jnp.int32, (rows, LANES), 1) < HEAD_DIM
    return jnp.where(first, stacked[:rows], stacked[rows:])


def pair_forward(queries, keys, values, keep):
    stacked = split_heads(queries * jnp.asarray(HEAD_DIM**-0.5, BF16))
    scores = jnp.where(keep, nt(stacked, keys), NEG)
    top = jnp.max(scores, axis=1, keepdims=True)
    weights = jnp.exp(scores - top)
    total = jnp.sum(weights, axis=1, keepdims=True)
    probs = (weights * (1.0 / total)).astype(BF16)
    return join_heads(nn(probs, values)).astype(BF16)


def pair_backward(queries, keys, values, grad, keep):
    scaling = HEAD_DIM**-0.5
    stacked = split_heads(queries * jnp.asarray(scaling, BF16))
    grads = split_heads(grad)
    scores = jnp.where(keep, nt(keys, stacked), NEG)
    top = jnp.max(scores, axis=0, keepdims=True)
    weights = jnp.exp(scores - top)
    total = jnp.sum(weights, axis=0, keepdims=True)
    probs = weights * (1.0 / total)
    grad_probs = nt(values, grads)
    mean = jnp.sum(probs * grad_probs, axis=0, keepdims=True)
    grad_scores = (probs * (grad_probs - mean)).astype(BF16)
    grad_values = nn(probs.astype(BF16), grads)
    grad_keys = nn(grad_scores, stacked)
    grad_queries = join_heads(tn(grad_scores, keys)) * scaling
    return (grad_queries.astype(BF16), grad_keys.astype(BF16), grad_values.astype(BF16))


def columns(kind, pair):
    start = (kind * PAIRS + pair) * LANES
    return slice(start, start + LANES)


def find(refs, kind, pair):
    cols = columns(kind, pair)
    for ref in refs:
        size = ref.shape[-1]
        if cols.start < size:
            return (ref, cols)
        cols = slice(cols.start - size, cols.stop - size)


def load(refs, kind, pair):
    ref, cols = find(refs, kind, pair)
    return ref[..., cols].reshape(-1, LANES)


def store(refs, kind, pair, block):
    ref, cols = find(refs, kind, pair)
    ref[..., cols] = block.reshape(ref.shape[:-1] + (LANES,))


def keep_mask(shape, key_axis, group, patches):
    key = lax.broadcasted_iota(jnp.int32, shape, key_axis)
    if group is None:
        return key < patches
    query = lax.broadcasted_iota(jnp.int32, shape, 1 - key_axis)
    return (key % group) == (query % group)


def forward_kernel(group, patches, count, *refs):
    project, mixed = (refs[:count], refs[count:])
    rows = project[0].size // project[0].shape[-1]
    keep = keep_mask((2 * rows, rows), 1, group, patches)
    for pair in range(PAIRS):
        block = pair_forward(*[load(project, kind, pair) for kind in range(3)], keep)
        store(mixed, 0, pair, block)


def backward_kernel(group, patches, count, *refs):
    project, grad, outs = (refs[:count], refs[count : count + 1], refs[count + 1 :])
    rows = project[0].size // project[0].shape[-1]
    keep = keep_mask((rows, 2 * rows), 0, group, patches)
    for pair in range(PAIRS):
        results = pair_backward(*[load(project, kind, pair) for kind in range(3)], load(grad, 0, pair), keep)
        for kind, result in enumerate(results):
            store(outs, kind, pair, result)


def attention_call(kernel, count, arrays, out_cols, temporal, patches):
    clips, frames, rows, _ = arrays[0].shape
    if temporal:
        group, steps, shape = SUB, rows // SUB, (1, frames, SUB)
        index = lambda c, i: (c, 0, i, 0)
    else:
        group, steps, shape = None, frames, (1, 1, rows)
        index = lambda c, i: (c, i, 0, 0)
    tokens = clips * frames * rows
    backward = kernel is backward_kernel
    return pl.pallas_call(
        partial(kernel, group, patches, count),
        grid=(clips, steps),
        in_specs=[pl.BlockSpec(shape + (a.shape[-1],), index) for a in arrays],
        out_specs=[pl.BlockSpec(shape + (cols,), index) for cols in out_cols],
        out_shape=[jax.ShapeDtypeStruct((clips, frames, rows, cols), BF16) for cols in out_cols],
        compiler_params=pltpu.CompilerParams(dimension_semantics=("arbitrary", "arbitrary")),
        cost_estimate=pl.CostEstimate(
            flops=tokens * (14_000_000 if backward else 9_000_000), bytes_accessed=0, transcendentals=0
        ),
    )(*arrays)


def eights(rows):
    return rows.reshape(rows.shape[:-2] + (-1, 8, rows.shape[-1]))


def place_kernel(outs_plan, blocks, groups, dest_ref, *refs):
    pieces, refs = (refs[: groups * blocks], refs[groups * blocks :])
    outs, refs = (refs[: len(outs_plan)], refs[len(outs_plan) :])
    held, in_sem, out_sem = (refs[:-2], refs[-2], refs[-1])
    moves, slot = ([], 0)
    for target, entries in enumerate(outs_plan):
        for entry, (group, row, rows) in enumerate(entries):
            for block in range(blocks):
                buffer = held[target].at[entry, block]
                source = pieces[group * blocks + block].at[pl.ds(row // 8, rows // 8)]
                fetch = pltpu.make_async_copy(source, buffer, in_sem.at[slot])
                fetch.start()
                write = pltpu.make_async_copy(buffer, outs[target].at[entry, dest_ref[block]], out_sem.at[slot])
                moves.append((fetch, write))
                slot += 1
    for fetch, write in moves:
        fetch.wait()
        write.start()
    for _, write in moves:
        write.wait()


def place(groups, outs_plan, dest):
    blocks = len(groups[0])
    width = groups[0][0].shape[1]
    shapes = [(len(entries), blocks, entries[0][2] // 8, 8, width) for entries in outs_plan]
    slots = sum(len(entries) for entries in outs_plan) * blocks
    size = sum(16 * s[0] * s[1] * s[2] * s[4] for s in shapes)
    flat = [eights(piece) for group in groups for piece in group]
    anywhere = pl.BlockSpec(memory_space=pl.ANY)
    outs = pl.pallas_call(
        partial(place_kernel, tuple(tuple(e) for e in outs_plan), blocks, len(groups)),
        in_specs=[pl.BlockSpec(memory_space=pltpu.SMEM)] + [anywhere] * len(flat),
        out_specs=[anywhere] * len(shapes),
        out_shape=[jax.ShapeDtypeStruct(s, BF16) for s in shapes],
        scratch_shapes=[pltpu.VMEM(s, BF16) for s in shapes]
        + [pltpu.SemaphoreType.DMA((slots,)), pltpu.SemaphoreType.DMA((slots,))],
        compiler_params=pltpu.CompilerParams(vmem_limit_bytes=size + (2 << 20)),
        cost_estimate=pl.CostEstimate(flops=0, bytes_accessed=4 * size, transcendentals=0),
    )(dest, *flat)
    return [out.reshape(out.shape[:2] + (-1, width)) for out in outs]


def split_kernel(spans, plane_rows, squares, core_ref, *refs):
    parts, refs = (refs[: len(spans)], refs[len(spans) :])
    keep, send = refs[:2]
    held, in_sem, out_sem = (refs[2:-2], refs[-2], refs[-1])
    core = core_ref[0]
    incoming, count, part, done = ({}, 0, 0, 0)
    for plane, rows in enumerate(plane_rows):
        for slot in range(2 * squares):
            offset, incoming[plane, slot] = (0, [])
            while offset < rows:
                first, length = spans[part]
                size = min(length - done, rows - offset)
                copy = pltpu.make_async_copy(
                    parts[part].at[pl.ds((first + done) // 8, size // 8)],
                    held[plane].at[slot, pl.ds(offset // 8, size // 8)],
                    in_sem.at[count],
                )
                copy.start()
                incoming[plane, slot].append(copy)
                count, offset, done = (count + 1, offset + size, done + size)
                if done == length:
                    part, done = (part + 1, 0)
    outgoing, row = ([], 0)
    for plane, rows in enumerate(plane_rows):
        for square in range(squares):
            for copy in incoming[plane, 2 * square] + incoming[plane, 2 * square + 1]:
                copy.wait()
            for target, side in ((send, 1 - core), (keep, core)):
                copy = pltpu.make_async_copy(
                    held[plane].at[2 * square + side], target.at[square, pl.ds(row // 8, rows // 8)], out_sem.at[len(outgoing)]
                )
                copy.start()
                outgoing.append(copy)
        row += rows
    for copy in outgoing:
        copy.wait()


def split_cores(parts, plane_rows, squares, core):
    spans = tuple((first, length) for _, first, length in parts)
    arrays = [eights(array) for array, _, _ in parts]
    width = arrays[0].shape[-1]
    slots = len(plane_rows) * squares * 2
    size = 2 * squares * sum(plane_rows) * width * 2
    anywhere = pl.BlockSpec(memory_space=pl.ANY)
    half = jax.ShapeDtypeStruct((squares, sum(plane_rows) // 8, 8, width), BF16)
    outs = pl.pallas_call(
        partial(split_kernel, spans, tuple(plane_rows), squares),
        in_specs=[pl.BlockSpec(memory_space=pltpu.SMEM)] + [anywhere] * len(arrays),
        out_specs=[anywhere, anywhere],
        out_shape=[half, half],
        scratch_shapes=[pltpu.VMEM((2 * squares, rows // 8, 8, width), BF16) for rows in plane_rows]
        + [pltpu.SemaphoreType.DMA((slots + len(parts),)), pltpu.SemaphoreType.DMA((slots,))],
        compiler_params=pltpu.CompilerParams(vmem_limit_bytes=size + (2 << 20)),
        cost_estimate=pl.CostEstimate(flops=0, bytes_accessed=4 * size, transcendentals=0),
    )(core, *arrays)
    return [out.reshape(squares, -1, width) for out in outs]


def tie(values, others):
    return lax.optimization_barrier((values, others))


class Whole:
    def __init__(self, axes, weights_in, weights_out, packed, width):
        self.axes, self.width = (axes, width)
        full_in = lax.all_gather(weights_in, axes, axis=0, tiled=True)
        full_out = lax.all_gather(weights_out, axes, axis=0, tiled=True)
        devices = lax.axis_size(axes)
        slot = lax.dynamic_update_slice(
            jnp.zeros((devices,) + packed.shape, F32), packed.astype(F32)[None], (lax.axis_index(axes), 0, 0)
        )
        self.small = lax.psum(slot, axes).transpose(1, 0, 2).reshape(packed.shape[0], width).astype(BF16)
        self.in_a, self.in_b = (full_in[: 5 * width // 2], full_in[5 * width // 2 : 3 * width])
        self.in_t, self.in_qk = (full_in[: 3 * width], full_in[3 * width : 5 * width])
        self.in_v, self.in_m = (full_in[5 * width : 6 * width], full_in[6 * width :])
        self.out_t, self.out_f = (full_out[:width], full_out[width : 2 * width])
        self.out_s, self.out_m = (full_out[2 * width : 3 * width], full_out[3 * width :])
        self.grads = {}

    def tick(self, name, *values):
        return values[0] if len(values) == 1 else values

    def total(self, small):
        g = self.grads
        d_in = jnp.concatenate([g["in_t"], g["in_qk"], g["in_v"], g["in_m"]], axis=0)
        d_out = jnp.concatenate([g["out_t"], g["out_f"], g["out_s"], g["out_m"]], axis=0)
        summed_in = lax.psum_scatter(d_in, self.axes, scatter_dimension=0, tiled=True).astype(F32)
        summed_out = lax.psum_scatter(d_out, self.axes, scatter_dimension=0, tiled=True).astype(F32)
        share = self.width // lax.axis_size(self.axes)
        at = (0, lax.axis_index(self.axes) * share)
        return (summed_in, summed_out, lax.dynamic_slice(lax.psum(small, self.axes), at, (small.shape[0], share)))


class Staged:
    def __init__(self, axes, weights_in, weights_out, packed, width):
        self.axes, self.width = (axes, width)
        me = lax.axis_index(axes)
        self.plane, self.spot, self.square, self.core = (me // 8, me % 8, me % 8 // 2, me % 2)
        self.spots = jnp.bitwise_xor(jnp.arange(8, dtype=jnp.int32), self.spot)
        self.planes = (self.plane + 4 - jnp.arange(4, dtype=jnp.int32)) % 4
        self.core_ref = self.core.astype(jnp.int32).reshape(1)
        self.rows_in, self.rows_out = (weights_in.shape[0], weights_out.shape[0])
        self.weights_out, self.count = (weights_out, packed.shape[0])
        self.grads = {}
        flat = packed.reshape(1, -1)
        tail = jnp.pad(flat, ((0, 7), (0, width - flat.shape[1])))
        pieces = self.shifted(jnp.concatenate([weights_in, tail], axis=0))
        self.column_in, self.column_small = self.columns(pieces, (self.rows_in, 8))

    def flip(self, x, bits):
        return lax.ppermute(x, self.axes, [(d, d ^ bits) for d in range(32)])

    def shift(self, x, step):
        return lax.ppermute(x, self.axes, [(d, (d + 8 * step) % 32) for d in range(32)])

    def shifted(self, shard):
        return [shard] + [self.shift(shard, step) for step in (1, 2, 3)]

    def columns(self, pieces, sizes):
        plan, row = ([], 0)
        for size in sizes:
            plan.append([(0, row, size)])
            row += size
        return [out[0] for out in place([pieces], plan, self.planes)]

    def over(self, piece):
        return [piece] + [self.flip(piece, bits) for bits in (2, 4, 6)]

    def cores(self, pieces):
        both = []
        for piece in pieces:
            both += [piece, self.flip(piece, 1)]
        return both

    def lay(self, groups, entries):
        out = place(groups, [entries], self.spots)[0]
        return out.reshape(-1, self.width)

    def begin(self):
        rows_in, rows_out, width = (self.rows_in, self.rows_out, self.width)
        smalls = self.column_small.reshape(-1, width)
        first = jnp.concatenate([self.column_in[0], smalls], axis=0)
        self.p1, self.p2, self.p3 = (self.column_in[k] for k in (1, 2, 3))
        p0 = self.over(first)
        p0[0], weights_out = tie(first, self.weights_out)
        self.q = self.shifted(weights_out)
        p0, self.p1 = tie(p0, self.p1)
        self.p1 = self.over(self.p1)
        self.p0 = self.cores(p0)
        low, small = place([self.p0], [[(0, 0, rows_in)], [(0, rows_in, 32)]], self.spots)
        self.in_a = low.reshape(-1, width)
        share = width // 32
        small = small.reshape(8, 4, 8, width)[:, :, 0, : self.count * share].reshape(8, 4, self.count, share)
        self.small = small.transpose(2, 1, 0, 3).reshape(self.count, width)

    def tick(self, name, *values):
        single = len(values) == 1
        rows_in, rows_out, width = (self.rows_in, self.rows_out, self.width)
        g = self.grads
        whole = lambda key: (g[key], 0, g[key].shape[0])
        if name == "query_t":
            values, (self.p1, self.q) = tie(values, (self.p1, self.q))
            column = self.columns(self.q, (rows_out,))[0]
            self.q01, self.q23 = (column[:2].reshape(-1, width), column[2:].reshape(-1, width))
            self.q01 = self.over(self.q01)
            self.p1 = self.cores(self.p1)
            low = self.lay([self.p0, self.p1], [(0, 0, rows_in), (1, 0, rows_in)])
            self.in_t, self.in_qk = (low[: 3 * width], low[3 * width :])
            self.in_b = self.in_t[5 * width // 2 :]
        elif name == "mixed_t":
            values, (self.q01, self.p2) = tie(values, (self.q01, self.p2))
            self.p2 = self.over(self.p2)
            self.q01 = self.cores(self.q01)
            early = self.lay([self.q01], [(0, 0, rows_out), (0, rows_out, rows_out)])
            self.out_t, self.out_f, self.out_s = (early[k * width : (k + 1) * width] for k in range(3))
        elif name == "query_s":
            values, (self.p2, self.p3) = tie(values, (self.p2, self.p3))
            self.p3 = self.over(self.p3)
            self.p2 = self.cores(self.p2)
            self.in_v = self.lay([self.p2], [(0, 0, rows_in)])[:width]
        elif name == "mixed_s":
            values, (self.p3, self.q23) = tie(values, (self.p3, self.q23))
            self.q23 = self.over(self.q23)
            self.p3 = self.cores(self.p3)
            high = self.lay([self.p2, self.p3], [(0, 0, rows_in), (1, 0, rows_in)])
            self.in_m = high[width:]
        elif name == "hidden":
            values, self.q23 = tie(values, self.q23)
            self.q23 = self.cores(self.q23)
            entries = [(0, rows_out, rows_out), (1, 0, rows_out), (1, rows_out, rows_out)]
            self.out_m = self.lay([self.q01, self.q23], entries)[3 * width - 8 * rows_out :]
        elif name == "out_m":
            start = 16 * rows_out - 3 * width
            d_out_m = g["out_m"]
            self.kept, send = self.halve([(d_out_m, start, d_out_m.shape[0] - start)], (rows_out, rows_out))
            values, send = tie(values, send)
            self.other = self.flip(send, 1)
        elif name == "grad_pre":
            values, (self.kept, self.other) = tie(values, (self.kept, self.other))
            self.d_q23 = self.across(self.kept, self.other)
        elif name == "in_m":
            start = 24 * rows_in - 6 * width
            d_in_m = g["in_m"]
            self.kept, send = self.halve([(d_in_m, start, d_in_m.shape[0] - start)], (rows_in,))
            values, send = tie(values, send)
            self.other = self.flip(send, 1)
        elif name == "grad_mixed_s":
            values, (self.d_q23, self.kept, self.other) = tie(values, (self.d_q23, self.kept, self.other))
            self.d_q23 = self.gathered(self.d_q23)
            self.d_p3 = self.across(self.kept, self.other)
        elif name == "grad_s":
            values, self.d_p3 = tie(values, self.d_p3)
            self.d_p3 = self.gathered(self.d_p3)
        elif name == "in_v":
            start = 24 * rows_in - 6 * width
            self.kept, send = self.halve([whole("in_v"), (g["in_m"], 0, start)], (rows_in,))
            values, send = tie(values, send)
            self.other = self.flip(send, 1)
        elif name == "in_qk":
            values, (self.kept, self.other) = tie(values, (self.kept, self.other))
            self.d_p2 = self.across(self.kept, self.other)
        elif name == "grad_t":
            values, self.d_p2 = tie(values, self.d_p2)
            self.d_p2 = self.gathered(self.d_p2)
        elif name == "out_t":
            start = 16 * rows_out - 3 * width
            self.kept, send = self.halve(
                [whole("out_t"), whole("out_f"), whole("out_s"), (g["out_m"], 0, start)], (rows_out, rows_out)
            )
            values, send = tie(values, send)
            self.other = self.flip(send, 1)
        elif name == "grad_mixed_t":
            values, (self.kept, self.other) = tie(values, (self.kept, self.other))
            self.d_q01 = self.across(self.kept, self.other)
        elif name == "grad_project_t":
            values, self.d_q01 = tie(values, self.d_q01)
            self.d_q01 = self.gathered(self.d_q01)
            planes = [a[k * rows_out : (k + 1) * rows_out] for a in (self.d_q01, self.d_q23) for k in range(2)]
            self.out_pieces = self.along(planes)
        elif name == "in_t":
            kept, send = self.halve([whole("in_t"), whole("in_qk")], (rows_in, rows_in))
            half = lambda a, x: lax.dynamic_slice_in_dim(a, 2 * x, 2, 0).astype(F32)
            other = self.flip(send, 1)
            x = self.square // 2
            send = (half(kept, 1 - x) + half(other, 1 - x)).astype(BF16)
            own = (half(kept, x) + half(other, x)).astype(BF16)
            values, (own, send) = tie(values, (own, send))
            self.last = (own, self.flip(send, 4))
        elif name == "grad_clip":
            values, (own, other) = tie(values, self.last)
            y = self.square % 2
            line = lambda a, y: lax.dynamic_index_in_dim(a, y, 0, keepdims=False).astype(F32)
            send = (line(own, 1 - y) + line(other, 1 - y)).astype(BF16)
            arrived = self.flip(send, 2)
            values, (arrived, self.out_pieces) = tie(values, (arrived, self.out_pieces))
            self.d_p01 = (line(own, y) + line(other, y) + arrived.astype(F32)).astype(BF16)
        return values[0] if single else values

    def halve(self, parts, plane_rows):
        return split_cores(parts, plane_rows, 4, self.core_ref)

    def across(self, keep, other):
        result = []
        for bits in (0, 2, 4, 6):
            at = jnp.bitwise_xor(self.square, bits // 2)
            take = lambda a: lax.dynamic_index_in_dim(a, at, 0, keepdims=False).astype(F32)
            summed = (take(keep) + take(other)).astype(BF16)
            result.append(summed if bits == 0 else self.flip(summed, bits))
        return result

    def gathered(self, arrived):
        return self.added(arrived).astype(BF16)

    def along(self, planes):
        every = jnp.stack(planes, axis=0)
        pieces = [lax.dynamic_index_in_dim(every, self.plane, 0, keepdims=False)]
        for step in (1, 2, 3):
            block = lax.dynamic_index_in_dim(every, (self.plane + step) % 4, 0, keepdims=False)
            pieces.append(self.shift(block, step))
        return pieces

    def added(self, pieces):
        total = pieces[0].astype(F32)
        for piece in pieces[1:]:
            total = total + piece.astype(F32)
        return total

    def sum_small(self, small):
        count, width = small.shape
        share = width // 32
        tiles = -(-count * share // (8 * LANES))
        slots = small.reshape(count, 32, share).transpose(1, 0, 2).reshape(32, count * share)
        slots = jnp.pad(slots, ((0, 0), (0, tiles * 8 * LANES - count * share))).reshape(32, tiles * 8, LANES)
        slots = lax.all_to_all(slots, self.axes, split_axis=0, concat_axis=0)
        return jnp.sum(slots, axis=0).reshape(-1)[: count * share].reshape(count, share)

    def total(self, small):
        last, rows_in = (self.d_p01, self.rows_in)
        pieces = self.along([last[:rows_in], last[rows_in:], self.d_p2, self.d_p3])
        return (self.added(pieces), self.added(self.out_pieces), self.sum_small(small))


def norm_parts(values):
    centre = values - jnp.mean(values, axis=-1, keepdims=True)
    spread = jnp.mean(centre * centre, axis=-1, keepdims=True)
    scale = lax.rsqrt(spread + EPSILON)
    return (centre * scale, scale)


def layer_norm(values, gains, shifts):
    return (norm_parts(values)[0] * gains + shifts).astype(BF16)


def norm_backward(values, gains, grad):
    normed, scale = norm_parts(values)
    scaled = grad * gains
    first = jnp.mean(scaled, axis=-1, keepdims=True)
    second = jnp.mean(scaled * normed, axis=-1, keepdims=True)
    inner = (scaled - first - normed * second) * scale
    return (inner, jnp.sum(grad * normed, axis=0), jnp.sum(grad, axis=0))


def gelu_parts(values):
    cdf = 0.5 * (1.0 + lax.erf(values * (0.5**0.5)))
    density = jnp.exp(-0.5 * values * values) * 0.3989422804014327
    return (values * cdf, cdf + values * density)


def column_sum(rows):
    return jnp.sum(rows.astype(F32), axis=0)


def block(clip, target, leave, feed, gain_count, patches):
    shape = clip.shape
    width = shape[-1]
    grid = shape[:3]
    small32 = feed.small.astype(F32)
    gains32, shifts32, dense32 = (small32[:gain_count], small32[gain_count:-1], small32[-1])
    flat = lambda a: a.reshape(-1, a.shape[-1])
    cube = lambda a: a.reshape(grid + (a.shape[-1],))
    grads = feed.grads
    start = clip.reshape(-1, width).astype(F32)
    normed_t = layer_norm(start, gains32[0], shifts32[0])
    project_a = nt(normed_t, feed.in_a).astype(BF16)
    project_a, normed_t = feed.tick("query_t", project_a, normed_t)
    project_b = nt(normed_t, feed.in_b).astype(BF16)
    project_t = [cube(project_a), cube(project_b)]
    mixed_t = attention_call(forward_kernel, 2, project_t, (width,), True, patches)[0]
    mixed_t = flat(feed.tick("mixed_t", mixed_t))
    projected_t = (nn(mixed_t, feed.out_t) + shifts32[3]).astype(BF16)
    branch_t = (nn(projected_t, feed.out_f) + shifts32[4]).astype(BF16)
    after_t = start + branch_t.astype(F32)
    normed_s = layer_norm(after_t, gains32[1], shifts32[1])
    project_qk = nt(normed_s, feed.in_qk).astype(BF16)
    project_qk, normed_s = feed.tick("query_s", project_qk, normed_s)
    project_v = nt(normed_s, feed.in_v).astype(BF16)
    project_s = [cube(project_qk), cube(project_v)]
    mixed_s = attention_call(forward_kernel, 2, project_s, (width,), False, patches)[0]
    mixed_s = flat(feed.tick("mixed_s", mixed_s))
    grad_low = flat(target(mixed_s))
    after_s = after_t + (nn(mixed_s, feed.out_s) + shifts32[5])
    normed_m = layer_norm(after_s, gains32[2], shifts32[2])
    hidden_pre = nt(normed_m, feed.in_m) + shifts32[6:].reshape(-1)
    hidden32, slope32 = gelu_parts(hidden_pre)
    hidden, slope = feed.tick("hidden", hidden32.astype(BF16), slope32.astype(BF16))
    output = (after_s + (nn(hidden, feed.out_m) + dense32)).astype(BF16)
    output = leave(output.reshape(shape))

    grad_out = grad_low.astype(F32)
    grads["out_m"] = tn(hidden, grad_low).astype(BF16)
    grad_low = feed.tick("out_m", grad_low)
    s_dense = column_sum(grad_low)
    grad_pre = (nt(grad_low, feed.out_m) * slope.astype(F32)).astype(BF16)
    grad_pre = feed.tick("grad_pre", grad_pre)
    grads["in_m"] = tn(grad_pre, normed_m).astype(BF16)
    grad_pre = feed.tick("in_m", grad_pre)
    s_hidden = column_sum(grad_pre).reshape(-1, width)
    part, g_m, b_m = norm_backward(after_s, gains32[2], nn(grad_pre, feed.in_m))
    grad_s = grad_out + part
    grad_branch_s = grad_s.astype(BF16)
    grads["out_s"] = tn(mixed_s, grad_branch_s).astype(BF16)
    s_space = column_sum(grad_branch_s)
    grad_mixed_s = nt(grad_branch_s, feed.out_s).astype(BF16)
    grad_mixed_s, output = feed.tick("grad_mixed_s", grad_mixed_s, output)
    grad_qk, grad_v = attention_call(
        backward_kernel, 2, project_s + [cube(grad_mixed_s)], (2 * width, width), False, patches
    )
    grad_qk, grad_v = feed.tick("grad_s", flat(grad_qk), flat(grad_v))
    grads["in_v"] = tn(grad_v, normed_s).astype(BF16)
    grad_qk, grad_v = feed.tick("in_v", grad_qk, grad_v)
    d_in_qk = tn(grad_qk, normed_s).astype(BF16)
    grads["in_qk"], grad_qk, grad_v = feed.tick("in_qk", d_in_qk, grad_qk, grad_v)
    part, g_s, b_s = norm_backward(after_t, gains32[1], nn(grad_qk, feed.in_qk) + nn(grad_v, feed.in_v))
    grad_t = grad_s + part
    grad_branch_t = feed.tick("grad_t", grad_t.astype(BF16))
    grads["out_f"] = tn(projected_t, grad_branch_t).astype(BF16)
    s_fc = column_sum(grad_branch_t)
    grad_projected = nt(grad_branch_t, feed.out_f).astype(BF16)
    grads["out_t"] = tn(mixed_t, grad_projected).astype(BF16)
    grad_projected = feed.tick("out_t", grad_projected)
    s_time = column_sum(grad_projected)
    grad_mixed_t = feed.tick("grad_mixed_t", nt(grad_projected, feed.out_t).astype(BF16))
    grad_project_t = attention_call(
        backward_kernel, 2, project_t + [cube(grad_mixed_t)], (3 * width,), True, patches
    )[0]
    grad_project_t = feed.tick("grad_project_t", flat(grad_project_t))
    grads["in_t"] = tn(grad_project_t, normed_t).astype(BF16)
    grad_project_t = feed.tick("in_t", grad_project_t)
    part, g_t, b_t = norm_backward(start, gains32[0], nn(grad_project_t, feed.in_t))
    grad_clip = (grad_t + part.astype(BF16).astype(F32)).astype(BF16)
    grad_clip, g_t, b_t, s_time = feed.tick("grad_clip", grad_clip, g_t, b_t, s_time)
    small = jnp.concatenate(
        [
            jnp.stack([g_t, g_s, g_m, b_t, b_s, b_m, s_time, s_fc, s_space], axis=0),
            s_hidden,
            s_dense[None, :],
        ],
        axis=0,
    )
    return (output, leave(grad_clip.reshape(shape)).astype(F32)) + feed.total(small)


def shards(clips_in, cotangent, clip_live, weights_in, weights_out, norm_gain, shift_rows, dense_shift):
    both = ("dp", "seq")
    group = lax.axis_size("seq")
    count, _, patches, width = clips_in.shape
    own = count // group
    rows = -(-patches // SUB) * SUB
    gain_count = norm_gain.shape[0]
    shift_count = shift_rows.shape[0]
    staged = lax.axis_size(both) == 32 and group == 4 and weights_in.shape[0] == 240 and weights_out.shape[0] == 168

    def enter(x):
        x = lax.all_to_all(x, "seq", split_axis=0, concat_axis=1, tiled=True)
        return jnp.pad(x, ((0, 0), (0, 0), (0, rows - patches), (0, 0)))

    def leave(x):
        x = x[:, :, :patches]
        return lax.all_to_all(x, "seq", split_axis=1, concat_axis=0, tiled=True)

    packed = jnp.concatenate([norm_gain, shift_rows, dense_shift[None, :]], axis=0)
    feed = (Staged if staged else Whole)(both, weights_in, weights_out, packed, width)
    clip = enter(clips_in)
    if staged:
        feed.begin()
    live = lax.dynamic_slice(clip_live, (lax.axis_index("seq") * own,), (own,)).astype(BF16)

    def target(after):
        gradient = cotangent * 1
        if staged:
            gradient = tie(gradient, after)[0]
        return enter(gradient) * live[:, None, None, None]

    output, grad_clip, summed_in, summed_out, owned = block(clip, target, leave, feed, gain_count, patches)
    return (
        output,
        grad_clip,
        summed_in,
        summed_out,
        owned[:gain_count],
        owned[gain_count : gain_count + shift_count],
        owned[-1],
    )


def solution(mesh):
    clip = P("dp", "seq", None, None)
    row = P(("dp", "seq"), None)
    col = P(None, ("dp", "seq"))
    flat = P(("dp", "seq"))
    return jax.shard_map(
        shards,
        mesh=mesh,
        in_specs=(clip, clip, P("dp"), row, row, col, col, flat),
        out_specs=(clip, clip, row, row, col, col, flat),
        check_vma=False,
    )
```

```python
from functools import partial

import jax
import jax.numpy as jnp
from jax import lax
from jax.experimental import pallas as pl
from jax.experimental.pallas import tpu as pltpu
from jax.sharding import PartitionSpec as P

HEADS = 12
HEAD_DIM = 64
EPSILON = 1e-06
PAIRS = HEADS // 2
LANES = 2 * HEAD_DIM
SUB = 16
NEG = -1e30
COPY_VMEM = 60 << 20
F32 = jnp.float32
BF16 = jnp.bfloat16


def nt(left, right):
    return lax.dot_general(left, right, (((1,), (1,)), ((), ())), preferred_element_type=F32)


def nn(left, right):
    return lax.dot_general(left, right, (((1,), (0,)), ((), ())), preferred_element_type=F32)


def tn(left, right):
    return lax.dot_general(left, right, (((0,), (0,)), ((), ())), preferred_element_type=F32)


def split_heads(pair):
    first = lax.broadcasted_iota(jnp.int32, pair.shape, 1) < HEAD_DIM
    zero = jnp.zeros_like(pair)
    return jnp.concatenate([jnp.where(first, pair, zero), jnp.where(first, zero, pair)], axis=0)


def join_heads(stacked):
    rows = stacked.shape[0] // 2
    first = lax.broadcasted_iota(jnp.int32, (rows, LANES), 1) < HEAD_DIM
    return jnp.where(first, stacked[:rows], stacked[rows:])


def pair_forward(queries, keys, values, keep):
    stacked = split_heads(queries * jnp.asarray(HEAD_DIM**-0.5, BF16))
    scores = jnp.where(keep, nt(stacked, keys), NEG)
    top = jnp.max(scores, axis=1, keepdims=True)
    weights = jnp.exp(scores - top)
    total = jnp.sum(weights, axis=1, keepdims=True)
    probs = (weights * (1.0 / total)).astype(BF16)
    return join_heads(nn(probs, values)).astype(BF16)


def pair_backward(queries, keys, values, grad, keep):
    scaling = HEAD_DIM**-0.5
    stacked = split_heads(queries * jnp.asarray(scaling, BF16))
    grads = split_heads(grad)
    scores = jnp.where(keep, nt(keys, stacked), NEG)
    top = jnp.max(scores, axis=0, keepdims=True)
    weights = jnp.exp(scores - top)
    total = jnp.sum(weights, axis=0, keepdims=True)
    probs = weights * (1.0 / total)
    grad_probs = nt(values, grads)
    mean = jnp.sum(probs * grad_probs, axis=0, keepdims=True)
    grad_scores = (probs * (grad_probs - mean)).astype(BF16)
    grad_values = nn(probs.astype(BF16), grads)
    grad_keys = nn(grad_scores, stacked)
    grad_queries = join_heads(tn(grad_scores, keys)) * scaling
    return (grad_queries.astype(BF16), grad_keys.astype(BF16), grad_values.astype(BF16))


def columns(kind, pair):
    start = (kind * PAIRS + pair) * LANES
    return slice(start, start + LANES)


def find(refs, kind, pair):
    cols = columns(kind, pair)
    for ref in refs:
        size = ref.shape[-1]
        if cols.start < size:
            return (ref, cols)
        cols = slice(cols.start - size, cols.stop - size)


def load(refs, kind, pair):
    ref, cols = find(refs, kind, pair)
    return ref[..., cols].reshape(-1, LANES)


def store(refs, kind, pair, block):
    ref, cols = find(refs, kind, pair)
    ref[..., cols] = block.reshape(ref.shape[:-1] + (LANES,))


def keep_mask(shape, key_axis, group, patches):
    key = lax.broadcasted_iota(jnp.int32, shape, key_axis)
    if group is None:
        return key < patches
    query = lax.broadcasted_iota(jnp.int32, shape, 1 - key_axis)
    return (key % group) == (query % group)


def forward_kernel(group, patches, count, *refs):
    project, mixed = (refs[:count], refs[count:])
    rows = project[0].size // project[0].shape[-1]
    keep = keep_mask((2 * rows, rows), 1, group, patches)
    for pair in range(PAIRS):
        block = pair_forward(*[load(project, kind, pair) for kind in range(3)], keep)
        store(mixed, 0, pair, block)


def backward_kernel(group, patches, count, *refs):
    project, grad, outs = (refs[:count], refs[count : count + 1], refs[count + 1 :])
    rows = project[0].size // project[0].shape[-1]
    keep = keep_mask((rows, 2 * rows), 0, group, patches)
    for pair in range(PAIRS):
        results = pair_backward(*[load(project, kind, pair) for kind in range(3)], load(grad, 0, pair), keep)
        for kind, result in enumerate(results):
            store(outs, kind, pair, result)


def attention_call(kernel, count, arrays, out_cols, temporal, patches):
    clips, frames, rows, _ = arrays[0].shape
    if temporal:
        group, steps, shape = SUB, rows // SUB, (1, frames, SUB)
        index = lambda c, i: (c, 0, i, 0)
    else:
        group, steps, shape = None, frames, (1, 1, rows)
        index = lambda c, i: (c, i, 0, 0)
    tokens = clips * frames * rows
    backward = kernel is backward_kernel
    return pl.pallas_call(
        partial(kernel, group, patches, count),
        grid=(clips, steps),
        in_specs=[pl.BlockSpec(shape + (a.shape[-1],), index) for a in arrays],
        out_specs=[pl.BlockSpec(shape + (cols,), index) for cols in out_cols],
        out_shape=[jax.ShapeDtypeStruct((clips, frames, rows, cols), BF16) for cols in out_cols],
        compiler_params=pltpu.CompilerParams(dimension_semantics=("arbitrary", "arbitrary")),
        cost_estimate=pl.CostEstimate(
            flops=tokens * (14_000_000 if backward else 9_000_000), bytes_accessed=0, transcendentals=0
        ),
    )(*arrays)


def eights(rows):
    return rows.reshape(rows.shape[:-2] + (-1, 8, rows.shape[-1]))


def place_kernel(outs_plan, blocks, groups, dest_ref, *refs):
    pieces, refs = (refs[: groups * blocks], refs[groups * blocks :])
    outs, refs = (refs[: len(outs_plan)], refs[len(outs_plan) :])
    held, in_sem, out_sem = (refs[:-2], refs[-2], refs[-1])
    moves, slot = ([], 0)
    for target, entries in enumerate(outs_plan):
        for entry, (group, row, rows) in enumerate(entries):
            for block in range(blocks):
                buffer = held[target].at[entry, block]
                source = pieces[group * blocks + block].at[pl.ds(row // 8, rows // 8)]
                fetch = pltpu.make_async_copy(source, buffer, in_sem.at[slot])
                fetch.start()
                write = pltpu.make_async_copy(buffer, outs[target].at[entry, dest_ref[block]], out_sem.at[slot])
                moves.append((fetch, write))
                slot += 1
    for fetch, write in moves:
        fetch.wait()
        write.start()
    for _, write in moves:
        write.wait()


def place(groups, outs_plan, dest):
    blocks = len(groups[0])
    width = groups[0][0].shape[1]
    shapes = [(len(entries), blocks, entries[0][2] // 8, 8, width) for entries in outs_plan]
    slots = sum(len(entries) for entries in outs_plan) * blocks
    size = sum(16 * s[0] * s[1] * s[2] * s[4] for s in shapes)
    flat = [eights(piece) for group in groups for piece in group]
    anywhere = pl.BlockSpec(memory_space=pl.ANY)
    outs = pl.pallas_call(
        partial(place_kernel, tuple(tuple(e) for e in outs_plan), blocks, len(groups)),
        in_specs=[pl.BlockSpec(memory_space=pltpu.SMEM)] + [anywhere] * len(flat),
        out_specs=[anywhere] * len(shapes),
        out_shape=[jax.ShapeDtypeStruct(s, BF16) for s in shapes],
        scratch_shapes=[pltpu.VMEM(s, BF16) for s in shapes]
        + [pltpu.SemaphoreType.DMA((slots,)), pltpu.SemaphoreType.DMA((slots,))],
        compiler_params=pltpu.CompilerParams(vmem_limit_bytes=COPY_VMEM),
        cost_estimate=pl.CostEstimate(flops=0, bytes_accessed=4 * size, transcendentals=0),
    )(dest, *flat)
    return [out.reshape(out.shape[:2] + (-1, width)) for out in outs]


def split_kernel(spans, plane_rows, squares, core_ref, *refs):
    parts, refs = (refs[: len(spans)], refs[len(spans) :])
    keep, send = refs[:2]
    held, in_sem, out_sem = (refs[2:-2], refs[-2], refs[-1])
    core = core_ref[0]
    incoming, count, part, done = ({}, 0, 0, 0)
    for plane, rows in enumerate(plane_rows):
        for slot in range(2 * squares):
            offset, incoming[plane, slot] = (0, [])
            while offset < rows:
                first, length = spans[part]
                size = min(length - done, rows - offset)
                copy = pltpu.make_async_copy(
                    parts[part].at[pl.ds((first + done) // 8, size // 8)],
                    held[plane].at[slot, pl.ds(offset // 8, size // 8)],
                    in_sem.at[count],
                )
                copy.start()
                incoming[plane, slot].append(copy)
                count, offset, done = (count + 1, offset + size, done + size)
                if done == length:
                    part, done = (part + 1, 0)
    outgoing, row = ([], 0)
    for plane, rows in enumerate(plane_rows):
        for square in range(squares):
            for copy in incoming[plane, 2 * square] + incoming[plane, 2 * square + 1]:
                copy.wait()
            for target, side in ((send, 1 - core), (keep, core)):
                copy = pltpu.make_async_copy(
                    held[plane].at[2 * square + side], target.at[square, pl.ds(row // 8, rows // 8)], out_sem.at[len(outgoing)]
                )
                copy.start()
                outgoing.append(copy)
        row += rows
    for copy in outgoing:
        copy.wait()


def split_cores(parts, plane_rows, squares, core):
    spans = tuple((first, length) for _, first, length in parts)
    arrays = [eights(array) for array, _, _ in parts]
    width = arrays[0].shape[-1]
    slots = len(plane_rows) * squares * 2
    size = 2 * squares * sum(plane_rows) * width * 2
    anywhere = pl.BlockSpec(memory_space=pl.ANY)
    half = jax.ShapeDtypeStruct((squares, sum(plane_rows) // 8, 8, width), BF16)
    outs = pl.pallas_call(
        partial(split_kernel, spans, tuple(plane_rows), squares),
        in_specs=[pl.BlockSpec(memory_space=pltpu.SMEM)] + [anywhere] * len(arrays),
        out_specs=[anywhere, anywhere],
        out_shape=[half, half],
        scratch_shapes=[pltpu.VMEM((2 * squares, rows // 8, 8, width), BF16) for rows in plane_rows]
        + [pltpu.SemaphoreType.DMA((slots + len(parts),)), pltpu.SemaphoreType.DMA((slots,))],
        compiler_params=pltpu.CompilerParams(vmem_limit_bytes=COPY_VMEM),
        cost_estimate=pl.CostEstimate(flops=0, bytes_accessed=4 * size, transcendentals=0),
    )(core, *arrays)
    return [out.reshape(squares, -1, width) for out in outs]


def pack_kernel(devices, *refs):
    parts, out_ref, held = (refs[:-2], refs[-2], refs[-1])
    held[...] = jnp.zeros_like(held)
    out_ref[...] = jnp.zeros_like(out_ref)
    row = 0
    for part in parts:
        held[row : row + part.shape[0], :] = part[...]
        row += part.shape[0]
    share = held.shape[1] // devices
    for device in range(devices):
        out_ref[device, :, :share] = held[:, device * share : (device + 1) * share]


def pack(parts, devices):
    rows = -(-sum(part.shape[0] for part in parts) // 8) * 8
    width = parts[0].shape[1]
    return pl.pallas_call(
        partial(pack_kernel, devices),
        out_shape=jax.ShapeDtypeStruct((devices, rows, LANES), F32),
        scratch_shapes=[pltpu.VMEM((rows, width), F32)],
    )(*parts)


def tie(values, others):
    return lax.optimization_barrier((values, others))


class Whole:
    def __init__(self, axes, weights_in, weights_out, packed, width):
        self.axes, self.width = (axes, width)
        full_in = lax.all_gather(weights_in, axes, axis=0, tiled=True)
        full_out = lax.all_gather(weights_out, axes, axis=0, tiled=True)
        devices = lax.axis_size(axes)
        slot = lax.dynamic_update_slice(
            jnp.zeros((devices,) + packed.shape, F32), packed.astype(F32)[None], (lax.axis_index(axes), 0, 0)
        )
        self.small = lax.psum(slot, axes).transpose(1, 0, 2).reshape(packed.shape[0], width).astype(BF16)
        self.in_a, self.in_b = (full_in[: 5 * width // 2], full_in[5 * width // 2 : 3 * width])
        self.in_t, self.in_qk = (full_in[: 3 * width], full_in[3 * width : 5 * width])
        self.in_v, self.in_m = (full_in[5 * width : 6 * width], full_in[6 * width :])
        self.out_t, self.out_f = (full_out[:width], full_out[width : 2 * width])
        self.out_s, self.out_m = (full_out[2 * width : 3 * width], full_out[3 * width :])
        self.grads = {}

    def tick(self, name, *values):
        return values[0] if len(values) == 1 else values

    def total(self, parts):
        g, small = (self.grads, jnp.concatenate(parts, axis=0))
        d_in = jnp.concatenate([g["in_t"], g["in_qk"], g["in_v"], g["in_m"]], axis=0)
        d_out = jnp.concatenate([g["out_t"], g["out_f"], g["out_s"], g["out_m"]], axis=0)
        summed_in = lax.psum_scatter(d_in, self.axes, scatter_dimension=0, tiled=True).astype(F32)
        summed_out = lax.psum_scatter(d_out, self.axes, scatter_dimension=0, tiled=True).astype(F32)
        share = self.width // lax.axis_size(self.axes)
        at = (0, lax.axis_index(self.axes) * share)
        return (summed_in, summed_out, lax.dynamic_slice(lax.psum(small, self.axes), at, (small.shape[0], share)))


class Staged:
    def __init__(self, axes, weights_in, weights_out, packed, width):
        self.axes, self.width = (axes, width)
        me = lax.axis_index(axes)
        self.plane, self.spot, self.square, self.core = (me // 8, me % 8, me % 8 // 2, me % 2)
        self.spots = jnp.bitwise_xor(jnp.arange(8, dtype=jnp.int32), self.spot)
        self.planes = (self.plane + 4 - jnp.arange(4, dtype=jnp.int32)) % 4
        self.core_ref = self.core.astype(jnp.int32).reshape(1)
        self.rows_in, self.rows_out = (weights_in.shape[0], weights_out.shape[0])
        self.weights_out, self.count = (weights_out, packed.shape[0])
        self.grads = {}
        flat = packed.reshape(1, -1)
        tail = jnp.pad(flat, ((0, 7), (0, width - flat.shape[1])))
        pieces = self.shifted(jnp.concatenate([weights_in, tail], axis=0))
        self.column_in, self.column_small = self.columns(pieces, (self.rows_in, 8))

    def flip(self, x, bits):
        return lax.ppermute(x, self.axes, [(d, d ^ bits) for d in range(32)])

    def shift(self, x, step):
        return lax.ppermute(x, self.axes, [(d, (d + 8 * step) % 32) for d in range(32)])

    def shifted(self, shard):
        return [shard] + [self.shift(shard, step) for step in (1, 2, 3)]

    def columns(self, pieces, sizes):
        plan, row = ([], 0)
        for size in sizes:
            plan.append([(0, row, size)])
            row += size
        return [out[0] for out in place([pieces], plan, self.planes)]

    def planes_exchange(self, blocks):
        groups = [[spot + 8 * plane for plane in range(4)] for spot in range(8)]
        return lax.all_to_all(blocks, self.axes, split_axis=0, concat_axis=0, axis_index_groups=groups)

    def over(self, piece):
        return [piece] + [self.flip(piece, bits) for bits in (2, 4, 6)]

    def cores(self, pieces):
        both = []
        for piece in pieces:
            both += [piece, self.flip(piece, 1)]
        return both

    def lay(self, groups, entries):
        out = place(groups, [entries], self.spots)[0]
        return out.reshape(-1, self.width)

    def begin(self, clip):
        rows_in, rows_out, width = (self.rows_in, self.rows_out, self.width)
        smalls = self.column_small.reshape(-1, width)
        first = jnp.concatenate([self.column_in[0], smalls], axis=0)
        self.p1, self.p2, self.p3 = (self.column_in[k] for k in (1, 2, 3))
        p0 = self.over(first)
        first, weights_out = tie(first, self.weights_out)
        column = self.planes_exchange(jnp.broadcast_to(weights_out[None], (4,) + weights_out.shape))
        p0, (clip, column) = tie(p0, (clip, column))
        self.q01, self.q23 = (column[:2].reshape(-1, width), column[2:].reshape(-1, width))
        self.p0 = self.cores(p0)
        low, small = place([self.p0], [[(0, 0, rows_in)], [(0, rows_in, 32)]], self.spots)
        low, self.p1 = tie(low, self.p1)
        self.p1 = self.over(self.p1)
        self.in_a = low.reshape(-1, width)
        share = width // 32
        small = small.reshape(8, 4, 8, width)[:, :, 0, : self.count * share].reshape(8, 4, self.count, share)
        self.small = small.transpose(2, 1, 0, 3).reshape(self.count, width)
        return clip

    def tick(self, name, *values):
        single = len(values) == 1
        rows_in, rows_out, width = (self.rows_in, self.rows_out, self.width)
        g = self.grads
        whole = lambda key: (g[key], 0, g[key].shape[0])
        if name == "query_t":
            values, (self.p1, self.q01) = tie(values, (self.p1, self.q01))
            self.q01 = self.over(self.q01)
            self.p1 = self.cores(self.p1)
            low = self.lay([self.p0, self.p1], [(0, 0, rows_in), (1, 0, rows_in)])
            self.in_t, self.in_qk = (low[: 3 * width], low[3 * width :])
            self.in_b = self.in_t[5 * width // 2 :]
        elif name == "mixed_t":
            values, (self.q01, self.p2) = tie(values, (self.q01, self.p2))
            self.p2 = self.over(self.p2)
            self.q01 = self.cores(self.q01)
            early = self.lay([self.q01], [(0, 0, rows_out), (0, rows_out, rows_out)])
            self.out_t, self.out_f, self.out_s = (early[k * width : (k + 1) * width] for k in range(3))
        elif name == "query_s":
            values, (self.p2, self.p3) = tie(values, (self.p2, self.p3))
            self.p3 = self.over(self.p3)
            self.p2 = self.cores(self.p2)
            self.in_v = self.lay([self.p2], [(0, 0, rows_in)])[:width]
        elif name == "mixed_s":
            values, (self.p3, self.q23) = tie(values, (self.p3, self.q23))
            self.q23 = self.over(self.q23)
            self.p3 = self.cores(self.p3)
            high = self.lay([self.p2, self.p3], [(0, 0, rows_in), (1, 0, rows_in)])
            self.in_m = high[width:]
        elif name == "hidden":
            values, self.q23 = tie(values, self.q23)
            self.q23 = self.cores(self.q23)
            entries = [(0, rows_out, rows_out), (1, 0, rows_out), (1, rows_out, rows_out)]
            self.out_m = self.lay([self.q01, self.q23], entries)[3 * width - 8 * rows_out :]
        elif name == "out_m":
            start = 16 * rows_out - 3 * width
            d_out_m = g["out_m"]
            self.kept, send = self.halve([(d_out_m, start, d_out_m.shape[0] - start)], (rows_out, rows_out))
            values, send = tie(values, send)
            self.other = self.flip(send, 1)
        elif name == "grad_pre":
            values, (self.kept, self.other) = tie(values, (self.kept, self.other))
            self.d_q23 = self.across(self.kept, self.other)
        elif name == "in_m":
            start = 24 * rows_in - 6 * width
            d_in_m = g["in_m"]
            self.kept, send = self.halve([(d_in_m, start, d_in_m.shape[0] - start)], (rows_in,))
            values, send = tie(values, send)
            self.other = self.flip(send, 1)
        elif name == "grad_mixed_s":
            values, (self.d_q23, self.kept, self.other) = tie(values, (self.d_q23, self.kept, self.other))
            self.d_q23 = self.gathered(self.d_q23)
            self.d_p3 = self.across(self.kept, self.other)
        elif name == "grad_s":
            values, self.d_p3 = tie(values, self.d_p3)
            self.d_p3 = self.gathered(self.d_p3)
        elif name == "in_v":
            start = 24 * rows_in - 6 * width
            self.kept, send = self.halve([whole("in_v"), (g["in_m"], 0, start)], (rows_in,))
            values, send = tie(values, send)
            self.other = self.flip(send, 1)
        elif name == "in_qk":
            values, (self.kept, self.other) = tie(values, (self.kept, self.other))
            self.d_p2 = self.across(self.kept, self.other)
        elif name == "grad_t":
            values, self.d_p2 = tie(values, self.d_p2)
            self.d_p2 = self.gathered(self.d_p2)
            late = jnp.zeros((8 * rows_in - 2 * width, width), BF16)
            self.kept, send = self.halve([(late, 0, late.shape[0]), whole("in_qk")], (rows_in,))
            values, send = tie(values, send)
            self.other = self.flip(send, 1)
        elif name == "out_t":
            values, (self.kept, self.other) = tie(values, (self.kept, self.other))
            self.d_p1 = self.across(self.kept, self.other)
            start = 16 * rows_out - 3 * width
            self.kept, send = self.halve(
                [whole("out_t"), whole("out_f"), whole("out_s"), (g["out_m"], 0, start)], (rows_out, rows_out)
            )
            values, send = tie(values, send)
            self.other = self.flip(send, 1)
        elif name == "grad_mixed_t":
            values, (self.kept, self.other) = tie(values, (self.kept, self.other))
            self.d_q01 = self.across(self.kept, self.other)
        elif name == "grad_project_t":
            values, self.d_p1 = tie(values, self.d_p1)
            self.d_p1 = self.gathered(self.d_p1)
            planes = [jnp.zeros_like(self.d_p1), self.d_p1, self.d_p2, self.d_p3]
            self.in_pieces = self.planes_exchange(jnp.stack(planes, axis=0))
        elif name == "in_t":
            d_in_t = g["in_t"]
            kept, send = self.halve([whole("in_t")], (rows_in, d_in_t.shape[0] // 8 - rows_in))
            values, send = tie(values, send)
            half = lambda a, x: lax.dynamic_slice_in_dim(a, 2 * x, 2, 0).astype(F32)
            other = self.flip(send, 1)
            x = self.square // 2
            send = (half(kept, 1 - x) + half(other, 1 - x)).astype(BF16)
            own = (half(kept, x) + half(other, x)).astype(BF16)
            values, (own, send, self.d_q01) = tie(values, (own, send, self.d_q01))
            self.last = (own, self.flip(send, 4))
            self.d_q01 = self.gathered(self.d_q01)
            planes = [a[k * rows_out : (k + 1) * rows_out] for a in (self.d_q01, self.d_q23) for k in range(2)]
            self.out_pieces = self.planes_exchange(jnp.stack(planes, axis=0))
        elif name == "dx_t":
            values, (own, other, self.in_pieces) = tie(values, self.last + (self.in_pieces,))
            y = self.square % 2
            line = lambda a, y: lax.dynamic_index_in_dim(a, y, 0, keepdims=False).astype(F32)
            send = (line(own, 1 - y) + line(other, 1 - y)).astype(BF16)
            own = (line(own, y) + line(other, y)).astype(BF16)
            self.last = (own, self.flip(send, 2))
        elif name == "grad_clip":
            small = lax.all_to_all(pack(values[1:], 32), self.axes, split_axis=0, concat_axis=0)
            tied = tie(values[0], self.last + (small, self.out_pieces))
            clip, (own, arrived, self.small_sums, self.out_pieces) = tied
            values = (clip,) + tuple(values[1:])
            self.d_last = self.gathered([own, arrived])
        return values[0] if single else values

    def halve(self, parts, plane_rows):
        return split_cores(parts, plane_rows, 4, self.core_ref)

    def across(self, keep, other):
        result = []
        for bits in (0, 2, 4, 6):
            at = jnp.bitwise_xor(self.square, bits // 2)
            take = lambda a: lax.dynamic_index_in_dim(a, at, 0, keepdims=False).astype(F32)
            summed = (take(keep) + take(other)).astype(BF16)
            result.append(summed if bits == 0 else self.flip(summed, bits))
        return result

    def gathered(self, arrived):
        return self.added(arrived).astype(BF16)

    def towards(self, block, plane):
        pieces = [block]
        for step in (1, 2, 3):
            pairs = [(d, (d + 8 * step) % 32) for d in range(32) if (d // 8 + step) % 4 == plane]
            pieces.append(lax.ppermute(block, self.axes, pairs))
        return pieces

    def added(self, pieces):
        total = pieces[0].astype(F32)
        for piece in pieces[1:]:
            total = total + piece.astype(F32)
        return total

    def total(self, parts):
        rows, last = (self.rows_in, self.d_last)
        extra, first = tie(self.towards(last[rows:], 1), last[:rows])
        first = self.added(self.towards(first, 0))
        extra = self.added(extra).astype(BF16)
        extra = jnp.concatenate([extra, self.flip(extra, 1)], axis=0)
        blocks = [extra]
        for bits in (2, 4, 6):
            blocks.append(lax.ppermute(extra, self.axes, [(8 + bits + core, 8 + core) for core in range(2)]))
        extra = jnp.concatenate(blocks, axis=0).reshape(8, -1, self.width)
        swapped = jnp.stack([extra[4], extra[7], extra[6]], axis=0).reshape(-1, self.width)
        swapped = jnp.pad(swapped, ((0, rows - swapped.shape[0]), (0, 0)))
        extra = jnp.where(self.core == 0, extra.reshape(-1, self.width)[:rows], swapped).astype(F32)
        extra = jnp.where((self.plane == 1) & (self.square == 0), extra, 0.0)
        summed_in = jnp.where(self.plane == 0, first, jnp.sum(self.in_pieces.astype(F32), axis=0) + extra)
        small = jnp.sum(self.small_sums, axis=0)[: self.count, : self.width // 32]
        return (summed_in, jnp.sum(self.out_pieces.astype(F32), axis=0), small)


def norm_parts(values):
    centre = values - jnp.mean(values, axis=-1, keepdims=True)
    spread = jnp.mean(centre * centre, axis=-1, keepdims=True)
    scale = lax.rsqrt(spread + EPSILON)
    return (centre * scale, scale)


def layer_norm(values, gains, shifts):
    return (norm_parts(values)[0] * gains + shifts).astype(BF16)


def norm_backward(values, gains, grad, hook=lambda *sums: sums):
    normed, scale = norm_parts(values)
    scaled = grad * gains
    first = jnp.mean(scaled, axis=-1, keepdims=True)
    second = jnp.mean(scaled * normed, axis=-1, keepdims=True)
    sums = (first, second, jnp.sum(grad * normed, axis=0), jnp.sum(grad, axis=0))
    grad, first, second, d_gain, d_shift = hook(grad, *sums)
    inner = (grad * gains - first - normed * second) * scale
    return (inner, d_gain, d_shift)


def gelu_parts(values):
    cdf = 0.5 * (1.0 + lax.erf(values * (0.5**0.5)))
    density = jnp.exp(-0.5 * values * values) * 0.3989422804014327
    return (values * cdf, cdf + values * density)


def column_sum(rows):
    return jnp.sum(rows.astype(F32), axis=0)


def block(clip, target, leave, feed, gain_count, patches):
    shape = clip.shape
    width = shape[-1]
    grid = shape[:3]
    small32 = feed.small.astype(F32)
    gains32, shifts32, dense32 = (small32[:gain_count], small32[gain_count:-1], small32[-1])
    flat = lambda a: a.reshape(-1, a.shape[-1])
    cube = lambda a: a.reshape(grid + (a.shape[-1],))
    grads = feed.grads
    start = clip.reshape(-1, width).astype(F32)
    normed_t = layer_norm(start, gains32[0], shifts32[0])
    project_a = nt(normed_t, feed.in_a).astype(BF16)
    project_a, normed_t = feed.tick("query_t", project_a, normed_t)
    project_b = nt(normed_t, feed.in_b).astype(BF16)
    project_t = [cube(project_a), cube(project_b)]
    mixed_t = attention_call(forward_kernel, 2, project_t, (width,), True, patches)[0]
    mixed_t = flat(feed.tick("mixed_t", mixed_t))
    grad_low = flat(target(mixed_t))
    projected_t = (nn(mixed_t, feed.out_t) + shifts32[3]).astype(BF16)
    branch_t = (nn(projected_t, feed.out_f) + shifts32[4]).astype(BF16)
    after_t = start + branch_t.astype(F32)
    normed_s = layer_norm(after_t, gains32[1], shifts32[1])
    project_qk = nt(normed_s, feed.in_qk).astype(BF16)
    project_qk, normed_s = feed.tick("query_s", project_qk, normed_s)
    project_v = nt(normed_s, feed.in_v).astype(BF16)
    project_s = [cube(project_qk), cube(project_v)]
    mixed_s = attention_call(forward_kernel, 2, project_s, (width,), False, patches)[0]
    mixed_s = flat(feed.tick("mixed_s", mixed_s))
    after_s = after_t + (nn(mixed_s, feed.out_s) + shifts32[5])
    normed_m = layer_norm(after_s, gains32[2], shifts32[2])
    hidden_pre = nt(normed_m, feed.in_m) + shifts32[6:].reshape(-1)
    hidden32, slope32 = gelu_parts(hidden_pre)
    hidden, slope = feed.tick("hidden", hidden32.astype(BF16), slope32.astype(BF16))
    output = (after_s + (nn(hidden, feed.out_m) + dense32)).astype(BF16)
    output = leave(output.reshape(shape))

    grad_out = grad_low.astype(F32)
    grads["out_m"] = tn(hidden, grad_low).astype(BF16)
    grad_low = feed.tick("out_m", grad_low)
    s_dense = column_sum(grad_low)
    grad_pre = (nt(grad_low, feed.out_m) * slope.astype(F32)).astype(BF16)
    grad_pre = feed.tick("grad_pre", grad_pre)
    grads["in_m"] = tn(grad_pre, normed_m).astype(BF16)
    grad_pre = feed.tick("in_m", grad_pre)
    s_hidden = column_sum(grad_pre).reshape(-1, width)
    part, g_m, b_m = norm_backward(after_s, gains32[2], nn(grad_pre, feed.in_m))
    grad_s = grad_out + part
    grad_branch_s = grad_s.astype(BF16)
    grads["out_s"] = tn(mixed_s, grad_branch_s).astype(BF16)
    s_space = column_sum(grad_branch_s)
    grad_mixed_s = nt(grad_branch_s, feed.out_s).astype(BF16)
    grad_mixed_s, output = feed.tick("grad_mixed_s", grad_mixed_s, output)
    grad_qk, grad_v = attention_call(
        backward_kernel, 2, project_s + [cube(grad_mixed_s)], (2 * width, width), False, patches
    )
    grad_qk, grad_v = feed.tick("grad_s", flat(grad_qk), flat(grad_v))
    grads["in_v"] = tn(grad_v, normed_s).astype(BF16)
    grad_qk, grad_v = feed.tick("in_v", grad_qk, grad_v)
    d_in_qk = tn(grad_qk, normed_s).astype(BF16)
    grads["in_qk"], grad_qk, grad_v = feed.tick("in_qk", d_in_qk, grad_qk, grad_v)
    part, g_s, b_s = norm_backward(after_t, gains32[1], nn(grad_qk, feed.in_qk) + nn(grad_v, feed.in_v))
    grad_t = grad_s + part
    grad_branch_t = feed.tick("grad_t", grad_t.astype(BF16))
    grads["out_f"] = tn(projected_t, grad_branch_t).astype(BF16)
    s_fc = column_sum(grad_branch_t)
    grad_projected = nt(grad_branch_t, feed.out_f).astype(BF16)
    grads["out_t"] = tn(mixed_t, grad_projected).astype(BF16)
    grad_projected = feed.tick("out_t", grad_projected)
    s_time = column_sum(grad_projected)
    grad_mixed_t = feed.tick("grad_mixed_t", nt(grad_projected, feed.out_t).astype(BF16))
    grad_project_t = attention_call(
        backward_kernel, 2, project_t + [cube(grad_mixed_t)], (3 * width,), True, patches
    )[0]
    grad_project_t = feed.tick("grad_project_t", flat(grad_project_t))
    grads["in_t"] = tn(grad_project_t, normed_t).astype(BF16)
    grad_project_t = feed.tick("in_t", grad_project_t)
    hook = lambda *sums: feed.tick("dx_t", *sums)
    part, g_t, b_t = norm_backward(start, gains32[0], nn(grad_project_t, feed.in_t), hook)
    grad_clip = (grad_t + part.astype(BF16).astype(F32)).astype(BF16)
    parts = [g_t, g_s, g_m, b_t, b_s, b_m, s_time, s_fc, s_space, s_hidden, s_dense]
    grad_clip, *parts = feed.tick("grad_clip", grad_clip, *[part.reshape(-1, width) for part in parts])
    return (output, leave(grad_clip.reshape(shape)).astype(F32)) + feed.total(parts)


def shards(clips_in, cotangent, clip_live, weights_in, weights_out, norm_gain, shift_rows, dense_shift):
    both = ("dp", "seq")
    group = lax.axis_size("seq")
    count, _, patches, width = clips_in.shape
    own = count // group
    rows = -(-patches // SUB) * SUB
    gain_count = norm_gain.shape[0]
    shift_count = shift_rows.shape[0]
    staged = lax.axis_size(both) == 32 and group == 4 and weights_in.shape[0] == 240 and weights_out.shape[0] == 168

    def enter(x):
        x = lax.all_to_all(x, "seq", split_axis=0, concat_axis=1, tiled=True)
        return jnp.pad(x, ((0, 0), (0, 0), (0, rows - patches), (0, 0)))

    def leave(x):
        x = x[:, :, :patches]
        return lax.all_to_all(x, "seq", split_axis=1, concat_axis=0, tiled=True)

    packed = jnp.concatenate([norm_gain, shift_rows, dense_shift[None, :]], axis=0)
    feed = (Staged if staged else Whole)(both, weights_in, weights_out, packed, width)
    clip = enter(clips_in)
    if staged:
        clip = feed.begin(clip)
    live = lax.dynamic_slice(clip_live, (lax.axis_index("seq") * own,), (own,)).astype(BF16)

    def target(after):
        gradient = cotangent * 1
        if staged:
            gradient = tie(gradient, after)[0]
        return enter(gradient) * live[:, None, None, None]

    output, grad_clip, summed_in, summed_out, owned = block(clip, target, leave, feed, gain_count, patches)
    return (
        output,
        grad_clip,
        summed_in,
        summed_out,
        owned[:gain_count],
        owned[gain_count : gain_count + shift_count],
        owned[-1],
    )


def solution(mesh):
    clip = P("dp", "seq", None, None)
    row = P(("dp", "seq"), None)
    col = P(None, ("dp", "seq"))
    flat = P(("dp", "seq"))
    return jax.shard_map(
        shards,
        mesh=mesh,
        in_specs=(clip, clip, P("dp"), row, row, col, col, flat),
        out_specs=(clip, clip, row, row, col, col, flat),
        check_vma=False,
    )
```

```python
from functools import partial

import jax
import jax.numpy as jnp
from jax import lax
from jax.experimental import pallas as pl
from jax.experimental.pallas import tpu as pltpu
from jax.sharding import PartitionSpec as P

HEADS = 12
HEAD_DIM = 64
EPSILON = 1e-06
PAIRS = HEADS // 2
LANES = 2 * HEAD_DIM
SUB = 16
NEG = -1e30
COPY_VMEM = 60 << 20
F32 = jnp.float32
BF16 = jnp.bfloat16


def nt(left, right):
    return lax.dot_general(left, right, (((1,), (1,)), ((), ())), preferred_element_type=F32)


def nn(left, right):
    return lax.dot_general(left, right, (((1,), (0,)), ((), ())), preferred_element_type=F32)


def tn(left, right):
    return lax.dot_general(left, right, (((0,), (0,)), ((), ())), preferred_element_type=F32)


def split_heads(pair):
    first = lax.broadcasted_iota(jnp.int32, pair.shape, 1) < HEAD_DIM
    zero = jnp.zeros_like(pair)
    return jnp.concatenate([jnp.where(first, pair, zero), jnp.where(first, zero, pair)], axis=0)


def join_heads(stacked):
    rows = stacked.shape[0] // 2
    first = lax.broadcasted_iota(jnp.int32, (rows, LANES), 1) < HEAD_DIM
    return jnp.where(first, stacked[:rows], stacked[rows:])


def pair_forward(queries, keys, values, keep):
    stacked = split_heads(queries * jnp.asarray(HEAD_DIM**-0.5, BF16))
    scores = jnp.where(keep, nt(stacked, keys), NEG)
    top = jnp.max(scores, axis=1, keepdims=True)
    weights = jnp.exp(scores - top)
    total = jnp.sum(weights, axis=1, keepdims=True)
    probs = (weights * (1.0 / total)).astype(BF16)
    return join_heads(nn(probs, values)).astype(BF16)


def pair_backward(queries, keys, values, grad, keep):
    scaling = HEAD_DIM**-0.5
    stacked = split_heads(queries * jnp.asarray(scaling, BF16))
    grads = split_heads(grad)
    scores = jnp.where(keep, nt(keys, stacked), NEG)
    top = jnp.max(scores, axis=0, keepdims=True)
    weights = jnp.exp(scores - top)
    total = jnp.sum(weights, axis=0, keepdims=True)
    probs = weights * (1.0 / total)
    grad_probs = nt(values, grads)
    mean = jnp.sum(probs * grad_probs, axis=0, keepdims=True)
    grad_scores = (probs * (grad_probs - mean)).astype(BF16)
    grad_values = nn(probs.astype(BF16), grads)
    grad_keys = nn(grad_scores, stacked)
    grad_queries = join_heads(tn(grad_scores, keys)) * scaling
    return (grad_queries.astype(BF16), grad_keys.astype(BF16), grad_values.astype(BF16))


def columns(kind, pair):
    start = (kind * PAIRS + pair) * LANES
    return slice(start, start + LANES)


def find(refs, kind, pair):
    cols = columns(kind, pair)
    for ref in refs:
        size = ref.shape[-1]
        if cols.start < size:
            return (ref, cols)
        cols = slice(cols.start - size, cols.stop - size)


def load(refs, kind, pair):
    ref, cols = find(refs, kind, pair)
    return ref[..., cols].reshape(-1, LANES)


def store(refs, kind, pair, block):
    ref, cols = find(refs, kind, pair)
    ref[..., cols] = block.reshape(ref.shape[:-1] + (LANES,))


def keep_mask(shape, key_axis, group, patches):
    key = lax.broadcasted_iota(jnp.int32, shape, key_axis)
    if group is None:
        return key < patches
    query = lax.broadcasted_iota(jnp.int32, shape, 1 - key_axis)
    return (key % group) == (query % group)


def forward_kernel(group, patches, count, *refs):
    project, mixed = (refs[:count], refs[count:])
    rows = project[0].size // project[0].shape[-1]
    keep = keep_mask((2 * rows, rows), 1, group, patches)
    for pair in range(PAIRS):
        block = pair_forward(*[load(project, kind, pair) for kind in range(3)], keep)
        store(mixed, 0, pair, block)


def backward_kernel(group, patches, count, *refs):
    project, grad, outs = (refs[:count], refs[count : count + 1], refs[count + 1 :])
    rows = project[0].size // project[0].shape[-1]
    keep = keep_mask((rows, 2 * rows), 0, group, patches)
    for pair in range(PAIRS):
        results = pair_backward(*[load(project, kind, pair) for kind in range(3)], load(grad, 0, pair), keep)
        for kind, result in enumerate(results):
            store(outs, kind, pair, result)


def attention_call(kernel, count, arrays, out_cols, temporal, patches):
    clips, frames, rows, _ = arrays[0].shape
    if temporal:
        group, steps, shape = SUB, rows // SUB, (1, frames, SUB)
        index = lambda c, i: (c, 0, i, 0)
    else:
        group, steps, shape = None, frames, (1, 1, rows)
        index = lambda c, i: (c, i, 0, 0)
    tokens = clips * frames * rows
    backward = kernel is backward_kernel
    return pl.pallas_call(
        partial(kernel, group, patches, count),
        grid=(clips, steps),
        in_specs=[pl.BlockSpec(shape + (a.shape[-1],), index) for a in arrays],
        out_specs=[pl.BlockSpec(shape + (cols,), index) for cols in out_cols],
        out_shape=[jax.ShapeDtypeStruct((clips, frames, rows, cols), BF16) for cols in out_cols],
        compiler_params=pltpu.CompilerParams(dimension_semantics=("arbitrary", "arbitrary")),
        cost_estimate=pl.CostEstimate(
            flops=tokens * (14_000_000 if backward else 9_000_000), bytes_accessed=0, transcendentals=0
        ),
    )(*arrays)


def eights(rows):
    return rows.reshape(rows.shape[:-2] + (-1, 8, rows.shape[-1]))


def place_kernel(outs_plan, blocks, groups, dest_ref, *refs):
    pieces, refs = (refs[: groups * blocks], refs[groups * blocks :])
    outs, refs = (refs[: len(outs_plan)], refs[len(outs_plan) :])
    held, in_sem, out_sem = (refs[:-2], refs[-2], refs[-1])
    moves, slot = ([], 0)
    for target, entries in enumerate(outs_plan):
        for entry, (group, row, rows) in enumerate(entries):
            for block in range(blocks):
                buffer = held[target].at[entry, block]
                source = pieces[group * blocks + block].at[pl.ds(row // 8, rows // 8)]
                fetch = pltpu.make_async_copy(source, buffer, in_sem.at[slot])
                fetch.start()
                write = pltpu.make_async_copy(buffer, outs[target].at[entry, dest_ref[block]], out_sem.at[slot])
                moves.append((fetch, write))
                slot += 1
    for fetch, write in moves:
        fetch.wait()
        write.start()
    for _, write in moves:
        write.wait()


def place(groups, outs_plan, dest):
    blocks = len(groups[0])
    width = groups[0][0].shape[1]
    shapes = [(len(entries), blocks, entries[0][2] // 8, 8, width) for entries in outs_plan]
    slots = sum(len(entries) for entries in outs_plan) * blocks
    size = sum(16 * s[0] * s[1] * s[2] * s[4] for s in shapes)
    flat = [eights(piece) for group in groups for piece in group]
    anywhere = pl.BlockSpec(memory_space=pl.ANY)
    outs = pl.pallas_call(
        partial(place_kernel, tuple(tuple(e) for e in outs_plan), blocks, len(groups)),
        in_specs=[pl.BlockSpec(memory_space=pltpu.SMEM)] + [anywhere] * len(flat),
        out_specs=[anywhere] * len(shapes),
        out_shape=[jax.ShapeDtypeStruct(s, BF16) for s in shapes],
        scratch_shapes=[pltpu.VMEM(s, BF16) for s in shapes]
        + [pltpu.SemaphoreType.DMA((slots,)), pltpu.SemaphoreType.DMA((slots,))],
        compiler_params=pltpu.CompilerParams(vmem_limit_bytes=size + (2 << 20)),
        cost_estimate=pl.CostEstimate(flops=0, bytes_accessed=4 * size, transcendentals=0),
    )(dest, *flat)
    return [out.reshape(out.shape[:2] + (-1, width)) for out in outs]


def split_kernel(spans, plane_rows, squares, core_ref, *refs):
    parts, refs = (refs[: len(spans)], refs[len(spans) :])
    keep, send = refs[:2]
    held, in_sem, out_sem = (refs[2:-2], refs[-2], refs[-1])
    core = core_ref[0]
    incoming, count, part, done = ({}, 0, 0, 0)
    for plane, rows in enumerate(plane_rows):
        for slot in range(2 * squares):
            offset, incoming[plane, slot] = (0, [])
            while offset < rows:
                first, length = spans[part]
                size = min(length - done, rows - offset)
                copy = pltpu.make_async_copy(
                    parts[part].at[pl.ds((first + done) // 8, size // 8)],
                    held[plane].at[slot, pl.ds(offset // 8, size // 8)],
                    in_sem.at[count],
                )
                copy.start()
                incoming[plane, slot].append(copy)
                count, offset, done = (count + 1, offset + size, done + size)
                if done == length:
                    part, done = (part + 1, 0)
    outgoing, row = ([], 0)
    for plane, rows in enumerate(plane_rows):
        for square in range(squares):
            for copy in incoming[plane, 2 * square] + incoming[plane, 2 * square + 1]:
                copy.wait()
            for target, side in ((send, 1 - core), (keep, core)):
                copy = pltpu.make_async_copy(
                    held[plane].at[2 * square + side], target.at[square, pl.ds(row // 8, rows // 8)], out_sem.at[len(outgoing)]
                )
                copy.start()
                outgoing.append(copy)
        row += rows
    for copy in outgoing:
        copy.wait()


def split_cores(parts, plane_rows, squares, core):
    spans = tuple((first, length) for _, first, length in parts)
    arrays = [eights(array) for array, _, _ in parts]
    width = arrays[0].shape[-1]
    slots = len(plane_rows) * squares * 2
    size = 2 * squares * sum(plane_rows) * width * 2
    anywhere = pl.BlockSpec(memory_space=pl.ANY)
    half = jax.ShapeDtypeStruct((squares, sum(plane_rows) // 8, 8, width), BF16)
    outs = pl.pallas_call(
        partial(split_kernel, spans, tuple(plane_rows), squares),
        in_specs=[pl.BlockSpec(memory_space=pltpu.SMEM)] + [anywhere] * len(arrays),
        out_specs=[anywhere, anywhere],
        out_shape=[half, half],
        scratch_shapes=[pltpu.VMEM((2 * squares, rows // 8, 8, width), BF16) for rows in plane_rows]
        + [pltpu.SemaphoreType.DMA((slots + len(parts),)), pltpu.SemaphoreType.DMA((slots,))],
        compiler_params=pltpu.CompilerParams(vmem_limit_bytes=size + (2 << 20)),
        cost_estimate=pl.CostEstimate(flops=0, bytes_accessed=4 * size, transcendentals=0),
    )(core, *arrays)
    return [out.reshape(squares, -1, width) for out in outs]


def join_kernel(chunks, *refs):
    parts, (out, held, in_sem, out_sem) = (refs[:-4], refs[-4:])
    moves = []
    for slot, (part, row) in enumerate(chunks):
        size = held.shape[1]
        fetch = pltpu.make_async_copy(parts[part].at[pl.ds(row, size)], held.at[slot], in_sem.at[slot])
        fetch.start()
        moves.append((fetch, pltpu.make_async_copy(held.at[slot], out.at[pl.ds(slot * size, size)], out_sem.at[slot])))
    for fetch, write in moves:
        fetch.wait()
        write.start()
    for _, write in moves:
        write.wait()


def join(parts, rows):
    width = parts[0].shape[1]
    chunks = [(k, row // 8) for k, part in enumerate(parts) for row in range(0, part.shape[0], rows)]
    count = len(chunks)
    anywhere = pl.BlockSpec(memory_space=pl.ANY)
    out = pl.pallas_call(
        partial(join_kernel, tuple(chunks)),
        in_specs=[anywhere] * len(parts),
        out_specs=anywhere,
        out_shape=jax.ShapeDtypeStruct((count * rows // 8, 8, width), BF16),
        scratch_shapes=[
            pltpu.VMEM((count, rows // 8, 8, width), BF16),
            pltpu.SemaphoreType.DMA((count,)),
            pltpu.SemaphoreType.DMA((count,)),
        ],
        compiler_params=pltpu.CompilerParams(vmem_limit_bytes=COPY_VMEM),
        cost_estimate=pl.CostEstimate(flops=0, bytes_accessed=8 * count * rows * width, transcendentals=0),
    )(*[eights(part) for part in parts])
    return out.reshape(-1, width)


def pack_kernel(devices, *refs):
    parts, out_ref, held = (refs[:-2], refs[-2], refs[-1])
    held[...] = jnp.zeros_like(held)
    out_ref[...] = jnp.zeros_like(out_ref)
    row = 0
    for part in parts:
        held[row : row + part.shape[0], :] = part[...]
        row += part.shape[0]
    share = held.shape[1] // devices
    for device in range(devices):
        out_ref[device, :, :share] = held[:, device * share : (device + 1) * share]


def pack(parts, devices):
    rows = -(-sum(part.shape[0] for part in parts) // 8) * 8
    width = parts[0].shape[1]
    return pl.pallas_call(
        partial(pack_kernel, devices),
        out_shape=jax.ShapeDtypeStruct((devices, rows, LANES), F32),
        scratch_shapes=[pltpu.VMEM((rows, width), F32)],
    )(*parts)


def tie(values, others):
    return lax.optimization_barrier((values, others))


class Whole:
    def __init__(self, axes, weights_in, weights_out, packed, width):
        self.axes, self.width = (axes, width)
        full_in = lax.all_gather(weights_in, axes, axis=0, tiled=True)
        full_out = lax.all_gather(weights_out, axes, axis=0, tiled=True)
        devices = lax.axis_size(axes)
        slot = lax.dynamic_update_slice(
            jnp.zeros((devices,) + packed.shape, F32), packed.astype(F32)[None], (lax.axis_index(axes), 0, 0)
        )
        self.small = lax.psum(slot, axes).transpose(1, 0, 2).reshape(packed.shape[0], width).astype(BF16)
        self.in_a, self.in_b = (full_in[: 5 * width // 2], full_in[5 * width // 2 : 3 * width])
        self.in_t, self.in_qk = (full_in[: 3 * width], full_in[3 * width : 5 * width])
        self.in_v, self.in_m = (full_in[5 * width : 6 * width], full_in[6 * width :])
        self.out_t, self.out_f = (full_out[:width], full_out[width : 2 * width])
        self.out_s, self.out_m = (full_out[2 * width : 3 * width], full_out[3 * width :])
        self.grads = {}

    def tick(self, name, *values):
        return values[0] if len(values) == 1 else values

    def total(self, parts):
        g, small = (self.grads, jnp.concatenate(parts, axis=0))
        d_in = jnp.concatenate([g["in_t"], g["in_qk"], g["in_v"], g["in_m"]], axis=0)
        d_out = jnp.concatenate([g["out_t"], g["out_f"], g["out_s"], g["out_m"]], axis=0)
        summed_in = lax.psum_scatter(d_in, self.axes, scatter_dimension=0, tiled=True).astype(F32)
        summed_out = lax.psum_scatter(d_out, self.axes, scatter_dimension=0, tiled=True).astype(F32)
        share = self.width // lax.axis_size(self.axes)
        at = (0, lax.axis_index(self.axes) * share)
        return (summed_in, summed_out, lax.dynamic_slice(lax.psum(small, self.axes), at, (small.shape[0], share)))


class Staged:
    def __init__(self, axes, weights_in, weights_out, packed, width):
        self.axes, self.width = (axes, width)
        me = lax.axis_index(axes)
        self.plane, self.spot, self.square, self.core = (me // 8, me % 8, me % 8 // 2, me % 2)
        self.spots = jnp.bitwise_xor(jnp.arange(8, dtype=jnp.int32), self.spot)
        self.planes = (self.plane + 4 - jnp.arange(4, dtype=jnp.int32)) % 4
        self.core_ref = self.core.astype(jnp.int32).reshape(1)
        self.rows_in, self.count = (weights_in.shape[0], packed.shape[0])
        full_out = lax.all_gather(weights_out, axes, axis=0, tiled=True)
        self.out_t, self.out_f = (full_out[:width], full_out[width : 2 * width])
        self.out_s, self.out_m = (full_out[2 * width : 3 * width], full_out[3 * width :])
        self.grads = {}
        flat = packed.reshape(1, -1)
        tail = jnp.pad(flat, ((0, 7), (0, width - flat.shape[1])))
        pieces = self.shifted(jnp.concatenate([weights_in, tail], axis=0))
        self.column_in, self.column_small = self.columns(pieces, (self.rows_in, 8))

    def flip(self, x, bits):
        return lax.ppermute(x, self.axes, [(d, d ^ bits) for d in range(32)])

    def shift(self, x, step):
        return lax.ppermute(x, self.axes, [(d, (d + 8 * step) % 32) for d in range(32)])

    def shifted(self, shard):
        return [shard] + [self.shift(shard, step) for step in (1, 2, 3)]

    def columns(self, pieces, sizes):
        plan, row = ([], 0)
        for size in sizes:
            plan.append([(0, row, size)])
            row += size
        return [out[0] for out in place([pieces], plan, self.planes)]

    def planes_exchange(self, blocks):
        groups = [[spot + 8 * plane for plane in range(4)] for spot in range(8)]
        return lax.all_to_all(blocks, self.axes, split_axis=0, concat_axis=0, axis_index_groups=groups)

    def over(self, piece):
        return [piece] + [self.flip(piece, bits) for bits in (2, 4, 6)]

    def cores(self, pieces):
        both = []
        for piece in pieces:
            both += [piece, self.flip(piece, 1)]
        return both

    def lay(self, groups, entries):
        out = place(groups, [entries], self.spots)[0]
        return out.reshape(-1, self.width)

    def begin(self, clip):
        rows_in, width = (self.rows_in, self.width)
        smalls = self.column_small.reshape(-1, width)
        first = jnp.concatenate([self.column_in[0], smalls], axis=0)
        self.p1, self.p2, self.p3 = (self.column_in[k] for k in (1, 2, 3))
        p0 = self.over(first)
        p0, clip = tie(p0, clip)
        self.p0 = self.cores(p0)
        low, small = place([self.p0], [[(0, 0, rows_in)], [(0, rows_in, 32)]], self.spots)
        low, self.p1 = tie(low, self.p1)
        self.p1 = self.over(self.p1)
        self.in_a = low.reshape(-1, width)
        share = width // 32
        small = small.reshape(8, 4, 8, width)[:, :, 0, : self.count * share].reshape(8, 4, self.count, share)
        self.small = small.transpose(2, 1, 0, 3).reshape(self.count, width)
        return clip

    def tick(self, name, *values):
        single = len(values) == 1
        rows_in, width = (self.rows_in, self.width)
        g = self.grads
        whole = lambda key: (g[key], 0, g[key].shape[0])
        if name == "query_t":
            values, (self.p1, self.p2) = tie(values, (self.p1, self.p2))
            self.p2 = self.over(self.p2)
            self.p1 = self.cores(self.p1)
            low = self.lay([self.p0, self.p1], [(0, 0, rows_in), (1, 0, rows_in)])
            self.in_t, self.in_qk = (low[: 3 * width], low[3 * width :])
            self.in_b = self.in_t[5 * width // 2 :]
        elif name == "mixed_t":
            values, (self.p2, self.p3) = tie(values, (self.p2, self.p3))
            self.p3 = self.over(self.p3)
        elif name == "query_s":
            self.p2 = self.cores(self.p2)
            self.in_v = self.lay([self.p2], [(0, 0, rows_in)])[:width]
        elif name == "mixed_s":
            values, self.p3 = tie(values, self.p3)
            self.p3 = self.cores(self.p3)
            high = self.lay([self.p2, self.p3], [(0, 0, rows_in), (1, 0, rows_in)])
            self.in_m = high[width:]
        elif name == "hidden":
            values = lax.optimization_barrier(values)
        elif name == "in_m":
            start = 24 * rows_in - 6 * width
            d_in_m = g["in_m"]
            self.kept, send = self.halve([(d_in_m, start, d_in_m.shape[0] - start)], (rows_in,))
            values, send = tie(values, send)
            self.other = self.flip(send, 1)
        elif name == "grad_mixed_s":
            values, (self.kept, self.other) = tie(values, (self.kept, self.other))
            self.d_p3 = self.across(self.kept, self.other)
        elif name == "grad_s":
            values, self.d_p3 = tie(values, self.d_p3)
            self.d_p3 = self.gathered(self.d_p3)
        elif name == "in_v":
            start = 24 * rows_in - 6 * width
            self.kept, send = self.halve([whole("in_v"), (g["in_m"], 0, start)], (rows_in,))
            values, send = tie(values, send)
            self.other = self.flip(send, 1)
        elif name == "in_qk":
            values, (self.kept, self.other) = tie(values, (self.kept, self.other))
            self.d_p2 = self.across(self.kept, self.other)
        elif name == "grad_t":
            values, self.d_p2 = tie(values, self.d_p2)
            self.d_p2 = self.gathered(self.d_p2)
            late = jnp.zeros((8 * rows_in - 2 * width, width), BF16)
            self.kept, send = self.halve([(late, 0, late.shape[0]), whole("in_qk")], (rows_in,))
            values, send = tie(values, send)
            self.other = self.flip(send, 1)
        elif name == "out_t":
            values, (self.kept, self.other) = tie(values, (self.kept, self.other))
            self.d_p1 = self.across(self.kept, self.other)
            d_out = join([g["out_t"], g["out_f"], g["out_s"], g["out_m"]], width // 2)
            values, d_out = tie(values, d_out)
            self.summed_out = lax.psum_scatter(d_out, self.axes, scatter_dimension=0, tiled=True).astype(F32)
        elif name == "grad_project_t":
            values, self.d_p1 = tie(values, self.d_p1)
            self.d_p1 = self.gathered(self.d_p1)
            planes = [jnp.zeros_like(self.d_p1), self.d_p1, self.d_p2, self.d_p3]
            self.in_pieces = self.planes_exchange(jnp.stack(planes, axis=0))
        elif name == "in_t":
            d_in_t = g["in_t"]
            kept, send = self.halve([whole("in_t")], (rows_in, d_in_t.shape[0] // 8 - rows_in))
            values, send = tie(values, send)
            half = lambda a, x: lax.dynamic_slice_in_dim(a, 2 * x, 2, 0).astype(F32)
            other = self.flip(send, 1)
            x = self.square // 2
            send = (half(kept, 1 - x) + half(other, 1 - x)).astype(BF16)
            own = (half(kept, x) + half(other, x)).astype(BF16)
            values, (own, send) = tie(values, (own, send))
            self.last = (own, self.flip(send, 4))
        elif name == "dx_t":
            values, (own, other, self.in_pieces) = tie(values, self.last + (self.in_pieces,))
            y = self.square % 2
            line = lambda a, y: lax.dynamic_index_in_dim(a, y, 0, keepdims=False).astype(F32)
            send = (line(own, 1 - y) + line(other, 1 - y)).astype(BF16)
            own = (line(own, y) + line(other, y)).astype(BF16)
            self.last = (own, self.flip(send, 2))
        elif name == "grad_clip":
            small = lax.all_to_all(pack(values[1:], 32), self.axes, split_axis=0, concat_axis=0)
            clip, (own, arrived, self.small_sums) = tie(values[0], self.last + (small,))
            values = (clip,) + tuple(values[1:])
            self.d_last = self.gathered([own, arrived])
        return values[0] if single else values

    def halve(self, parts, plane_rows):
        return split_cores(parts, plane_rows, 4, self.core_ref)

    def across(self, keep, other):
        result = []
        for bits in (0, 2, 4, 6):
            at = jnp.bitwise_xor(self.square, bits // 2)
            take = lambda a: lax.dynamic_index_in_dim(a, at, 0, keepdims=False).astype(F32)
            summed = (take(keep) + take(other)).astype(BF16)
            result.append(summed if bits == 0 else self.flip(summed, bits))
        return result

    def gathered(self, arrived):
        return self.added(arrived).astype(BF16)

    def towards(self, block, plane):
        pieces = [block]
        for step in (1, 2, 3):
            pairs = [(d, (d + 8 * step) % 32) for d in range(32) if (d // 8 + step) % 4 == plane]
            pieces.append(lax.ppermute(block, self.axes, pairs))
        return pieces

    def added(self, pieces):
        total = pieces[0].astype(F32)
        for piece in pieces[1:]:
            total = total + piece.astype(F32)
        return total

    def total(self, parts):
        rows, last = (self.rows_in, self.d_last)
        extra, first = tie(self.towards(last[rows:], 1), last[:rows])
        first = self.added(self.towards(first, 0))
        extra = self.added(extra).astype(BF16)
        extra = jnp.concatenate([extra, self.flip(extra, 1)], axis=0)
        blocks = [extra]
        for bits in (2, 4, 6):
            blocks.append(lax.ppermute(extra, self.axes, [(8 + bits + core, 8 + core) for core in range(2)]))
        extra = jnp.concatenate(blocks, axis=0).reshape(8, -1, self.width)
        swapped = jnp.stack([extra[4], extra[7], extra[6]], axis=0).reshape(-1, self.width)
        swapped = jnp.pad(swapped, ((0, rows - swapped.shape[0]), (0, 0)))
        extra = jnp.where(self.core == 0, extra.reshape(-1, self.width)[:rows], swapped).astype(F32)
        extra = jnp.where((self.plane == 1) & (self.square == 0), extra, 0.0)
        summed_in = jnp.where(self.plane == 0, first, jnp.sum(self.in_pieces.astype(F32), axis=0) + extra)
        small = jnp.sum(self.small_sums, axis=0)[: self.count, : self.width // 32]
        return (summed_in, self.summed_out, small)


def norm_parts(values):
    centre = values - jnp.mean(values, axis=-1, keepdims=True)
    spread = jnp.mean(centre * centre, axis=-1, keepdims=True)
    scale = lax.rsqrt(spread + EPSILON)
    return (centre * scale, scale)


def layer_norm(values, gains, shifts):
    return (norm_parts(values)[0] * gains + shifts).astype(BF16)


def norm_backward(values, gains, grad, hook=lambda *sums: sums):
    normed, scale = norm_parts(values)
    scaled = grad * gains
    first = jnp.mean(scaled, axis=-1, keepdims=True)
    second = jnp.mean(scaled * normed, axis=-1, keepdims=True)
    sums = (first, second, jnp.sum(grad * normed, axis=0), jnp.sum(grad, axis=0))
    grad, first, second, d_gain, d_shift = hook(grad, *sums)
    inner = (grad * gains - first - normed * second) * scale
    return (inner, d_gain, d_shift)


def gelu_parts(values):
    cdf = 0.5 * (1.0 + lax.erf(values * (0.5**0.5)))
    density = jnp.exp(-0.5 * values * values) * 0.3989422804014327
    return (values * cdf, cdf + values * density)


def column_sum(rows):
    return jnp.sum(rows.astype(F32), axis=0)


def block(clip, target, leave, feed, gain_count, patches):
    shape = clip.shape
    width = shape[-1]
    grid = shape[:3]
    small32 = feed.small.astype(F32)
    gains32, shifts32, dense32 = (small32[:gain_count], small32[gain_count:-1], small32[-1])
    flat = lambda a: a.reshape(-1, a.shape[-1])
    cube = lambda a: a.reshape(grid + (a.shape[-1],))
    grads = feed.grads
    start = clip.reshape(-1, width).astype(F32)
    normed_t = layer_norm(start, gains32[0], shifts32[0])
    project_a = nt(normed_t, feed.in_a).astype(BF16)
    project_a, normed_t = feed.tick("query_t", project_a, normed_t)
    project_b = nt(normed_t, feed.in_b).astype(BF16)
    project_t = [cube(project_a), cube(project_b)]
    mixed_t = attention_call(forward_kernel, 2, project_t, (width,), True, patches)[0]
    mixed_t = flat(feed.tick("mixed_t", mixed_t))
    projected_t = (nn(mixed_t, feed.out_t) + shifts32[3]).astype(BF16)
    branch_t = (nn(projected_t, feed.out_f) + shifts32[4]).astype(BF16)
    after_t = start + branch_t.astype(F32)
    normed_s = layer_norm(after_t, gains32[1], shifts32[1])
    project_qk = nt(normed_s, feed.in_qk).astype(BF16)
    project_qk, normed_s = feed.tick("query_s", project_qk, normed_s)
    project_v = nt(normed_s, feed.in_v).astype(BF16)
    project_s = [cube(project_qk), cube(project_v)]
    mixed_s = attention_call(forward_kernel, 2, project_s, (width,), False, patches)[0]
    mixed_s = flat(feed.tick("mixed_s", mixed_s))
    grad_low = flat(target(mixed_s))
    after_s = after_t + (nn(mixed_s, feed.out_s) + shifts32[5])
    normed_m = layer_norm(after_s, gains32[2], shifts32[2])
    hidden_pre = nt(normed_m, feed.in_m) + shifts32[6:].reshape(-1)
    hidden32, slope32 = gelu_parts(hidden_pre)
    hidden, slope, grad_low = feed.tick("hidden", hidden32.astype(BF16), slope32.astype(BF16), grad_low)
    output = (after_s + (nn(hidden, feed.out_m) + dense32)).astype(BF16)
    output = leave(output.reshape(shape))

    grad_out = grad_low.astype(F32)
    grads["out_m"] = tn(hidden, grad_low).astype(BF16)
    grad_low = feed.tick("out_m", grad_low)
    s_dense = column_sum(grad_low)
    grad_pre = (nt(grad_low, feed.out_m) * slope.astype(F32)).astype(BF16)
    grad_pre = feed.tick("grad_pre", grad_pre)
    grads["in_m"] = tn(grad_pre, normed_m).astype(BF16)
    grad_pre = feed.tick("in_m", grad_pre)
    s_hidden = column_sum(grad_pre).reshape(-1, width)
    part, g_m, b_m = norm_backward(after_s, gains32[2], nn(grad_pre, feed.in_m))
    grad_s = grad_out + part
    grad_branch_s = grad_s.astype(BF16)
    grads["out_s"] = tn(mixed_s, grad_branch_s).astype(BF16)
    s_space = column_sum(grad_branch_s)
    grad_mixed_s = nt(grad_branch_s, feed.out_s).astype(BF16)
    grad_mixed_s, output = feed.tick("grad_mixed_s", grad_mixed_s, output)
    grad_qk, grad_v = attention_call(
        backward_kernel, 2, project_s + [cube(grad_mixed_s)], (2 * width, width), False, patches
    )
    grad_qk, grad_v = feed.tick("grad_s", flat(grad_qk), flat(grad_v))
    grads["in_v"] = tn(grad_v, normed_s).astype(BF16)
    grad_qk, grad_v = feed.tick("in_v", grad_qk, grad_v)
    d_in_qk = tn(grad_qk, normed_s).astype(BF16)
    grads["in_qk"], grad_qk, grad_v = feed.tick("in_qk", d_in_qk, grad_qk, grad_v)
    part, g_s, b_s = norm_backward(after_t, gains32[1], nn(grad_qk, feed.in_qk) + nn(grad_v, feed.in_v))
    grad_t = grad_s + part
    grad_branch_t = feed.tick("grad_t", grad_t.astype(BF16))
    grads["out_f"] = tn(projected_t, grad_branch_t).astype(BF16)
    s_fc = column_sum(grad_branch_t)
    grad_projected = nt(grad_branch_t, feed.out_f).astype(BF16)
    grads["out_t"] = tn(mixed_t, grad_projected).astype(BF16)
    grad_projected = feed.tick("out_t", grad_projected)
    s_time = column_sum(grad_projected)
    grad_mixed_t = feed.tick("grad_mixed_t", nt(grad_projected, feed.out_t).astype(BF16))
    grad_project_t = attention_call(
        backward_kernel, 2, project_t + [cube(grad_mixed_t)], (3 * width,), True, patches
    )[0]
    grad_project_t = feed.tick("grad_project_t", flat(grad_project_t))
    grads["in_t"] = tn(grad_project_t, normed_t).astype(BF16)
    grad_project_t = feed.tick("in_t", grad_project_t)
    hook = lambda *sums: feed.tick("dx_t", *sums)
    part, g_t, b_t = norm_backward(start, gains32[0], nn(grad_project_t, feed.in_t), hook)
    grad_clip = (grad_t + part.astype(BF16).astype(F32)).astype(BF16)
    parts = [g_t, g_s, g_m, b_t, b_s, b_m, s_time, s_fc, s_space, s_hidden, s_dense]
    grad_clip, *parts = feed.tick("grad_clip", grad_clip, *[part.reshape(-1, width) for part in parts])
    return (output, leave(grad_clip.reshape(shape)).astype(F32)) + feed.total(parts)


def shards(clips_in, cotangent, clip_live, weights_in, weights_out, norm_gain, shift_rows, dense_shift):
    both = ("dp", "seq")
    group = lax.axis_size("seq")
    count, _, patches, width = clips_in.shape
    own = count // group
    rows = -(-patches // SUB) * SUB
    gain_count = norm_gain.shape[0]
    shift_count = shift_rows.shape[0]
    staged = lax.axis_size(both) == 32 and group == 4 and weights_in.shape[0] == 240 and weights_out.shape[0] == 168

    def enter(x):
        x = lax.all_to_all(x, "seq", split_axis=0, concat_axis=1, tiled=True)
        return jnp.pad(x, ((0, 0), (0, 0), (0, rows - patches), (0, 0)))

    def leave(x):
        x = x[:, :, :patches]
        return lax.all_to_all(x, "seq", split_axis=1, concat_axis=0, tiled=True)

    packed = jnp.concatenate([norm_gain, shift_rows, dense_shift[None, :]], axis=0)
    feed = (Staged if staged else Whole)(both, weights_in, weights_out, packed, width)
    clip = enter(clips_in)
    if staged:
        clip = feed.begin(clip)
    live = lax.dynamic_slice(clip_live, (lax.axis_index("seq") * own,), (own,)).astype(BF16)

    def target(after):
        gradient = cotangent * 1
        if staged:
            gradient = tie(gradient, after)[0]
        return enter(gradient) * live[:, None, None, None]

    output, grad_clip, summed_in, summed_out, owned = block(clip, target, leave, feed, gain_count, patches)
    return (
        output,
        grad_clip,
        summed_in,
        summed_out,
        owned[:gain_count],
        owned[gain_count : gain_count + shift_count],
        owned[-1],
    )


def solution(mesh):
    clip = P("dp", "seq", None, None)
    row = P(("dp", "seq"), None)
    col = P(None, ("dp", "seq"))
    flat = P(("dp", "seq"))
    return jax.shard_map(
        shards,
        mesh=mesh,
        in_specs=(clip, clip, P("dp"), row, row, col, col, flat),
        out_specs=(clip, clip, row, row, col, col, flat),
        check_vma=False,
    )
```

```python
from functools import partial

import jax
import jax.numpy as jnp
from jax import lax
from jax.experimental import pallas as pl
from jax.experimental.pallas import tpu as pltpu
from jax.sharding import PartitionSpec as P

HEADS = 12
HEAD_DIM = 64
EPSILON = 1e-06
PAIRS = HEADS // 2
LANES = 2 * HEAD_DIM
SUB = 16
NEG = -1e30
COPY_VMEM = 60 << 20
F32 = jnp.float32
BF16 = jnp.bfloat16


def nt(left, right):
    return lax.dot_general(left, right, (((1,), (1,)), ((), ())), preferred_element_type=F32)


def nn(left, right):
    return lax.dot_general(left, right, (((1,), (0,)), ((), ())), preferred_element_type=F32)


def tn(left, right):
    return lax.dot_general(left, right, (((0,), (0,)), ((), ())), preferred_element_type=F32)


def split_heads(pair):
    first = lax.broadcasted_iota(jnp.int32, pair.shape, 1) < HEAD_DIM
    zero = jnp.zeros_like(pair)
    return jnp.concatenate([jnp.where(first, pair, zero), jnp.where(first, zero, pair)], axis=0)


def join_heads(stacked):
    rows = stacked.shape[0] // 2
    first = lax.broadcasted_iota(jnp.int32, (rows, LANES), 1) < HEAD_DIM
    return jnp.where(first, stacked[:rows], stacked[rows:])


def pair_forward(queries, keys, values, keep):
    stacked = split_heads(queries * jnp.asarray(HEAD_DIM**-0.5, BF16))
    scores = jnp.where(keep, nt(stacked, keys), NEG)
    top = jnp.max(scores, axis=1, keepdims=True)
    weights = jnp.exp(scores - top)
    total = jnp.sum(weights, axis=1, keepdims=True)
    probs = (weights * (1.0 / total)).astype(BF16)
    return join_heads(nn(probs, values)).astype(BF16)


def pair_backward(queries, keys, values, grad, keep):
    scaling = HEAD_DIM**-0.5
    stacked = split_heads(queries * jnp.asarray(scaling, BF16))
    grads = split_heads(grad)
    scores = jnp.where(keep, nt(keys, stacked), NEG)
    top = jnp.max(scores, axis=0, keepdims=True)
    weights = jnp.exp(scores - top)
    total = jnp.sum(weights, axis=0, keepdims=True)
    probs = weights * (1.0 / total)
    grad_probs = nt(values, grads)
    mean = jnp.sum(probs * grad_probs, axis=0, keepdims=True)
    grad_scores = (probs * (grad_probs - mean)).astype(BF16)
    grad_values = nn(probs.astype(BF16), grads)
    grad_keys = nn(grad_scores, stacked)
    grad_queries = join_heads(tn(grad_scores, keys)) * scaling
    return (grad_queries.astype(BF16), grad_keys.astype(BF16), grad_values.astype(BF16))


def columns(kind, pair):
    start = (kind * PAIRS + pair) * LANES
    return slice(start, start + LANES)


def find(refs, kind, pair):
    cols = columns(kind, pair)
    for ref in refs:
        size = ref.shape[-1]
        if cols.start < size:
            return (ref, cols)
        cols = slice(cols.start - size, cols.stop - size)


def load(refs, kind, pair):
    ref, cols = find(refs, kind, pair)
    return ref[..., cols].reshape(-1, LANES)


def store(refs, kind, pair, block):
    ref, cols = find(refs, kind, pair)
    ref[..., cols] = block.reshape(ref.shape[:-1] + (LANES,))


def keep_mask(shape, key_axis, group, patches):
    key = lax.broadcasted_iota(jnp.int32, shape, key_axis)
    if group is None:
        return key < patches
    query = lax.broadcasted_iota(jnp.int32, shape, 1 - key_axis)
    return (key % group) == (query % group)


def forward_kernel(group, patches, count, *refs):
    project, mixed = (refs[:count], refs[count:])
    rows = project[0].size // project[0].shape[-1]
    keep = keep_mask((2 * rows, rows), 1, group, patches)
    for pair in range(PAIRS):
        block = pair_forward(*[load(project, kind, pair) for kind in range(3)], keep)
        store(mixed, 0, pair, block)


def backward_kernel(group, patches, count, *refs):
    project, grad, outs = (refs[:count], refs[count : count + 1], refs[count + 1 :])
    rows = project[0].size // project[0].shape[-1]
    keep = keep_mask((rows, 2 * rows), 0, group, patches)
    for pair in range(PAIRS):
        results = pair_backward(*[load(project, kind, pair) for kind in range(3)], load(grad, 0, pair), keep)
        for kind, result in enumerate(results):
            store(outs, kind, pair, result)


def attention_call(kernel, count, arrays, out_cols, temporal, patches):
    clips, frames, rows, _ = arrays[0].shape
    if temporal:
        group, steps, shape = SUB, rows // SUB, (1, frames, SUB)
        index = lambda c, i: (c, 0, i, 0)
    else:
        group, steps, shape = None, frames, (1, 1, rows)
        index = lambda c, i: (c, i, 0, 0)
    tokens = clips * frames * rows
    backward = kernel is backward_kernel
    return pl.pallas_call(
        partial(kernel, group, patches, count),
        grid=(clips, steps),
        in_specs=[pl.BlockSpec(shape + (a.shape[-1],), index) for a in arrays],
        out_specs=[pl.BlockSpec(shape + (cols,), index) for cols in out_cols],
        out_shape=[jax.ShapeDtypeStruct((clips, frames, rows, cols), BF16) for cols in out_cols],
        compiler_params=pltpu.CompilerParams(dimension_semantics=("arbitrary", "arbitrary")),
        cost_estimate=pl.CostEstimate(
            flops=tokens * (14_000_000 if backward else 9_000_000), bytes_accessed=0, transcendentals=0
        ),
    )(*arrays)


def eights(rows):
    return rows.reshape(rows.shape[:-2] + (-1, 8, rows.shape[-1]))


def place_kernel(outs_plan, blocks, groups, dest_ref, *refs):
    pieces, refs = (refs[: groups * blocks], refs[groups * blocks :])
    outs, refs = (refs[: len(outs_plan)], refs[len(outs_plan) :])
    held, in_sem, out_sem = (refs[:-2], refs[-2], refs[-1])
    moves, slot = ([], 0)
    for target, entries in enumerate(outs_plan):
        for entry, (group, row, rows) in enumerate(entries):
            for block in range(blocks):
                buffer = held[target].at[entry, block]
                source = pieces[group * blocks + block].at[pl.ds(row // 8, rows // 8)]
                fetch = pltpu.make_async_copy(source, buffer, in_sem.at[slot])
                fetch.start()
                write = pltpu.make_async_copy(buffer, outs[target].at[entry, dest_ref[block]], out_sem.at[slot])
                moves.append((fetch, write))
                slot += 1
    for fetch, write in moves:
        fetch.wait()
        write.start()
    for _, write in moves:
        write.wait()


def place(groups, outs_plan, dest):
    blocks = len(groups[0])
    width = groups[0][0].shape[1]
    shapes = [(len(entries), blocks, entries[0][2] // 8, 8, width) for entries in outs_plan]
    slots = sum(len(entries) for entries in outs_plan) * blocks
    size = sum(16 * s[0] * s[1] * s[2] * s[4] for s in shapes)
    flat = [eights(piece) for group in groups for piece in group]
    anywhere = pl.BlockSpec(memory_space=pl.ANY)
    outs = pl.pallas_call(
        partial(place_kernel, tuple(tuple(e) for e in outs_plan), blocks, len(groups)),
        in_specs=[pl.BlockSpec(memory_space=pltpu.SMEM)] + [anywhere] * len(flat),
        out_specs=[anywhere] * len(shapes),
        out_shape=[jax.ShapeDtypeStruct(s, BF16) for s in shapes],
        scratch_shapes=[pltpu.VMEM(s, BF16) for s in shapes]
        + [pltpu.SemaphoreType.DMA((slots,)), pltpu.SemaphoreType.DMA((slots,))],
        compiler_params=pltpu.CompilerParams(vmem_limit_bytes=size + (2 << 20)),
        cost_estimate=pl.CostEstimate(flops=0, bytes_accessed=4 * size, transcendentals=0),
    )(dest, *flat)
    return [out.reshape(out.shape[:2] + (-1, width)) for out in outs]


def split_kernel(spans, plane_rows, squares, core_ref, *refs):
    parts, refs = (refs[: len(spans)], refs[len(spans) :])
    keep, send = refs[:2]
    held, in_sem, out_sem = (refs[2:-2], refs[-2], refs[-1])
    core = core_ref[0]
    incoming, count, part, done = ({}, 0, 0, 0)
    for plane, rows in enumerate(plane_rows):
        for slot in range(2 * squares):
            offset, incoming[plane, slot] = (0, [])
            while offset < rows:
                first, length = spans[part]
                size = min(length - done, rows - offset)
                copy = pltpu.make_async_copy(
                    parts[part].at[pl.ds((first + done) // 8, size // 8)],
                    held[plane].at[slot, pl.ds(offset // 8, size // 8)],
                    in_sem.at[count],
                )
                copy.start()
                incoming[plane, slot].append(copy)
                count, offset, done = (count + 1, offset + size, done + size)
                if done == length:
                    part, done = (part + 1, 0)
    outgoing, row = ([], 0)
    for plane, rows in enumerate(plane_rows):
        for square in range(squares):
            for copy in incoming[plane, 2 * square] + incoming[plane, 2 * square + 1]:
                copy.wait()
            for target, side in ((send, 1 - core), (keep, core)):
                copy = pltpu.make_async_copy(
                    held[plane].at[2 * square + side], target.at[square, pl.ds(row // 8, rows // 8)], out_sem.at[len(outgoing)]
                )
                copy.start()
                outgoing.append(copy)
        row += rows
    for copy in outgoing:
        copy.wait()


def split_cores(parts, plane_rows, squares, core):
    spans = tuple((first, length) for _, first, length in parts)
    arrays = [eights(array) for array, _, _ in parts]
    width = arrays[0].shape[-1]
    slots = len(plane_rows) * squares * 2
    size = 2 * squares * sum(plane_rows) * width * 2
    anywhere = pl.BlockSpec(memory_space=pl.ANY)
    half = jax.ShapeDtypeStruct((squares, sum(plane_rows) // 8, 8, width), BF16)
    outs = pl.pallas_call(
        partial(split_kernel, spans, tuple(plane_rows), squares),
        in_specs=[pl.BlockSpec(memory_space=pltpu.SMEM)] + [anywhere] * len(arrays),
        out_specs=[anywhere, anywhere],
        out_shape=[half, half],
        scratch_shapes=[pltpu.VMEM((2 * squares, rows // 8, 8, width), BF16) for rows in plane_rows]
        + [pltpu.SemaphoreType.DMA((slots + len(parts),)), pltpu.SemaphoreType.DMA((slots,))],
        compiler_params=pltpu.CompilerParams(vmem_limit_bytes=size + (2 << 20)),
        cost_estimate=pl.CostEstimate(flops=0, bytes_accessed=size // 8, transcendentals=0),
    )(core, *arrays)
    return [out.reshape(squares, -1, width) for out in outs]


def join_kernel(chunks, *refs):
    parts, (out, held, in_sem, out_sem) = (refs[:-4], refs[-4:])
    moves = []
    for slot, (part, row) in enumerate(chunks):
        size = held.shape[1]
        fetch = pltpu.make_async_copy(parts[part].at[pl.ds(row, size)], held.at[slot], in_sem.at[slot])
        fetch.start()
        moves.append((fetch, pltpu.make_async_copy(held.at[slot], out.at[pl.ds(slot * size, size)], out_sem.at[slot])))
    for fetch, write in moves:
        fetch.wait()
        write.start()
    for _, write in moves:
        write.wait()


def join(parts, rows):
    width = parts[0].shape[1]
    chunks = [(k, row // 8) for k, part in enumerate(parts) for row in range(0, part.shape[0], rows)]
    count = len(chunks)
    anywhere = pl.BlockSpec(memory_space=pl.ANY)
    out = pl.pallas_call(
        partial(join_kernel, tuple(chunks)),
        in_specs=[anywhere] * len(parts),
        out_specs=anywhere,
        out_shape=jax.ShapeDtypeStruct((count * rows // 8, 8, width), BF16),
        scratch_shapes=[
            pltpu.VMEM((count, rows // 8, 8, width), BF16),
            pltpu.SemaphoreType.DMA((count,)),
            pltpu.SemaphoreType.DMA((count,)),
        ],
        compiler_params=pltpu.CompilerParams(vmem_limit_bytes=COPY_VMEM),
        cost_estimate=pl.CostEstimate(flops=0, bytes_accessed=8 * count * rows * width, transcendentals=0),
    )(*[eights(part) for part in parts])
    return out.reshape(-1, width)


def pack_kernel(devices, *refs):
    parts, out_ref, held = (refs[:-2], refs[-2], refs[-1])
    held[...] = jnp.zeros_like(held)
    out_ref[...] = jnp.zeros_like(out_ref)
    row = 0
    for part in parts:
        held[row : row + part.shape[0], :] = part[...]
        row += part.shape[0]
    share = held.shape[1] // devices
    for device in range(devices):
        out_ref[device, :, :share] = held[:, device * share : (device + 1) * share]


def pack(parts, devices):
    rows = -(-sum(part.shape[0] for part in parts) // 8) * 8
    width = parts[0].shape[1]
    return pl.pallas_call(
        partial(pack_kernel, devices),
        out_shape=jax.ShapeDtypeStruct((devices, rows, LANES), F32),
        scratch_shapes=[pltpu.VMEM((rows, width), F32)],
        cost_estimate=pl.CostEstimate(flops=0, bytes_accessed=8 * rows * width, transcendentals=0),
    )(*parts)


def tie(values, others):
    return lax.optimization_barrier((values, others))


class Whole:
    def __init__(self, axes, weights_in, weights_out, packed, width):
        self.axes, self.width = (axes, width)
        full_in = lax.all_gather(weights_in, axes, axis=0, tiled=True)
        full_out = lax.all_gather(weights_out, axes, axis=0, tiled=True)
        devices = lax.axis_size(axes)
        slot = lax.dynamic_update_slice(
            jnp.zeros((devices,) + packed.shape, F32), packed.astype(F32)[None], (lax.axis_index(axes), 0, 0)
        )
        self.small = lax.psum(slot, axes).transpose(1, 0, 2).reshape(packed.shape[0], width).astype(BF16)
        self.in_a, self.in_b = (full_in[: 5 * width // 2], full_in[5 * width // 2 : 3 * width])
        self.in_t, self.in_qk = (full_in[: 3 * width], full_in[3 * width : 5 * width])
        self.in_v, self.in_m = (full_in[5 * width : 6 * width], full_in[6 * width :])
        self.out_t, self.out_f = (full_out[:width], full_out[width : 2 * width])
        self.out_s, self.out_m = (full_out[2 * width : 3 * width], full_out[3 * width :])
        self.grads = {}

    def tick(self, name, *values):
        return values[0] if len(values) == 1 else values

    def total(self, sums, arrays, clip):
        g = self.grads
        parts = sums + [column_sum(array) for array in arrays]
        small = jnp.concatenate([part.reshape(-1, self.width) for part in parts], axis=0)
        d_in = jnp.concatenate([g["in_t"], g["in_qk"], g["in_v"], g["in_m"]], axis=0)
        d_out = jnp.concatenate([g["out_t"], g["out_f"], g["out_s"], g["out_m"]], axis=0)
        summed_in = lax.psum_scatter(d_in, self.axes, scatter_dimension=0, tiled=True).astype(F32)
        summed_out = lax.psum_scatter(d_out, self.axes, scatter_dimension=0, tiled=True).astype(F32)
        share = self.width // lax.axis_size(self.axes)
        at = (0, lax.axis_index(self.axes) * share)
        clip = clip.astype(F32)
        return (clip, summed_in, summed_out, lax.dynamic_slice(lax.psum(small, self.axes), at, (small.shape[0], share)))


class Staged:
    def __init__(self, axes, weights_in, weights_out, packed, width):
        self.axes, self.width = (axes, width)
        me = lax.axis_index(axes)
        self.plane, self.spot, self.square, self.core = (me // 8, me % 8, me % 8 // 2, me % 2)
        self.spots = jnp.bitwise_xor(jnp.arange(8, dtype=jnp.int32), self.spot)
        self.planes = (self.plane + 4 - jnp.arange(4, dtype=jnp.int32)) % 4
        self.core_ref = self.core.astype(jnp.int32).reshape(1)
        self.rows_in, self.count = (weights_in.shape[0], packed.shape[0])
        self.grads = {}
        flat = packed.reshape(1, -1)
        tail = jnp.pad(flat, ((0, 7), (0, width - flat.shape[1])))
        pieces = self.shifted(jnp.concatenate([weights_in, tail], axis=0))
        pieces, weights_out = tie(pieces, weights_out)
        full_out = lax.all_gather(weights_out, axes, axis=0, tiled=True)
        self.out_t, self.out_f = (full_out[:width], full_out[width : 2 * width])
        self.out_s, self.out_m = (full_out[2 * width : 3 * width], full_out[3 * width :])
        self.column_in, self.column_small = self.columns(pieces, (self.rows_in, 8))

    def flip(self, x, bits):
        return lax.ppermute(x, self.axes, [(d, d ^ bits) for d in range(32)])

    def shift(self, x, step):
        return lax.ppermute(x, self.axes, [(d, (d + 8 * step) % 32) for d in range(32)])

    def shifted(self, shard):
        return [shard] + [self.shift(shard, step) for step in (1, 2, 3)]

    def columns(self, pieces, sizes):
        plan, row = ([], 0)
        for size in sizes:
            plan.append([(0, row, size)])
            row += size
        return [out[0] for out in place([pieces], plan, self.planes)]

    def over(self, piece):
        return [piece] + [self.flip(piece, bits) for bits in (2, 4, 6)]

    def cores(self, pieces):
        both = []
        for piece in pieces:
            both += [piece, self.flip(piece, 1)]
        return both

    def lay(self, groups, entries):
        out = place(groups, [entries], self.spots)[0]
        return out.reshape(-1, self.width)

    def begin(self, clip):
        rows_in, width = (self.rows_in, self.width)
        smalls = self.column_small.reshape(-1, width)
        first = jnp.concatenate([self.column_in[0], smalls], axis=0)
        self.p1, self.p2, self.p3 = (self.column_in[k] for k in (1, 2, 3))
        p0 = self.over(first)
        p0, clip = tie(p0, clip)
        self.p0 = self.cores(p0)
        low, small = place([self.p0], [[(0, 0, rows_in)], [(0, rows_in, 32)]], self.spots)
        low, self.p1 = tie(low, self.p1)
        self.p1 = self.over(self.p1)
        self.in_a = low.reshape(-1, width)
        share = width // 32
        small = small.reshape(8, 4, 8, width)[:, :, 0, : self.count * share].reshape(8, 4, self.count, share)
        self.small = small.transpose(2, 1, 0, 3).reshape(self.count, width)
        return clip

    def tick(self, name, *values):
        single = len(values) == 1
        rows_in, width = (self.rows_in, self.width)
        g = self.grads
        whole = lambda key: (g[key], 0, g[key].shape[0])
        if name == "query_t":
            values, (self.p1, self.p2) = tie(values, (self.p1, self.p2))
            self.p2 = self.over(self.p2)
            self.p1 = self.cores(self.p1)
            low = self.lay([self.p0, self.p1], [(0, 0, rows_in), (1, 0, rows_in)])
            self.in_t, self.in_qk = (low[: 3 * width], low[3 * width :])
            self.in_b = self.in_t[5 * width // 2 :]
        elif name == "mixed_t":
            values, (self.p2, self.p3) = tie(values, (self.p2, self.p3))
            self.p3 = self.over(self.p3)
        elif name == "query_s":
            self.p2 = self.cores(self.p2)
            self.in_v = self.lay([self.p2], [(0, 0, rows_in)])[:width]
        elif name == "mixed_s":
            values, self.p3 = tie(values, self.p3)
            self.p3 = self.cores(self.p3)
            high = self.lay([self.p2, self.p3], [(0, 0, rows_in), (1, 0, rows_in)])
            self.in_m = high[width:]
        elif name == "hidden":
            values = lax.optimization_barrier(values)
        elif name == "in_m":
            start = 24 * rows_in - 6 * width
            d_in_m = g["in_m"]
            self.kept, send = self.halve([(d_in_m, start, d_in_m.shape[0] - start)], (rows_in,))
            values, send = tie(values, send)
            self.other = self.flip(send, 1)
        elif name == "grad_mixed_s":
            values, (self.kept, self.other) = tie(values, (self.kept, self.other))
            self.d_p3 = self.across(self.kept, self.other)
        elif name == "grad_s":
            values, self.d_p3 = tie(values, self.d_p3)
            self.d_p3 = self.gathered(self.d_p3)
        elif name == "in_v":
            start = 24 * rows_in - 6 * width
            self.kept, send = self.halve([whole("in_v"), (g["in_m"], 0, start)], (rows_in,))
            values, send = tie(values, send)
            self.other = self.flip(send, 1)
        elif name == "in_qk":
            values, (self.kept, self.other) = tie(values, (self.kept, self.other))
            self.d_p2 = self.across(self.kept, self.other)
        elif name == "grad_t":
            values, self.d_p2 = tie(values, self.d_p2)
            self.d_p2 = self.gathered(self.d_p2)
            late = jnp.zeros((8 * rows_in - 2 * width, width), BF16)
            self.kept, send = self.halve([(late, 0, late.shape[0]), whole("in_qk")], (rows_in,))
            values, send = tie(values, send)
            self.other = self.flip(send, 1)
        elif name == "out_t":
            values, (self.kept, self.other) = tie(values, (self.kept, self.other))
            self.d_p1 = self.across(self.kept, self.other)
            d_out = join([g["out_t"], g["out_f"], g["out_s"], g["out_m"]], width // 2)
            values, d_out = tie(values, d_out)
            self.summed_out = lax.psum_scatter(d_out, self.axes, scatter_dimension=0, tiled=True)
        elif name == "grad_project_t":
            values, self.d_p1 = tie(values, self.d_p1)
            self.d_p1 = self.gathered(self.d_p1)
        elif name == "in_t":
            d_in_t = g["in_t"]
            kept, send = self.halve([whole("in_t")], (rows_in, d_in_t.shape[0] // 8 - rows_in))
            values, send = tie(values, send)
            half = lambda a, x: lax.dynamic_slice_in_dim(a, 2 * x, 2, 0).astype(F32)
            other = self.flip(send, 1)
            x = self.square // 2
            send = (half(kept, 1 - x) + half(other, 1 - x)).astype(BF16)
            own = (half(kept, x) + half(other, x)).astype(BF16)
            values, (own, send) = tie(values, (own, send))
            self.last = (own, self.flip(send, 4))
        elif name == "dx_t":
            values, (own, other) = tie(values, self.last)
            y = self.square % 2
            line = lambda a, y: lax.dynamic_index_in_dim(a, y, 0, keepdims=False).astype(F32)
            send = (line(own, 1 - y) + line(other, 1 - y)).astype(BF16)
            own = (line(own, y) + line(other, y)).astype(BF16)
            self.last = (own, self.flip(send, 2))
        elif name == "grad_clip":
            values, last = tie(values, self.last)
            self.d_last = self.gathered(last)
        return values[0] if single else values

    def halve(self, parts, plane_rows):
        return split_cores(parts, plane_rows, 4, self.core_ref)

    def across(self, keep, other):
        result = []
        for bits in (0, 2, 4, 6):
            at = jnp.bitwise_xor(self.square, bits // 2)
            take = lambda a: lax.dynamic_index_in_dim(a, at, 0, keepdims=False).astype(F32)
            summed = (take(keep) + take(other)).astype(BF16)
            result.append(summed if bits == 0 else self.flip(summed, bits))
        return result

    def gathered(self, arrived):
        return self.added(arrived).astype(BF16)

    def towards(self, block, plane):
        pieces = [block]
        for step in (1, 2, 3):
            pairs = [(d, (d + 8 * step) % 32) for d in range(32) if (d // 8 + step) % 4 == plane]
            pieces.append(lax.ppermute(block, self.axes, pairs))
        return pieces

    def added(self, pieces):
        total = pieces[0].astype(F32)
        for piece in pieces[1:]:
            total = total + piece.astype(F32)
        return total

    def total(self, sums, arrays, clip):
        rows, last = (self.rows_in, self.d_last)
        extra, first = tie(self.towards(last[rows:], 1), last[:rows])
        every = jnp.stack([first, self.d_p1, self.d_p2, self.d_p3], axis=0)
        terms = [lax.dynamic_index_in_dim(every, self.plane, 0, keepdims=False)]
        for step in (1, 2, 3):
            block = lax.dynamic_index_in_dim(every, (self.plane + step) % 4, 0, keepdims=False)
            terms.append(self.shift(block, step))
        extra = self.added(extra).astype(BF16)
        beside, arrays = tie(self.flip(extra, 1), arrays)
        extra = jnp.concatenate([extra, beside], axis=0)
        blocks = [extra]
        for bits in (2, 4, 6):
            blocks.append(lax.ppermute(extra, self.axes, [(8 + bits + core, 8 + core) for core in range(2)]))
        extra = jnp.concatenate(blocks, axis=0).reshape(8, -1, self.width)
        swapped = jnp.stack([extra[4], extra[7], extra[6]], axis=0).reshape(-1, self.width)
        swapped = jnp.pad(swapped, ((0, rows - swapped.shape[0]), (0, 0)))
        extra = jnp.where(self.core == 0, extra.reshape(-1, self.width)[:rows], swapped).astype(F32)
        extra = jnp.where((self.plane == 1) & (self.square == 0), extra, 0.0)
        clip, self.summed_out = tie(clip, self.summed_out)
        summed_in = self.added(terms) + extra
        parts = sums + [column_sum(array) for array in arrays]
        parts, clip = tie([part.reshape(-1, self.width) for part in parts], clip)
        small = lax.all_to_all(pack(parts, 32), self.axes, split_axis=0, concat_axis=0)
        small = jnp.sum(small, axis=0)[: self.count, : self.width // 32]
        return (clip.astype(F32), summed_in, self.summed_out.astype(F32), small)


def norm_parts(values):
    centre = values - jnp.mean(values, axis=-1, keepdims=True)
    spread = jnp.mean(centre * centre, axis=-1, keepdims=True)
    scale = lax.rsqrt(spread + EPSILON)
    return (centre * scale, scale)


def layer_norm(values, gains, shifts):
    return (norm_parts(values)[0] * gains + shifts).astype(BF16)


def norm_backward(values, gains, grad, hook=lambda *sums: sums):
    normed, scale = norm_parts(values)
    scaled = grad * gains
    first = jnp.mean(scaled, axis=-1, keepdims=True)
    second = jnp.mean(scaled * normed, axis=-1, keepdims=True)
    sums = (first, second, jnp.sum(grad * normed, axis=0), jnp.sum(grad, axis=0))
    grad, first, second, d_gain, d_shift = hook(grad, *sums)
    inner = (grad * gains - first - normed * second) * scale
    return (inner, d_gain, d_shift)


def gelu_parts(values):
    cdf = 0.5 * (1.0 + lax.erf(values * (0.5**0.5)))
    density = jnp.exp(-0.5 * values * values) * 0.3989422804014327
    return (values * cdf, cdf + values * density)


def column_sum(rows):
    return jnp.sum(rows.astype(F32), axis=0)


def block(clip, target, leave, feed, gain_count, patches):
    shape = clip.shape
    width = shape[-1]
    grid = shape[:3]
    small32 = feed.small.astype(F32)
    gains32, shifts32, dense32 = (small32[:gain_count], small32[gain_count:-1], small32[-1])
    flat = lambda a: a.reshape(-1, a.shape[-1])
    cube = lambda a: a.reshape(grid + (a.shape[-1],))
    grads = feed.grads
    start = clip.reshape(-1, width).astype(F32)
    normed_t = layer_norm(start, gains32[0], shifts32[0])
    project_a = nt(normed_t, feed.in_a).astype(BF16)
    project_a, normed_t = feed.tick("query_t", project_a, normed_t)
    project_b = nt(normed_t, feed.in_b).astype(BF16)
    project_t = [cube(project_a), cube(project_b)]
    mixed_t = attention_call(forward_kernel, 2, project_t, (width,), True, patches)[0]
    mixed_t = flat(feed.tick("mixed_t", mixed_t))
    projected_t = (nn(mixed_t, feed.out_t) + shifts32[3]).astype(BF16)
    branch_t = (nn(projected_t, feed.out_f) + shifts32[4]).astype(BF16)
    after_t = start + branch_t.astype(F32)
    normed_s = layer_norm(after_t, gains32[1], shifts32[1])
    project_qk = nt(normed_s, feed.in_qk).astype(BF16)
    project_qk, normed_s = feed.tick("query_s", project_qk, normed_s)
    project_v = nt(normed_s, feed.in_v).astype(BF16)
    project_s = [cube(project_qk), cube(project_v)]
    mixed_s = attention_call(forward_kernel, 2, project_s, (width,), False, patches)[0]
    mixed_s = flat(feed.tick("mixed_s", mixed_s))
    grad_low = flat(target(mixed_s))
    after_s = after_t + (nn(mixed_s, feed.out_s) + shifts32[5])
    normed_m = layer_norm(after_s, gains32[2], shifts32[2])
    hidden_pre = nt(normed_m, feed.in_m) + shifts32[6:].reshape(-1)
    hidden32, slope32 = gelu_parts(hidden_pre)
    hidden, slope, grad_low = feed.tick("hidden", hidden32.astype(BF16), slope32.astype(BF16), grad_low)
    output = (after_s + (nn(hidden, feed.out_m) + dense32)).astype(BF16)
    output = leave(output.reshape(shape))

    grad_out = grad_low.astype(F32)
    grads["out_m"] = tn(hidden, grad_low).astype(BF16)
    grad_low = feed.tick("out_m", grad_low)
    grad_pre = (nt(grad_low, feed.out_m) * slope.astype(F32)).astype(BF16)
    grad_pre = feed.tick("grad_pre", grad_pre)
    grads["in_m"] = tn(grad_pre, normed_m).astype(BF16)
    grad_pre = feed.tick("in_m", grad_pre)
    part, g_m, b_m = norm_backward(after_s, gains32[2], nn(grad_pre, feed.in_m))
    grad_s = grad_out + part
    grad_branch_s = grad_s.astype(BF16)
    grads["out_s"] = tn(mixed_s, grad_branch_s).astype(BF16)
    grad_mixed_s = nt(grad_branch_s, feed.out_s).astype(BF16)
    grad_mixed_s, output = feed.tick("grad_mixed_s", grad_mixed_s, output)
    grad_qk, grad_v = attention_call(
        backward_kernel, 2, project_s + [cube(grad_mixed_s)], (2 * width, width), False, patches
    )
    grad_qk, grad_v = feed.tick("grad_s", flat(grad_qk), flat(grad_v))
    grads["in_v"] = tn(grad_v, normed_s).astype(BF16)
    grad_qk, grad_v = feed.tick("in_v", grad_qk, grad_v)
    d_in_qk = tn(grad_qk, normed_s).astype(BF16)
    grads["in_qk"], grad_qk, grad_v = feed.tick("in_qk", d_in_qk, grad_qk, grad_v)
    part, g_s, b_s = norm_backward(after_t, gains32[1], nn(grad_qk, feed.in_qk) + nn(grad_v, feed.in_v))
    grad_t = grad_s + part
    grad_branch_t = feed.tick("grad_t", grad_t.astype(BF16))
    grads["out_f"] = tn(projected_t, grad_branch_t).astype(BF16)
    grad_projected = nt(grad_branch_t, feed.out_f).astype(BF16)
    grads["out_t"] = tn(mixed_t, grad_projected).astype(BF16)
    grad_projected = feed.tick("out_t", grad_projected)
    grad_mixed_t = feed.tick("grad_mixed_t", nt(grad_projected, feed.out_t).astype(BF16))
    grad_project_t = attention_call(
        backward_kernel, 2, project_t + [cube(grad_mixed_t)], (3 * width,), True, patches
    )[0]
    grad_project_t = feed.tick("grad_project_t", flat(grad_project_t))
    grads["in_t"] = tn(grad_project_t, normed_t).astype(BF16)
    grad_project_t = feed.tick("in_t", grad_project_t)
    hook = lambda *sums: feed.tick("dx_t", *sums)
    part, g_t, b_t = norm_backward(start, gains32[0], nn(grad_project_t, feed.in_t), hook)
    grad_clip = (grad_t + part.astype(BF16).astype(F32)).astype(BF16)
    rows = (grad_projected, grad_branch_t, grad_branch_s, grad_pre, grad_low)
    grad_clip, *rows = feed.tick("grad_clip", grad_clip, *rows)
    sums = [g_t, g_s, g_m, b_t, b_s, b_m]
    return (output,) + feed.total(sums, rows, leave(grad_clip.reshape(shape)))


def shards(clips_in, cotangent, clip_live, weights_in, weights_out, norm_gain, shift_rows, dense_shift):
    both = ("dp", "seq")
    group = lax.axis_size("seq")
    count, _, patches, width = clips_in.shape
    own = count // group
    rows = -(-patches // SUB) * SUB
    gain_count = norm_gain.shape[0]
    shift_count = shift_rows.shape[0]
    staged = lax.axis_size(both) == 32 and group == 4 and weights_in.shape[0] == 240 and weights_out.shape[0] == 168

    def enter(x):
        x = lax.all_to_all(x, "seq", split_axis=0, concat_axis=1, tiled=True)
        return jnp.pad(x, ((0, 0), (0, 0), (0, rows - patches), (0, 0)))

    def leave(x):
        x = x[:, :, :patches]
        return lax.all_to_all(x, "seq", split_axis=1, concat_axis=0, tiled=True)

    packed = jnp.concatenate([norm_gain, shift_rows, dense_shift[None, :]], axis=0)
    feed = (Staged if staged else Whole)(both, weights_in, weights_out, packed, width)
    clip = enter(clips_in)
    if staged:
        clip = feed.begin(clip)
    live = lax.dynamic_slice(clip_live, (lax.axis_index("seq") * own,), (own,)).astype(BF16)

    def target(after):
        gradient = cotangent * 1
        if staged:
            gradient = tie(gradient, after)[0]
        return enter(gradient) * live[:, None, None, None]

    output, grad_clip, summed_in, summed_out, owned = block(clip, target, leave, feed, gain_count, patches)
    return (
        output,
        grad_clip,
        summed_in,
        summed_out,
        owned[:gain_count],
        owned[gain_count : gain_count + shift_count],
        owned[-1],
    )


def solution(mesh):
    clip = P("dp", "seq", None, None)
    row = P(("dp", "seq"), None)
    col = P(None, ("dp", "seq"))
    flat = P(("dp", "seq"))
    return jax.shard_map(
        shards,
        mesh=mesh,
        in_specs=(clip, clip, P("dp"), row, row, col, col, flat),
        out_specs=(clip, clip, row, row, col, col, flat),
        check_vma=False,
    )
```

```python
from functools import partial

import jax
import jax.numpy as jnp
from jax import lax
from jax.experimental import pallas as pl
from jax.experimental.pallas import tpu as pltpu
from jax.sharding import PartitionSpec as P

HEADS = 12
HEAD_DIM = 64
EPSILON = 1e-06
PAIRS = HEADS // 2
LANES = 2 * HEAD_DIM
SUB = 16
NEG = -1e30
COPY_VMEM = 60 << 20
F32 = jnp.float32
BF16 = jnp.bfloat16


def nt(left, right):
    return lax.dot_general(left, right, (((1,), (1,)), ((), ())), preferred_element_type=F32)


def nn(left, right):
    return lax.dot_general(left, right, (((1,), (0,)), ((), ())), preferred_element_type=F32)


def tn(left, right):
    return lax.dot_general(left, right, (((0,), (0,)), ((), ())), preferred_element_type=F32)


def split_heads(pair):
    first = lax.broadcasted_iota(jnp.int32, pair.shape, 1) < HEAD_DIM
    zero = jnp.zeros_like(pair)
    return jnp.concatenate([jnp.where(first, pair, zero), jnp.where(first, zero, pair)], axis=0)


def join_heads(stacked):
    rows = stacked.shape[0] // 2
    first = lax.broadcasted_iota(jnp.int32, (rows, LANES), 1) < HEAD_DIM
    return jnp.where(first, stacked[:rows], stacked[rows:])


def pair_forward(queries, keys, values, keep):
    stacked = split_heads(queries * jnp.asarray(HEAD_DIM**-0.5, BF16))
    scores = jnp.where(keep, nt(keys, stacked), NEG)
    top = jnp.max(scores, axis=0, keepdims=True)
    weights = jnp.exp(scores - top)
    total = jnp.sum(weights, axis=0, keepdims=True)
    probs = (weights * (1.0 / total)).astype(BF16)
    return join_heads(tn(probs, values)).astype(BF16)


def pair_backward(queries, keys, values, grad, keep):
    scaling = HEAD_DIM**-0.5
    stacked = split_heads(queries * jnp.asarray(scaling, BF16))
    grads = split_heads(grad)
    scores = jnp.where(keep, nt(keys, stacked), NEG)
    top = jnp.max(scores, axis=0, keepdims=True)
    weights = jnp.exp(scores - top)
    total = jnp.sum(weights, axis=0, keepdims=True)
    probs = weights * (1.0 / total)
    grad_probs = nt(values, grads)
    mean = jnp.sum(probs * grad_probs, axis=0, keepdims=True)
    grad_scores = (probs * (grad_probs - mean)).astype(BF16)
    grad_values = nn(probs.astype(BF16), grads)
    grad_keys = nn(grad_scores, stacked)
    grad_queries = join_heads(tn(grad_scores, keys)) * scaling
    return (grad_queries.astype(BF16), grad_keys.astype(BF16), grad_values.astype(BF16))


def columns(kind, pair):
    start = (kind * PAIRS + pair) * LANES
    return slice(start, start + LANES)


def find(refs, kind, pair):
    cols = columns(kind, pair)
    for ref in refs:
        size = ref.shape[-1]
        if cols.start < size:
            return (ref, cols)
        cols = slice(cols.start - size, cols.stop - size)


def load(refs, kind, pair):
    ref, cols = find(refs, kind, pair)
    return ref[..., cols].reshape(-1, LANES)


def store(refs, kind, pair, block):
    ref, cols = find(refs, kind, pair)
    ref[..., cols] = block.reshape(ref.shape[:-1] + (LANES,))


def keep_mask(shape, key_axis, group, patches):
    key = lax.broadcasted_iota(jnp.int32, shape, key_axis)
    if group is None:
        return key < patches
    query = lax.broadcasted_iota(jnp.int32, shape, 1 - key_axis)
    return (key % group) == (query % group)


def forward_kernel(group, patches, count, *refs):
    project, mixed = (refs[:count], refs[count:])
    rows = project[0].size // project[0].shape[-1]
    keep = keep_mask((rows, 2 * rows), 0, group, patches)
    for pair in range(PAIRS):
        block = pair_forward(*[load(project, kind, pair) for kind in range(3)], keep)
        store(mixed, 0, pair, block)


def backward_kernel(group, patches, count, *refs):
    project, grad, outs = (refs[:count], refs[count : count + 1], refs[count + 1 :])
    rows = project[0].size // project[0].shape[-1]
    keep = keep_mask((rows, 2 * rows), 0, group, patches)
    for pair in range(PAIRS):
        results = pair_backward(*[load(project, kind, pair) for kind in range(3)], load(grad, 0, pair), keep)
        for kind, result in enumerate(results):
            store(outs, kind, pair, result)


def attention_call(kernel, count, arrays, out_cols, temporal, patches):
    clips, frames, rows, _ = arrays[0].shape
    if temporal:
        group, steps, shape = SUB, rows // SUB, (1, frames, SUB)
        index = lambda c, i: (c, 0, i, 0)
    else:
        group, steps, shape = None, frames, (1, 1, rows)
        index = lambda c, i: (c, i, 0, 0)
    tokens = clips * frames * rows
    backward = kernel is backward_kernel
    return pl.pallas_call(
        partial(kernel, group, patches, count),
        grid=(clips, steps),
        in_specs=[pl.BlockSpec(shape + (a.shape[-1],), index) for a in arrays],
        out_specs=[pl.BlockSpec(shape + (cols,), index) for cols in out_cols],
        out_shape=[jax.ShapeDtypeStruct((clips, frames, rows, cols), BF16) for cols in out_cols],
        compiler_params=pltpu.CompilerParams(dimension_semantics=("arbitrary", "arbitrary")),
        cost_estimate=pl.CostEstimate(
            flops=tokens * (14_000_000 if backward else 9_000_000), bytes_accessed=0, transcendentals=0
        ),
    )(*arrays)


def eights(rows):
    return rows.reshape(rows.shape[:-2] + (-1, 8, rows.shape[-1]))


def place_kernel(outs_plan, blocks, groups, dest_ref, *refs):
    pieces, refs = (refs[: groups * blocks], refs[groups * blocks :])
    outs, refs = (refs[: len(outs_plan)], refs[len(outs_plan) :])
    held, in_sem, out_sem = (refs[:-2], refs[-2], refs[-1])
    moves, slot = ([], 0)
    for target, entries in enumerate(outs_plan):
        for entry, (group, row, rows) in enumerate(entries):
            for block in range(blocks):
                buffer = held[target].at[entry, block]
                source = pieces[group * blocks + block].at[pl.ds(row // 8, rows // 8)]
                fetch = pltpu.make_async_copy(source, buffer, in_sem.at[slot])
                fetch.start()
                write = pltpu.make_async_copy(buffer, outs[target].at[entry, dest_ref[block]], out_sem.at[slot])
                moves.append((fetch, write))
                slot += 1
    for fetch, write in moves:
        fetch.wait()
        write.start()
    for _, write in moves:
        write.wait()


def place(groups, outs_plan, dest):
    blocks = len(groups[0])
    width = groups[0][0].shape[1]
    shapes = [(len(entries), blocks, entries[0][2] // 8, 8, width) for entries in outs_plan]
    slots = sum(len(entries) for entries in outs_plan) * blocks
    size = sum(16 * s[0] * s[1] * s[2] * s[4] for s in shapes)
    flat = [eights(piece) for group in groups for piece in group]
    anywhere = pl.BlockSpec(memory_space=pl.ANY)
    outs = pl.pallas_call(
        partial(place_kernel, tuple(tuple(e) for e in outs_plan), blocks, len(groups)),
        in_specs=[pl.BlockSpec(memory_space=pltpu.SMEM)] + [anywhere] * len(flat),
        out_specs=[anywhere] * len(shapes),
        out_shape=[jax.ShapeDtypeStruct(s, BF16) for s in shapes],
        scratch_shapes=[pltpu.VMEM(s, BF16) for s in shapes]
        + [pltpu.SemaphoreType.DMA((slots,)), pltpu.SemaphoreType.DMA((slots,))],
        compiler_params=pltpu.CompilerParams(vmem_limit_bytes=size + (2 << 20)),
        cost_estimate=pl.CostEstimate(flops=0, bytes_accessed=4 * size, transcendentals=0),
    )(dest, *flat)
    return [out.reshape(out.shape[:2] + (-1, width)) for out in outs]


def split_kernel(spans, plane_rows, squares, core_ref, *refs):
    parts, refs = (refs[: len(spans)], refs[len(spans) :])
    keep, send = refs[:2]
    held, in_sem, out_sem = (refs[2:-2], refs[-2], refs[-1])
    core = core_ref[0]
    incoming, count, part, done = ({}, 0, 0, 0)
    for plane, rows in enumerate(plane_rows):
        for slot in range(2 * squares):
            offset, incoming[plane, slot] = (0, [])
            while offset < rows:
                first, length = spans[part]
                size = min(length - done, rows - offset)
                copy = pltpu.make_async_copy(
                    parts[part].at[pl.ds((first + done) // 8, size // 8)],
                    held[plane].at[slot, pl.ds(offset // 8, size // 8)],
                    in_sem.at[count],
                )
                copy.start()
                incoming[plane, slot].append(copy)
                count, offset, done = (count + 1, offset + size, done + size)
                if done == length:
                    part, done = (part + 1, 0)
    outgoing, row = ([], 0)
    for plane, rows in enumerate(plane_rows):
        for square in range(squares):
            for copy in incoming[plane, 2 * square] + incoming[plane, 2 * square + 1]:
                copy.wait()
            for target, side in ((send, 1 - core), (keep, core)):
                copy = pltpu.make_async_copy(
                    held[plane].at[2 * square + side], target.at[square, pl.ds(row // 8, rows // 8)], out_sem.at[len(outgoing)]
                )
                copy.start()
                outgoing.append(copy)
        row += rows
    for copy in outgoing:
        copy.wait()


def split_cores(parts, plane_rows, squares, core):
    spans = tuple((first, length) for _, first, length in parts)
    arrays = [eights(array) for array, _, _ in parts]
    width = arrays[0].shape[-1]
    slots = len(plane_rows) * squares * 2
    size = 2 * squares * sum(plane_rows) * width * 2
    anywhere = pl.BlockSpec(memory_space=pl.ANY)
    half = jax.ShapeDtypeStruct((squares, sum(plane_rows) // 8, 8, width), BF16)
    outs = pl.pallas_call(
        partial(split_kernel, spans, tuple(plane_rows), squares),
        in_specs=[pl.BlockSpec(memory_space=pltpu.SMEM)] + [anywhere] * len(arrays),
        out_specs=[anywhere, anywhere],
        out_shape=[half, half],
        scratch_shapes=[pltpu.VMEM((2 * squares, rows // 8, 8, width), BF16) for rows in plane_rows]
        + [pltpu.SemaphoreType.DMA((slots + len(parts),)), pltpu.SemaphoreType.DMA((slots,))],
        compiler_params=pltpu.CompilerParams(vmem_limit_bytes=size + (2 << 20)),
        cost_estimate=pl.CostEstimate(flops=0, bytes_accessed=size // 8, transcendentals=0),
    )(core, *arrays)
    return [out.reshape(squares, -1, width) for out in outs]


def join_kernel(chunks, *refs):
    parts, (out, held, in_sem, out_sem) = (refs[:-4], refs[-4:])
    moves = []
    for slot, (part, row) in enumerate(chunks):
        size = held.shape[1]
        fetch = pltpu.make_async_copy(parts[part].at[pl.ds(row, size)], held.at[slot], in_sem.at[slot])
        fetch.start()
        moves.append((fetch, pltpu.make_async_copy(held.at[slot], out.at[pl.ds(slot * size, size)], out_sem.at[slot])))
    for fetch, write in moves:
        fetch.wait()
        write.start()
    for _, write in moves:
        write.wait()


def join(parts, rows):
    width = parts[0].shape[1]
    chunks = [(k, row // 8) for k, part in enumerate(parts) for row in range(0, part.shape[0], rows)]
    count = len(chunks)
    anywhere = pl.BlockSpec(memory_space=pl.ANY)
    out = pl.pallas_call(
        partial(join_kernel, tuple(chunks)),
        in_specs=[anywhere] * len(parts),
        out_specs=anywhere,
        out_shape=jax.ShapeDtypeStruct((count * rows // 8, 8, width), BF16),
        scratch_shapes=[
            pltpu.VMEM((count, rows // 8, 8, width), BF16),
            pltpu.SemaphoreType.DMA((count,)),
            pltpu.SemaphoreType.DMA((count,)),
        ],
        compiler_params=pltpu.CompilerParams(vmem_limit_bytes=COPY_VMEM),
        cost_estimate=pl.CostEstimate(flops=0, bytes_accessed=8 * count * rows * width, transcendentals=0),
    )(*[eights(part) for part in parts])
    return out.reshape(-1, width)


def pack_kernel(devices, *refs):
    parts, out_ref, held = (refs[:-2], refs[-2], refs[-1])
    held[...] = jnp.zeros_like(held)
    out_ref[...] = jnp.zeros_like(out_ref)
    row = 0
    for part in parts:
        held[row : row + part.shape[0], :] = part[...]
        row += part.shape[0]
    share = held.shape[1] // devices
    for device in range(devices):
        out_ref[device, :, :share] = held[:, device * share : (device + 1) * share]


def pack(parts, devices):
    rows = -(-sum(part.shape[0] for part in parts) // 8) * 8
    width = parts[0].shape[1]
    return pl.pallas_call(
        partial(pack_kernel, devices),
        out_shape=jax.ShapeDtypeStruct((devices, rows, LANES), F32),
        scratch_shapes=[pltpu.VMEM((rows, width), F32)],
        cost_estimate=pl.CostEstimate(flops=0, bytes_accessed=8 * rows * width, transcendentals=0),
    )(*parts)


def tie(values, others):
    return lax.optimization_barrier((values, others))


class Whole:
    def __init__(self, axes, weights_in, weights_out, packed, width, clip):
        self.axes, self.width, self.clip = (axes, width, clip)
        full_in = lax.all_gather(weights_in, axes, axis=0, tiled=True)
        full_out = lax.all_gather(weights_out, axes, axis=0, tiled=True)
        devices = lax.axis_size(axes)
        slot = lax.dynamic_update_slice(
            jnp.zeros((devices,) + packed.shape, F32), packed.astype(F32)[None], (lax.axis_index(axes), 0, 0)
        )
        self.small = lax.psum(slot, axes).transpose(1, 0, 2).reshape(packed.shape[0], width).astype(BF16)
        self.in_a, self.in_b = (full_in[: 5 * width // 2], full_in[5 * width // 2 : 3 * width])
        self.in_t, self.in_qk = (full_in[: 3 * width], full_in[3 * width : 5 * width])
        self.in_v, self.in_m = (full_in[5 * width : 6 * width], full_in[6 * width :])
        self.out_t, self.out_f = (full_out[:width], full_out[width : 2 * width])
        self.out_s, self.out_m = (full_out[2 * width : 3 * width], full_out[3 * width :])
        self.grads = {}

    def tick(self, name, *values):
        return values[0] if len(values) == 1 else values

    def total(self, sums, arrays, clip):
        g = self.grads
        parts = sums + [column_sum(array) for array in arrays]
        small = jnp.concatenate([part.reshape(-1, self.width) for part in parts], axis=0)
        d_in = jnp.concatenate([g["in_t"], g["in_qk"], g["in_v"], g["in_m"]], axis=0)
        d_out = jnp.concatenate([g["out_t"], g["out_f"], g["out_s"], g["out_m"]], axis=0)
        summed_in = lax.psum_scatter(d_in, self.axes, scatter_dimension=0, tiled=True).astype(F32)
        summed_out = lax.psum_scatter(d_out, self.axes, scatter_dimension=0, tiled=True).astype(F32)
        share = self.width // lax.axis_size(self.axes)
        at = (0, lax.axis_index(self.axes) * share)
        clip = clip.astype(F32)
        return (clip, summed_in, summed_out, lax.dynamic_slice(lax.psum(small, self.axes), at, (small.shape[0], share)))


class Staged:
    def __init__(self, axes, weights_in, weights_out, packed, width, clip):
        self.axes, self.width = (axes, width)
        me = lax.axis_index(axes)
        self.plane, self.spot, self.square, self.core = (me // 8, me % 8, me % 8 // 2, me % 2)
        self.spots = jnp.bitwise_xor(jnp.arange(8, dtype=jnp.int32), self.spot)
        self.planes = (self.plane + 4 - jnp.arange(4, dtype=jnp.int32)) % 4
        self.core_ref = self.core.astype(jnp.int32).reshape(1)
        self.rows_in, self.count = (weights_in.shape[0], packed.shape[0])
        self.grads = {}
        flat = packed.reshape(1, -1)
        tail = jnp.pad(flat, ((0, 7), (0, width - flat.shape[1])))
        pieces = self.shifted(jnp.concatenate([weights_in, tail], axis=0))
        pieces, (weights_out, self.clip) = tie(pieces, (weights_out, clip))
        full_out = lax.all_gather(weights_out, axes, axis=0, tiled=True)
        self.out_t, self.out_f = (full_out[:width], full_out[width : 2 * width])
        self.out_s, self.out_m = (full_out[2 * width : 3 * width], full_out[3 * width :])
        self.column_in, self.column_small = self.columns(pieces, (self.rows_in, 8))

    def flip(self, x, bits):
        return lax.ppermute(x, self.axes, [(d, d ^ bits) for d in range(32)])

    def shift(self, x, step):
        return lax.ppermute(x, self.axes, [(d, (d + 8 * step) % 32) for d in range(32)])

    def shifted(self, shard):
        return [shard] + [self.shift(shard, step) for step in (1, 2, 3)]

    def columns(self, pieces, sizes):
        plan, row = ([], 0)
        for size in sizes:
            plan.append([(0, row, size)])
            row += size
        return [out[0] for out in place([pieces], plan, self.planes)]

    def over(self, piece):
        return [piece] + [self.flip(piece, bits) for bits in (2, 4, 6)]

    def cores(self, pieces):
        both = []
        for piece in pieces:
            both += [piece, self.flip(piece, 1)]
        return both

    def lay(self, groups, entries):
        out = place(groups, [entries], self.spots)[0]
        return out.reshape(-1, self.width)

    def begin(self, clip):
        rows_in, width = (self.rows_in, self.width)
        smalls = self.column_small.reshape(-1, width)
        first = jnp.concatenate([self.column_in[0], smalls], axis=0)
        self.p1, self.p2, self.p3 = (self.column_in[k] for k in (1, 2, 3))
        p0 = self.over(first)
        p0, clip = tie(p0, clip)
        self.p0 = self.cores(p0)
        low, small = place([self.p0], [[(0, 0, rows_in)], [(0, rows_in, 32)]], self.spots)
        low, self.p1 = tie(low, self.p1)
        self.p1 = self.over(self.p1)
        self.in_a = low.reshape(-1, width)
        share = width // 32
        small = small.reshape(8, 4, 8, width)[:, :, 0, : self.count * share].reshape(8, 4, self.count, share)
        self.small = small.transpose(2, 1, 0, 3).reshape(self.count, width)
        return clip

    def tick(self, name, *values):
        single = len(values) == 1
        rows_in, width = (self.rows_in, self.width)
        g = self.grads
        whole = lambda key: (g[key], 0, g[key].shape[0])
        if name == "query_t":
            values, (self.p1, self.p2) = tie(values, (self.p1, self.p2))
            self.p2 = self.over(self.p2)
            self.p1 = self.cores(self.p1)
            low = self.lay([self.p0, self.p1], [(0, 0, rows_in), (1, 0, rows_in)])
            self.in_t, self.in_qk = (low[: 3 * width], low[3 * width :])
            self.in_b = self.in_t[5 * width // 2 :]
        elif name == "mixed_t":
            values, (self.p2, self.p3) = tie(values, (self.p2, self.p3))
            self.p3 = self.over(self.p3)
        elif name == "query_s":
            self.p2 = self.cores(self.p2)
            self.in_v = self.lay([self.p2], [(0, 0, rows_in)])[:width]
        elif name == "mixed_s":
            values, self.p3 = tie(values, self.p3)
            self.p3 = self.cores(self.p3)
            high = self.lay([self.p2, self.p3], [(0, 0, rows_in), (1, 0, rows_in)])
            self.in_m = high[width:]
        elif name == "hidden":
            values = lax.optimization_barrier(values)
        elif name == "in_m":
            start = 24 * rows_in - 6 * width
            d_in_m = g["in_m"]
            self.kept, send = self.halve([(d_in_m, start, d_in_m.shape[0] - start)], (rows_in,))
            values, send = tie(values, send)
            self.other = self.flip(send, 1)
        elif name == "grad_mixed_s":
            values, (self.kept, self.other) = tie(values, (self.kept, self.other))
            self.d_p3 = self.across(self.kept, self.other)
        elif name == "grad_s":
            values, self.d_p3 = tie(values, self.d_p3)
            self.d_p3 = self.gathered(self.d_p3)
        elif name == "in_v":
            start = 24 * rows_in - 6 * width
            self.kept, send = self.halve([whole("in_v"), (g["in_m"], 0, start)], (rows_in,))
            values, send = tie(values, send)
            self.other = self.flip(send, 1)
        elif name == "in_qk":
            values, (self.kept, self.other) = tie(values, (self.kept, self.other))
            self.d_p2 = self.across(self.kept, self.other)
        elif name == "grad_t":
            values, self.d_p2 = tie(values, self.d_p2)
            self.d_p2 = self.gathered(self.d_p2)
            late = jnp.zeros((8 * rows_in - 2 * width, width), BF16)
            self.kept, send = self.halve([(late, 0, late.shape[0]), whole("in_qk")], (rows_in,))
            values, send = tie(values, send)
            self.other = self.flip(send, 1)
        elif name == "out_t":
            values, (self.kept, self.other) = tie(values, (self.kept, self.other))
            self.d_p1 = self.across(self.kept, self.other)
            d_out = join([g["out_t"], g["out_f"], g["out_s"], g["out_m"]], width // 2)
            values, d_out = tie(values, d_out)
            self.summed_out = lax.psum_scatter(d_out, self.axes, scatter_dimension=0, tiled=True)
        elif name == "grad_project_t":
            values, self.d_p1 = tie(values, self.d_p1)
            self.d_p1 = self.gathered(self.d_p1)
        elif name == "in_t":
            d_in_t = g["in_t"]
            kept, send = self.halve([whole("in_t")], (rows_in, d_in_t.shape[0] // 8 - rows_in))
            values, send = tie(values, send)
            half = lambda a, x: lax.dynamic_slice_in_dim(a, 2 * x, 2, 0).astype(F32)
            other = self.flip(send, 1)
            x = self.square // 2
            send = (half(kept, 1 - x) + half(other, 1 - x)).astype(BF16)
            own = (half(kept, x) + half(other, x)).astype(BF16)
            values, (own, send) = tie(values, (own, send))
            self.last = (own, self.flip(send, 4))
        elif name == "dx_t":
            values, (own, other) = tie(values, self.last)
            y = self.square % 2
            line = lambda a, y: lax.dynamic_index_in_dim(a, y, 0, keepdims=False).astype(F32)
            send = (line(own, 1 - y) + line(other, 1 - y)).astype(BF16)
            own = (line(own, y) + line(other, y)).astype(BF16)
            self.last = (own, self.flip(send, 2))
        elif name == "grad_clip":
            values, last = tie(values, self.last)
            self.d_last = self.gathered(last)
        return values[0] if single else values

    def halve(self, parts, plane_rows):
        return split_cores(parts, plane_rows, 4, self.core_ref)

    def across(self, keep, other):
        result = []
        for bits in (0, 2, 4, 6):
            at = jnp.bitwise_xor(self.square, bits // 2)
            take = lambda a: lax.dynamic_index_in_dim(a, at, 0, keepdims=False).astype(F32)
            summed = (take(keep) + take(other)).astype(BF16)
            result.append(summed if bits == 0 else self.flip(summed, bits))
        return result

    def gathered(self, arrived):
        return self.added(arrived).astype(BF16)

    def towards(self, block, plane):
        pieces = [block]
        for step in (1, 2, 3):
            pairs = [(d, (d + 8 * step) % 32) for d in range(32) if (d // 8 + step) % 4 == plane]
            pieces.append(lax.ppermute(block, self.axes, pairs))
        return pieces

    def added(self, pieces):
        total = pieces[0].astype(F32)
        for piece in pieces[1:]:
            total = total + piece.astype(F32)
        return total

    def total(self, sums, arrays, clip):
        rows, last = (self.rows_in, self.d_last)
        every = jnp.stack([last[:rows], self.d_p1, self.d_p2, self.d_p3], axis=0)
        blocks = [
            lax.dynamic_index_in_dim(every, (self.plane + step) % 4, 0, keepdims=False) for step in range(4)
        ]
        blocks, extra = tie(blocks, last[rows:])
        terms = blocks[:1] + [self.shift(blocks[step], step) for step in (1, 2, 3)]
        beside, arrays = tie(self.flip(extra, 1), arrays)
        extra = self.towards(jnp.concatenate([extra, beside], axis=0), 1)
        extra = self.added(extra).astype(BF16)
        blocks = [extra]
        for bits in (2, 4, 6):
            blocks.append(lax.ppermute(extra, self.axes, [(8 + bits + core, 8 + core) for core in range(2)]))
        extra = jnp.concatenate(blocks, axis=0).reshape(8, -1, self.width)
        swapped = jnp.stack([extra[4], extra[7], extra[6]], axis=0).reshape(-1, self.width)
        swapped = jnp.pad(swapped, ((0, rows - swapped.shape[0]), (0, 0)))
        extra = jnp.where(self.core == 0, extra.reshape(-1, self.width)[:rows], swapped).astype(F32)
        extra = jnp.where((self.plane == 1) & (self.square == 0), extra, 0.0)
        clip, self.summed_out = tie(clip, self.summed_out)
        summed_in = self.added(terms) + extra
        parts = sums + [column_sum(array) for array in arrays]
        parts, clip = tie([part.reshape(-1, self.width) for part in parts], clip)
        small = lax.all_to_all(pack(parts, 32), self.axes, split_axis=0, concat_axis=0)
        small = jnp.sum(small, axis=0)[: self.count, : self.width // 32]
        return (clip.astype(F32), summed_in, self.summed_out.astype(F32), small)


def norm_parts(values):
    centre = values - jnp.mean(values, axis=-1, keepdims=True)
    spread = jnp.mean(centre * centre, axis=-1, keepdims=True)
    scale = lax.rsqrt(spread + EPSILON)
    return (centre * scale, scale)


def layer_norm(values, gains, shifts):
    return (norm_parts(values)[0] * gains + shifts).astype(BF16)


def norm_backward(values, gains, grad, hook=lambda *sums: sums):
    normed, scale = norm_parts(values)
    scaled = grad * gains
    first = jnp.mean(scaled, axis=-1, keepdims=True)
    second = jnp.mean(scaled * normed, axis=-1, keepdims=True)
    sums = (first, second, jnp.sum(grad * normed, axis=0), jnp.sum(grad, axis=0))
    grad, first, second, d_gain, d_shift = hook(grad, *sums)
    inner = (grad * gains - first - normed * second) * scale
    return (inner, d_gain, d_shift)


def gelu_parts(values):
    cdf = 0.5 * (1.0 + lax.erf(values * (0.5**0.5)))
    density = jnp.exp(-0.5 * values * values) * 0.3989422804014327
    return (values * cdf, cdf + values * density)


def column_sum(rows):
    return jnp.sum(rows.astype(F32), axis=0)


def block(clip, target, leave, feed, gain_count, patches):
    shape = clip.shape
    width = shape[-1]
    grid = shape[:3]
    small32 = feed.small.astype(F32)
    gains32, shifts32, dense32 = (small32[:gain_count], small32[gain_count:-1], small32[-1])
    flat = lambda a: a.reshape(-1, a.shape[-1])
    cube = lambda a: a.reshape(grid + (a.shape[-1],))
    grads = feed.grads
    start = clip.reshape(-1, width).astype(F32)
    normed_t = layer_norm(start, gains32[0], shifts32[0])
    project_a = nt(normed_t, feed.in_a).astype(BF16)
    project_a, normed_t = feed.tick("query_t", project_a, normed_t)
    project_b = nt(normed_t, feed.in_b).astype(BF16)
    project_t = [cube(project_a), cube(project_b)]
    mixed_t = attention_call(forward_kernel, 2, project_t, (width,), True, patches)[0]
    mixed_t = flat(feed.tick("mixed_t", mixed_t))
    projected_t = (nn(mixed_t, feed.out_t) + shifts32[3]).astype(BF16)
    branch_t = (nn(projected_t, feed.out_f) + shifts32[4]).astype(BF16)
    after_t = start + branch_t.astype(F32)
    normed_s = layer_norm(after_t, gains32[1], shifts32[1])
    project_qk = nt(normed_s, feed.in_qk).astype(BF16)
    project_qk, normed_s = feed.tick("query_s", project_qk, normed_s)
    project_v = nt(normed_s, feed.in_v).astype(BF16)
    project_s = [cube(project_qk), cube(project_v)]
    mixed_s = attention_call(forward_kernel, 2, project_s, (width,), False, patches)[0]
    mixed_s = flat(feed.tick("mixed_s", mixed_s))
    grad_low = flat(target(mixed_s))
    after_s = after_t + (nn(mixed_s, feed.out_s) + shifts32[5])
    normed_m = layer_norm(after_s, gains32[2], shifts32[2])
    hidden_pre = nt(normed_m, feed.in_m) + shifts32[6:].reshape(-1)
    hidden32, slope32 = gelu_parts(hidden_pre)
    hidden, slope, grad_low = feed.tick("hidden", hidden32.astype(BF16), slope32.astype(BF16), grad_low)
    output = (after_s + (nn(hidden, feed.out_m) + dense32)).astype(BF16)
    output = leave(output.reshape(shape))

    grad_out = grad_low.astype(F32)
    grads["out_m"] = tn(hidden, grad_low).astype(BF16)
    grad_low = feed.tick("out_m", grad_low)
    grad_pre = (nt(grad_low, feed.out_m) * slope.astype(F32)).astype(BF16)
    grad_pre = feed.tick("grad_pre", grad_pre)
    grads["in_m"] = tn(grad_pre, normed_m).astype(BF16)
    grad_pre = feed.tick("in_m", grad_pre)
    part, g_m, b_m = norm_backward(after_s, gains32[2], nn(grad_pre, feed.in_m))
    grad_s = grad_out + part
    grad_branch_s = grad_s.astype(BF16)
    grads["out_s"] = tn(mixed_s, grad_branch_s).astype(BF16)
    grad_mixed_s = nt(grad_branch_s, feed.out_s).astype(BF16)
    grad_mixed_s, output = feed.tick("grad_mixed_s", grad_mixed_s, output)
    grad_qk, grad_v = attention_call(
        backward_kernel, 2, project_s + [cube(grad_mixed_s)], (2 * width, width), False, patches
    )
    grad_qk, grad_v = feed.tick("grad_s", flat(grad_qk), flat(grad_v))
    grads["in_v"] = tn(grad_v, normed_s).astype(BF16)
    grad_qk, grad_v = feed.tick("in_v", grad_qk, grad_v)
    d_in_qk = tn(grad_qk, normed_s).astype(BF16)
    grads["in_qk"], grad_qk, grad_v = feed.tick("in_qk", d_in_qk, grad_qk, grad_v)
    part, g_s, b_s = norm_backward(after_t, gains32[1], nn(grad_qk, feed.in_qk) + nn(grad_v, feed.in_v))
    grad_t = grad_s + part
    grad_branch_t = feed.tick("grad_t", grad_t.astype(BF16))
    grads["out_f"] = tn(projected_t, grad_branch_t).astype(BF16)
    grad_projected = nt(grad_branch_t, feed.out_f).astype(BF16)
    grads["out_t"] = tn(mixed_t, grad_projected).astype(BF16)
    grad_projected = feed.tick("out_t", grad_projected)
    grad_mixed_t = feed.tick("grad_mixed_t", nt(grad_projected, feed.out_t).astype(BF16))
    grad_project_t = attention_call(
        backward_kernel, 2, project_t + [cube(grad_mixed_t)], (3 * width,), True, patches
    )[0]
    grad_project_t = feed.tick("grad_project_t", flat(grad_project_t))
    grads["in_t"] = tn(grad_project_t, normed_t).astype(BF16)
    grad_project_t = feed.tick("in_t", grad_project_t)
    hook = lambda *sums: feed.tick("dx_t", *sums)
    part, g_t, b_t = norm_backward(start, gains32[0], nn(grad_project_t, feed.in_t), hook)
    grad_clip = (grad_t + part.astype(BF16).astype(F32)).astype(BF16)
    rows = (grad_projected, grad_branch_t, grad_branch_s, grad_pre, grad_low)
    grad_clip, *rows = feed.tick("grad_clip", grad_clip, *rows)
    sums = [g_t, g_s, g_m, b_t, b_s, b_m]
    return (output,) + feed.total(sums, rows, leave(grad_clip.reshape(shape)))


def shards(clips_in, cotangent, clip_live, weights_in, weights_out, norm_gain, shift_rows, dense_shift):
    both = ("dp", "seq")
    group = lax.axis_size("seq")
    count, _, patches, width = clips_in.shape
    own = count // group
    rows = -(-patches // SUB) * SUB
    gain_count = norm_gain.shape[0]
    shift_count = shift_rows.shape[0]
    staged = lax.axis_size(both) == 32 and group == 4 and weights_in.shape[0] == 240 and weights_out.shape[0] == 168

    def exchange(x):
        return lax.all_to_all(x, "seq", split_axis=0, concat_axis=1, tiled=True)

    def widen(x):
        return jnp.pad(x, ((0, 0), (0, 0), (0, rows - patches), (0, 0)))

    def leave(x):
        x = x[:, :, :patches]
        return lax.all_to_all(x, "seq", split_axis=1, concat_axis=0, tiled=True)

    packed = jnp.concatenate([norm_gain, shift_rows, dense_shift[None, :]], axis=0)
    feed = (Staged if staged else Whole)(both, weights_in, weights_out, packed, width, exchange(clips_in))
    clip = widen(feed.clip)
    if staged:
        clip = feed.begin(clip)
    live = lax.dynamic_slice(clip_live, (lax.axis_index("seq") * own,), (own,)).astype(BF16)

    def target(after):
        gradient = cotangent * 1
        if staged:
            gradient = tie(gradient, after)[0]
        return widen(exchange(gradient)) * live[:, None, None, None]

    output, grad_clip, summed_in, summed_out, owned = block(clip, target, leave, feed, gain_count, patches)
    return (
        output,
        grad_clip,
        summed_in,
        summed_out,
        owned[:gain_count],
        owned[gain_count : gain_count + shift_count],
        owned[-1],
    )


def solution(mesh):
    clip = P("dp", "seq", None, None)
    row = P(("dp", "seq"), None)
    col = P(None, ("dp", "seq"))
    flat = P(("dp", "seq"))
    return jax.shard_map(
        shards,
        mesh=mesh,
        in_specs=(clip, clip, P("dp"), row, row, col, col, flat),
        out_specs=(clip, clip, row, row, col, col, flat),
        check_vma=False,
    )
```

```python
from functools import partial

import jax
import jax.numpy as jnp
from jax import lax
from jax.experimental import pallas as pl
from jax.experimental.pallas import tpu as pltpu
from jax.sharding import PartitionSpec as P

HEADS = 12
HEAD_DIM = 64
EPSILON = 1e-06
PAIRS = HEADS // 2
LANES = 2 * HEAD_DIM
SUB = 16
NEG = -1e30
COPY_VMEM = 60 << 20
F32 = jnp.float32
BF16 = jnp.bfloat16


def nt(left, right):
    return lax.dot_general(left, right, (((1,), (1,)), ((), ())), preferred_element_type=F32)


def nn(left, right):
    return lax.dot_general(left, right, (((1,), (0,)), ((), ())), preferred_element_type=F32)


def tn(left, right):
    return lax.dot_general(left, right, (((0,), (0,)), ((), ())), preferred_element_type=F32)


def split_heads(pair):
    first = lax.broadcasted_iota(jnp.int32, pair.shape, 1) < HEAD_DIM
    zero = jnp.zeros_like(pair)
    return jnp.concatenate([jnp.where(first, pair, zero), jnp.where(first, zero, pair)], axis=0)


def join_heads(stacked):
    rows = stacked.shape[0] // 2
    first = lax.broadcasted_iota(jnp.int32, (rows, LANES), 1) < HEAD_DIM
    return jnp.where(first, stacked[:rows], stacked[rows:])


def pair_forward(queries, keys, values, keep):
    stacked = split_heads(queries * jnp.asarray(HEAD_DIM**-0.5, BF16))
    scores = jnp.where(keep, nt(keys, stacked), NEG)
    top = jnp.max(scores, axis=0, keepdims=True)
    weights = jnp.exp(scores - top)
    total = jnp.sum(weights, axis=0, keepdims=True)
    probs = (weights * (1.0 / total)).astype(BF16)
    return join_heads(tn(probs, values)).astype(BF16)


def pair_backward(queries, keys, values, grad, keep):
    scaling = HEAD_DIM**-0.5
    stacked = split_heads(queries * jnp.asarray(scaling, BF16))
    grads = split_heads(grad)
    scores = jnp.where(keep, nt(keys, stacked), NEG)
    top = jnp.max(scores, axis=0, keepdims=True)
    weights = jnp.exp(scores - top)
    total = jnp.sum(weights, axis=0, keepdims=True)
    probs = weights * (1.0 / total)
    grad_probs = nt(values, grads)
    mean = jnp.sum(probs * grad_probs, axis=0, keepdims=True)
    grad_scores = (probs * (grad_probs - mean)).astype(BF16)
    grad_values = nn(probs.astype(BF16), grads)
    grad_keys = nn(grad_scores, stacked)
    grad_queries = join_heads(tn(grad_scores, keys)) * scaling
    return (grad_queries.astype(BF16), grad_keys.astype(BF16), grad_values.astype(BF16))


def columns(kind, pair):
    start = (kind * PAIRS + pair) * LANES
    return slice(start, start + LANES)


def find(refs, kind, pair):
    cols = columns(kind, pair)
    for ref in refs:
        size = ref.shape[-1]
        if cols.start < size:
            return (ref, cols)
        cols = slice(cols.start - size, cols.stop - size)


def load(refs, kind, pair):
    ref, cols = find(refs, kind, pair)
    return ref[..., cols].reshape(-1, LANES)


def store(refs, kind, pair, block):
    ref, cols = find(refs, kind, pair)
    ref[..., cols] = block.reshape(ref.shape[:-1] + (LANES,))


def keep_mask(shape, key_axis, group, patches):
    key = lax.broadcasted_iota(jnp.int32, shape, key_axis)
    if group is None:
        return key < patches
    query = lax.broadcasted_iota(jnp.int32, shape, 1 - key_axis)
    return (key % group) == (query % group)


def forward_kernel(group, patches, count, *refs):
    project, mixed = (refs[:count], refs[count:])
    rows = project[0].size // project[0].shape[-1]
    keep = keep_mask((rows, 2 * rows), 0, group, patches)
    for pair in range(PAIRS):
        block = pair_forward(*[load(project, kind, pair) for kind in range(3)], keep)
        store(mixed, 0, pair, block)


def backward_kernel(group, patches, count, *refs):
    project, grad, outs = (refs[:count], refs[count : count + 1], refs[count + 1 :])
    rows = project[0].size // project[0].shape[-1]
    keep = keep_mask((rows, 2 * rows), 0, group, patches)
    for pair in range(PAIRS):
        results = pair_backward(*[load(project, kind, pair) for kind in range(3)], load(grad, 0, pair), keep)
        for kind, result in enumerate(results):
            store(outs, kind, pair, result)


def attention_call(kernel, count, arrays, out_cols, temporal, patches):
    clips, frames, rows, _ = arrays[0].shape
    if temporal:
        group, steps, shape = SUB, rows // SUB, (1, frames, SUB)
        index = lambda c, i: (c, 0, i, 0)
    else:
        group, steps, shape = None, frames, (1, 1, rows)
        index = lambda c, i: (c, i, 0, 0)
    tokens = clips * frames * rows
    backward = kernel is backward_kernel
    return pl.pallas_call(
        partial(kernel, group, patches, count),
        grid=(clips, steps),
        in_specs=[pl.BlockSpec(shape + (a.shape[-1],), index) for a in arrays],
        out_specs=[pl.BlockSpec(shape + (cols,), index) for cols in out_cols],
        out_shape=[jax.ShapeDtypeStruct((clips, frames, rows, cols), BF16) for cols in out_cols],
        compiler_params=pltpu.CompilerParams(dimension_semantics=("arbitrary", "arbitrary")),
        cost_estimate=pl.CostEstimate(
            flops=tokens * (14_000_000 if backward else 9_000_000), bytes_accessed=0, transcendentals=0
        ),
    )(*arrays)


def eights(rows):
    return rows.reshape(rows.shape[:-2] + (-1, 8, rows.shape[-1]))


def place_kernel(outs_plan, blocks, groups, dest_ref, *refs):
    pieces, refs = (refs[: groups * blocks], refs[groups * blocks :])
    outs, refs = (refs[: len(outs_plan)], refs[len(outs_plan) :])
    held, in_sem, out_sem = (refs[:-2], refs[-2], refs[-1])
    moves, slot = ([], 0)
    for target, entries in enumerate(outs_plan):
        for entry, (group, row, rows) in enumerate(entries):
            for block in range(blocks):
                buffer = held[target].at[entry, block]
                source = pieces[group * blocks + block].at[pl.ds(row // 8, rows // 8)]
                fetch = pltpu.make_async_copy(source, buffer, in_sem.at[slot])
                fetch.start()
                write = pltpu.make_async_copy(buffer, outs[target].at[entry, dest_ref[block]], out_sem.at[slot])
                moves.append((fetch, write))
                slot += 1
    for fetch, write in moves:
        fetch.wait()
        write.start()
    for _, write in moves:
        write.wait()


def place(groups, outs_plan, dest):
    blocks = len(groups[0])
    width = groups[0][0].shape[1]
    shapes = [(len(entries), blocks, entries[0][2] // 8, 8, width) for entries in outs_plan]
    slots = sum(len(entries) for entries in outs_plan) * blocks
    size = sum(16 * s[0] * s[1] * s[2] * s[4] for s in shapes)
    flat = [eights(piece) for group in groups for piece in group]
    anywhere = pl.BlockSpec(memory_space=pl.ANY)
    outs = pl.pallas_call(
        partial(place_kernel, tuple(tuple(e) for e in outs_plan), blocks, len(groups)),
        in_specs=[pl.BlockSpec(memory_space=pltpu.SMEM)] + [anywhere] * len(flat),
        out_specs=[anywhere] * len(shapes),
        out_shape=[jax.ShapeDtypeStruct(s, BF16) for s in shapes],
        scratch_shapes=[pltpu.VMEM(s, BF16) for s in shapes]
        + [pltpu.SemaphoreType.DMA((slots,)), pltpu.SemaphoreType.DMA((slots,))],
        compiler_params=pltpu.CompilerParams(vmem_limit_bytes=size + (2 << 20)),
        cost_estimate=pl.CostEstimate(flops=0, bytes_accessed=4 * size, transcendentals=0),
    )(dest, *flat)
    return [out.reshape(out.shape[:2] + (-1, width)) for out in outs]


def split_kernel(spans, plane_rows, squares, core_ref, *refs):
    parts, refs = (refs[: len(spans)], refs[len(spans) :])
    keep, send = refs[:2]
    held, in_sem, out_sem = (refs[2:-2], refs[-2], refs[-1])
    core = core_ref[0]
    incoming, count, part, done = ({}, 0, 0, 0)
    for plane, rows in enumerate(plane_rows):
        for slot in range(2 * squares):
            offset, incoming[plane, slot] = (0, [])
            while offset < rows:
                first, length = spans[part]
                size = min(length - done, rows - offset)
                copy = pltpu.make_async_copy(
                    parts[part].at[pl.ds((first + done) // 8, size // 8)],
                    held[plane].at[slot, pl.ds(offset // 8, size // 8)],
                    in_sem.at[count],
                )
                copy.start()
                incoming[plane, slot].append(copy)
                count, offset, done = (count + 1, offset + size, done + size)
                if done == length:
                    part, done = (part + 1, 0)
    outgoing, row = ([], 0)
    for plane, rows in enumerate(plane_rows):
        for square in range(squares):
            for copy in incoming[plane, 2 * square] + incoming[plane, 2 * square + 1]:
                copy.wait()
            for target, side in ((send, 1 - core), (keep, core)):
                copy = pltpu.make_async_copy(
                    held[plane].at[2 * square + side], target.at[square, pl.ds(row // 8, rows // 8)], out_sem.at[len(outgoing)]
                )
                copy.start()
                outgoing.append(copy)
        row += rows
    for copy in outgoing:
        copy.wait()


def split_cores(parts, plane_rows, squares, core):
    spans = tuple((first, length) for _, first, length in parts)
    arrays = [eights(array) for array, _, _ in parts]
    width = arrays[0].shape[-1]
    slots = len(plane_rows) * squares * 2
    size = 2 * squares * sum(plane_rows) * width * 2
    anywhere = pl.BlockSpec(memory_space=pl.ANY)
    half = jax.ShapeDtypeStruct((squares, sum(plane_rows) // 8, 8, width), BF16)
    outs = pl.pallas_call(
        partial(split_kernel, spans, tuple(plane_rows), squares),
        in_specs=[pl.BlockSpec(memory_space=pltpu.SMEM)] + [anywhere] * len(arrays),
        out_specs=[anywhere, anywhere],
        out_shape=[half, half],
        scratch_shapes=[pltpu.VMEM((2 * squares, rows // 8, 8, width), BF16) for rows in plane_rows]
        + [pltpu.SemaphoreType.DMA((slots + len(parts),)), pltpu.SemaphoreType.DMA((slots,))],
        compiler_params=pltpu.CompilerParams(vmem_limit_bytes=size + (2 << 20)),
        cost_estimate=pl.CostEstimate(flops=0, bytes_accessed=size // 8, transcendentals=0),
    )(core, *arrays)
    return [out.reshape(squares, -1, width) for out in outs]


def join_kernel(chunks, *refs):
    parts, (out, held, in_sem, out_sem) = (refs[:-4], refs[-4:])
    moves = []
    for slot, (part, row) in enumerate(chunks):
        size = held.shape[1]
        fetch = pltpu.make_async_copy(parts[part].at[pl.ds(row, size)], held.at[slot], in_sem.at[slot])
        fetch.start()
        moves.append((fetch, pltpu.make_async_copy(held.at[slot], out.at[pl.ds(slot * size, size)], out_sem.at[slot])))
    for fetch, write in moves:
        fetch.wait()
        write.start()
    for _, write in moves:
        write.wait()


def join(parts, rows):
    width = parts[0].shape[1]
    chunks = [(k, row // 8) for k, part in enumerate(parts) for row in range(0, part.shape[0], rows)]
    count = len(chunks)
    anywhere = pl.BlockSpec(memory_space=pl.ANY)
    out = pl.pallas_call(
        partial(join_kernel, tuple(chunks)),
        in_specs=[anywhere] * len(parts),
        out_specs=anywhere,
        out_shape=jax.ShapeDtypeStruct((count * rows // 8, 8, width), BF16),
        scratch_shapes=[
            pltpu.VMEM((count, rows // 8, 8, width), BF16),
            pltpu.SemaphoreType.DMA((count,)),
            pltpu.SemaphoreType.DMA((count,)),
        ],
        compiler_params=pltpu.CompilerParams(vmem_limit_bytes=COPY_VMEM),
        cost_estimate=pl.CostEstimate(flops=0, bytes_accessed=8 * count * rows * width, transcendentals=0),
    )(*[eights(part) for part in parts])
    return out.reshape(-1, width)


def pack_kernel(devices, *refs):
    parts, out_ref, held = (refs[:-2], refs[-2], refs[-1])
    held[...] = jnp.zeros_like(held)
    out_ref[...] = jnp.zeros_like(out_ref)
    row = 0
    for part in parts:
        held[row : row + part.shape[0], :] = part[...]
        row += part.shape[0]
    share = held.shape[1] // devices
    for device in range(devices):
        out_ref[device, :, :share] = held[:, device * share : (device + 1) * share]


def pack(parts, devices):
    rows = -(-sum(part.shape[0] for part in parts) // 8) * 8
    width = parts[0].shape[1]
    return pl.pallas_call(
        partial(pack_kernel, devices),
        out_shape=jax.ShapeDtypeStruct((devices, rows, LANES), F32),
        scratch_shapes=[pltpu.VMEM((rows, width), F32)],
        cost_estimate=pl.CostEstimate(flops=0, bytes_accessed=8 * rows * width, transcendentals=0),
    )(*parts)


def tie(values, others):
    return lax.optimization_barrier((values, others))


class Whole:
    def __init__(self, axes, weights_in, weights_out, packed, width, clip):
        self.axes, self.width, self.clip = (axes, width, clip)
        full_in = lax.all_gather(weights_in, axes, axis=0, tiled=True)
        full_out = lax.all_gather(weights_out, axes, axis=0, tiled=True)
        devices = lax.axis_size(axes)
        slot = lax.dynamic_update_slice(
            jnp.zeros((devices,) + packed.shape, F32), packed.astype(F32)[None], (lax.axis_index(axes), 0, 0)
        )
        self.small = lax.psum(slot, axes).transpose(1, 0, 2).reshape(packed.shape[0], width).astype(BF16)
        self.in_a, self.in_b = (full_in[: 5 * width // 2], full_in[5 * width // 2 : 3 * width])
        self.in_t, self.in_qk = (full_in[: 3 * width], full_in[3 * width : 5 * width])
        self.in_v, self.in_m = (full_in[5 * width : 6 * width], full_in[6 * width :])
        self.out_t, self.out_f = (full_out[:width], full_out[width : 2 * width])
        self.out_s, self.out_m = (full_out[2 * width : 3 * width], full_out[3 * width :])
        self.grads = {}

    def tick(self, name, *values):
        return values[0] if len(values) == 1 else values

    def total(self, sums, arrays, clip):
        g = self.grads
        parts = sums + [column_sum(array) for array in arrays]
        small = jnp.concatenate([part.reshape(-1, self.width) for part in parts], axis=0)
        d_in = jnp.concatenate([g["in_t"], g["in_qk"], g["in_v"], g["in_m"]], axis=0)
        d_out = jnp.concatenate([g["out_t"], g["out_f"], g["out_s"], g["out_m"]], axis=0)
        summed_in = lax.psum_scatter(d_in, self.axes, scatter_dimension=0, tiled=True).astype(F32)
        summed_out = lax.psum_scatter(d_out, self.axes, scatter_dimension=0, tiled=True).astype(F32)
        share = self.width // lax.axis_size(self.axes)
        at = (0, lax.axis_index(self.axes) * share)
        clip = clip.astype(F32)
        return (clip, summed_in, summed_out, lax.dynamic_slice(lax.psum(small, self.axes), at, (small.shape[0], share)))


class Staged:
    def __init__(self, axes, weights_in, weights_out, packed, width, clip):
        self.axes, self.width = (axes, width)
        me = lax.axis_index(axes)
        self.plane, self.spot, self.square, self.core = (me // 8, me % 8, me % 8 // 2, me % 2)
        self.spots = jnp.bitwise_xor(jnp.arange(8, dtype=jnp.int32), self.spot)
        self.planes = (self.plane + 4 - jnp.arange(4, dtype=jnp.int32)) % 4
        self.core_ref = self.core.astype(jnp.int32).reshape(1)
        self.rows_in, self.count = (weights_in.shape[0], packed.shape[0])
        self.grads = {}
        flat = packed.reshape(1, -1)
        tail = jnp.pad(flat, ((0, 7), (0, width - flat.shape[1])))
        pieces = self.shifted(jnp.concatenate([weights_in, tail], axis=0))
        pieces, self.clip = tie(pieces, clip)
        full_out = lax.all_gather(weights_out, axes, axis=0, tiled=True)
        self.out_t, self.out_f = (full_out[:width], full_out[width : 2 * width])
        self.out_s, self.out_m = (full_out[2 * width : 3 * width], full_out[3 * width :])
        self.column_in, self.column_small = self.columns(pieces, (self.rows_in, 8))

    def flip(self, x, bits):
        return lax.ppermute(x, self.axes, [(d, d ^ bits) for d in range(32)])

    def shift(self, x, step):
        return lax.ppermute(x, self.axes, [(d, (d + 8 * step) % 32) for d in range(32)])

    def shifted(self, shard):
        return [shard] + [self.shift(shard, step) for step in (1, 2, 3)]

    def columns(self, pieces, sizes):
        plan, row = ([], 0)
        for size in sizes:
            plan.append([(0, row, size)])
            row += size
        return [out[0] for out in place([pieces], plan, self.planes)]

    def over(self, piece):
        return [piece] + [self.flip(piece, bits) for bits in (2, 4, 6)]

    def cores(self, pieces):
        both = []
        for piece in pieces:
            both += [piece, self.flip(piece, 1)]
        return both

    def lay(self, groups, entries):
        out = place(groups, [entries], self.spots)[0]
        return out.reshape(-1, self.width)

    def begin(self, clip):
        rows_in, width = (self.rows_in, self.width)
        smalls = self.column_small.reshape(-1, width)
        first = jnp.concatenate([self.column_in[0], smalls], axis=0)
        self.p1, self.p23 = (self.column_in[1], self.column_in[2:].reshape(-1, width))
        p0 = self.over(first)
        p0, clip = tie(p0, clip)
        self.p0 = self.cores(p0)
        low, small = place([self.p0], [[(0, 0, rows_in)], [(0, rows_in, 32)]], self.spots)
        low, self.p1 = tie(low, self.p1)
        self.p1 = self.over(self.p1)
        self.in_a = low.reshape(-1, width)
        share = width // 32
        small = small.reshape(8, 4, 8, width)[:, :, 0, : self.count * share].reshape(8, 4, self.count, share)
        self.small = small.transpose(2, 1, 0, 3).reshape(self.count, width)
        return clip

    def tick(self, name, *values):
        single = len(values) == 1
        rows_in, width = (self.rows_in, self.width)
        g = self.grads
        whole = lambda key: (g[key], 0, g[key].shape[0])
        if name == "query_t":
            values, (self.p1, self.p23) = tie(values, (self.p1, self.p23))
            self.p23 = self.over(self.p23)
            self.p1 = self.cores(self.p1)
            low = self.lay([self.p0, self.p1], [(0, 0, rows_in), (1, 0, rows_in)])
            self.in_t, self.in_qk = (low[: 3 * width], low[3 * width :])
            self.in_b = self.in_t[5 * width // 2 :]
        elif name == "query_s":
            values, self.p23 = tie(values, self.p23)
            self.p23 = self.cores(self.p23)
            high = self.lay([self.p23], [(0, 0, rows_in), (0, rows_in, rows_in)])
            self.in_v, self.in_m = (high[:width], high[width:])
        elif name == "hidden":
            values = lax.optimization_barrier(values)
        elif name == "in_m":
            start = 24 * rows_in - 6 * width
            d_in_m = g["in_m"]
            self.kept, send = self.halve([(d_in_m, start, d_in_m.shape[0] - start)], (rows_in,))
            values, send = tie(values, send)
            self.other = self.flip(send, 1)
        elif name == "grad_mixed_s":
            values, (self.kept, self.other) = tie(values, (self.kept, self.other))
            self.d_p3 = self.across(self.kept, self.other)
        elif name == "grad_s":
            values, self.d_p3 = tie(values, self.d_p3)
            self.d_p3 = self.gathered(self.d_p3)
        elif name == "in_v":
            start = 24 * rows_in - 6 * width
            self.kept, send = self.halve([whole("in_v"), (g["in_m"], 0, start)], (rows_in,))
            values, send = tie(values, send)
            self.other = self.flip(send, 1)
        elif name == "in_qk":
            values, (self.kept, self.other) = tie(values, (self.kept, self.other))
            self.d_p2 = self.across(self.kept, self.other)
        elif name == "grad_t":
            values, self.d_p2 = tie(values, self.d_p2)
            self.d_p2 = self.gathered(self.d_p2)
            late = jnp.zeros((8 * rows_in - 2 * width, width), BF16)
            self.kept, send = self.halve([(late, 0, late.shape[0]), whole("in_qk")], (rows_in,))
            values, send = tie(values, send)
            self.other = self.flip(send, 1)
        elif name == "out_t":
            values, (self.kept, self.other) = tie(values, (self.kept, self.other))
            self.d_p1 = self.across(self.kept, self.other)
            d_out = join([g["out_t"], g["out_f"], g["out_s"], g["out_m"]], width // 2)
            values, d_out = tie(values, d_out)
            self.summed_out = lax.psum_scatter(d_out, self.axes, scatter_dimension=0, tiled=True)
        elif name == "grad_project_t":
            values, self.d_p1 = tie(values, self.d_p1)
            self.d_p1 = self.gathered(self.d_p1)
        elif name == "in_t":
            d_in_t = g["in_t"]
            kept, send = self.halve([whole("in_t")], (rows_in, d_in_t.shape[0] // 8 - rows_in))
            values, send = tie(values, send)
            half = lambda a, x: lax.dynamic_slice_in_dim(a, 2 * x, 2, 0).astype(F32)
            other = self.flip(send, 1)
            x = self.square // 2
            send = (half(kept, 1 - x) + half(other, 1 - x)).astype(BF16)
            own = (half(kept, x) + half(other, x)).astype(BF16)
            values, (own, send) = tie(values, (own, send))
            self.last = (own, self.flip(send, 4))
        elif name == "dx_t":
            values, (own, other) = tie(values, self.last)
            y = self.square % 2
            line = lambda a, y: lax.dynamic_index_in_dim(a, y, 0, keepdims=False).astype(F32)
            send = (line(own, 1 - y) + line(other, 1 - y)).astype(BF16)
            own = (line(own, y) + line(other, y)).astype(BF16)
            self.last = (own, self.flip(send, 2))
        elif name == "grad_clip":
            values, last = tie(values, self.last)
            self.d_last = self.gathered(last)
        return values[0] if single else values

    def halve(self, parts, plane_rows):
        return split_cores(parts, plane_rows, 4, self.core_ref)

    def across(self, keep, other):
        result = []
        for bits in (0, 2, 4, 6):
            at = jnp.bitwise_xor(self.square, bits // 2)
            take = lambda a: lax.dynamic_index_in_dim(a, at, 0, keepdims=False).astype(F32)
            summed = (take(keep) + take(other)).astype(BF16)
            result.append(summed if bits == 0 else self.flip(summed, bits))
        return result

    def gathered(self, arrived):
        return self.added(arrived).astype(BF16)

    def towards(self, block, plane):
        pieces = [block]
        for step in (1, 2, 3):
            pairs = [(d, (d + 8 * step) % 32) for d in range(32) if (d // 8 + step) % 4 == plane]
            pieces.append(lax.ppermute(block, self.axes, pairs))
        return pieces

    def added(self, pieces):
        total = pieces[0].astype(F32)
        for piece in pieces[1:]:
            total = total + piece.astype(F32)
        return total

    def total(self, sums, arrays, clip):
        rows, last = (self.rows_in, self.d_last)
        every = jnp.stack([last[:rows], self.d_p1, self.d_p2, self.d_p3], axis=0)
        blocks = [
            lax.dynamic_index_in_dim(every, (self.plane + step) % 4, 0, keepdims=False) for step in range(4)
        ]
        blocks, extra = tie(blocks, last[rows:])
        terms = blocks[:1] + [self.shift(blocks[step], step) for step in (1, 2, 3)]
        beside, arrays = tie(self.flip(extra, 1), arrays)
        extra = self.towards(jnp.concatenate([extra, beside], axis=0), 1)
        extra = self.added(extra).astype(BF16)
        blocks = [extra]
        for bits in (2, 4, 6):
            blocks.append(lax.ppermute(extra, self.axes, [(8 + bits + core, 8 + core) for core in range(2)]))
        extra = jnp.concatenate(blocks, axis=0).reshape(8, -1, self.width)
        swapped = jnp.stack([extra[4], extra[7], extra[6]], axis=0).reshape(-1, self.width)
        swapped = jnp.pad(swapped, ((0, rows - swapped.shape[0]), (0, 0)))
        extra = jnp.where(self.core == 0, extra.reshape(-1, self.width)[:rows], swapped).astype(F32)
        extra = jnp.where((self.plane == 1) & (self.square == 0), extra, 0.0)
        clip, self.summed_out = tie(clip, self.summed_out)
        summed_in = self.added(terms) + extra
        parts = sums + [column_sum(array) for array in arrays]
        parts, clip = tie([part.reshape(-1, self.width) for part in parts], clip)
        small = lax.all_to_all(pack(parts, 32), self.axes, split_axis=0, concat_axis=0)
        small = jnp.sum(small, axis=0)[: self.count, : self.width // 32]
        return (clip.astype(F32), summed_in, self.summed_out.astype(F32), small)


def norm_parts(values):
    centre = values - jnp.mean(values, axis=-1, keepdims=True)
    spread = jnp.mean(centre * centre, axis=-1, keepdims=True)
    scale = lax.rsqrt(spread + EPSILON)
    return (centre * scale, scale)


def layer_norm(values, gains, shifts):
    return (norm_parts(values)[0] * gains + shifts).astype(BF16)


def norm_backward(values, gains, grad, hook=lambda *sums: sums):
    normed, scale = norm_parts(values)
    scaled = grad * gains
    first = jnp.mean(scaled, axis=-1, keepdims=True)
    second = jnp.mean(scaled * normed, axis=-1, keepdims=True)
    sums = (first, second, jnp.sum(grad * normed, axis=0), jnp.sum(grad, axis=0))
    grad, first, second, d_gain, d_shift = hook(grad, *sums)
    inner = (grad * gains - first - normed * second) * scale
    return (inner, d_gain, d_shift)


def gelu_parts(values):
    cdf = 0.5 * (1.0 + lax.erf(values * (0.5**0.5)))
    density = jnp.exp(-0.5 * values * values) * 0.3989422804014327
    return (values * cdf, cdf + values * density)


def column_sum(rows):
    return jnp.sum(rows.astype(F32), axis=0)


def block(clip, target, leave, feed, gain_count, patches):
    shape = clip.shape
    width = shape[-1]
    grid = shape[:3]
    small32 = feed.small.astype(F32)
    gains32, shifts32, dense32 = (small32[:gain_count], small32[gain_count:-1], small32[-1])
    flat = lambda a: a.reshape(-1, a.shape[-1])
    cube = lambda a: a.reshape(grid + (a.shape[-1],))
    grads = feed.grads
    start = clip.reshape(-1, width).astype(F32)
    normed_t = layer_norm(start, gains32[0], shifts32[0])
    project_a = nt(normed_t, feed.in_a).astype(BF16)
    project_a, normed_t = feed.tick("query_t", project_a, normed_t)
    project_b = nt(normed_t, feed.in_b).astype(BF16)
    project_t = [cube(project_a), cube(project_b)]
    mixed_t = attention_call(forward_kernel, 2, project_t, (width,), True, patches)[0]
    mixed_t = flat(feed.tick("mixed_t", mixed_t))
    projected_t = (nn(mixed_t, feed.out_t) + shifts32[3]).astype(BF16)
    branch_t = (nn(projected_t, feed.out_f) + shifts32[4]).astype(BF16)
    after_t = start + branch_t.astype(F32)
    normed_s = layer_norm(after_t, gains32[1], shifts32[1])
    project_qk = nt(normed_s, feed.in_qk).astype(BF16)
    project_qk, normed_s = feed.tick("query_s", project_qk, normed_s)
    project_v = nt(normed_s, feed.in_v).astype(BF16)
    project_s = [cube(project_qk), cube(project_v)]
    mixed_s = attention_call(forward_kernel, 2, project_s, (width,), False, patches)[0]
    mixed_s = flat(feed.tick("mixed_s", mixed_s))
    grad_low = flat(target(mixed_s))
    after_s = after_t + (nn(mixed_s, feed.out_s) + shifts32[5])
    normed_m = layer_norm(after_s, gains32[2], shifts32[2])
    hidden_pre = nt(normed_m, feed.in_m) + shifts32[6:].reshape(-1)
    hidden32, slope32 = gelu_parts(hidden_pre)
    hidden, slope, grad_low = feed.tick("hidden", hidden32.astype(BF16), slope32.astype(BF16), grad_low)
    output = (after_s + (nn(hidden, feed.out_m) + dense32)).astype(BF16)
    output = leave(output.reshape(shape))

    grad_out = grad_low.astype(F32)
    grads["out_m"] = tn(hidden, grad_low).astype(BF16)
    grad_low = feed.tick("out_m", grad_low)
    grad_pre = (nt(grad_low, feed.out_m) * slope.astype(F32)).astype(BF16)
    grad_pre = feed.tick("grad_pre", grad_pre)
    grads["in_m"] = tn(grad_pre, normed_m).astype(BF16)
    grad_pre = feed.tick("in_m", grad_pre)
    part, g_m, b_m = norm_backward(after_s, gains32[2], nn(grad_pre, feed.in_m))
    grad_s = grad_out + part
    grad_branch_s = grad_s.astype(BF16)
    grads["out_s"] = tn(mixed_s, grad_branch_s).astype(BF16)
    grad_mixed_s = nt(grad_branch_s, feed.out_s).astype(BF16)
    grad_mixed_s, output = feed.tick("grad_mixed_s", grad_mixed_s, output)
    grad_qk, grad_v = attention_call(
        backward_kernel, 2, project_s + [cube(grad_mixed_s)], (2 * width, width), False, patches
    )
    grad_qk, grad_v = feed.tick("grad_s", flat(grad_qk), flat(grad_v))
    grads["in_v"] = tn(grad_v, normed_s).astype(BF16)
    grad_qk, grad_v = feed.tick("in_v", grad_qk, grad_v)
    d_in_qk = tn(grad_qk, normed_s).astype(BF16)
    grads["in_qk"], grad_qk, grad_v = feed.tick("in_qk", d_in_qk, grad_qk, grad_v)
    part, g_s, b_s = norm_backward(after_t, gains32[1], nn(grad_qk, feed.in_qk) + nn(grad_v, feed.in_v))
    grad_t = grad_s + part
    grad_branch_t = feed.tick("grad_t", grad_t.astype(BF16))
    grads["out_f"] = tn(projected_t, grad_branch_t).astype(BF16)
    grad_projected = nt(grad_branch_t, feed.out_f).astype(BF16)
    grads["out_t"] = tn(mixed_t, grad_projected).astype(BF16)
    grad_projected = feed.tick("out_t", grad_projected)
    grad_mixed_t = feed.tick("grad_mixed_t", nt(grad_projected, feed.out_t).astype(BF16))
    grad_project_t = attention_call(
        backward_kernel, 2, project_t + [cube(grad_mixed_t)], (3 * width,), True, patches
    )[0]
    grad_project_t = feed.tick("grad_project_t", flat(grad_project_t))
    grads["in_t"] = tn(grad_project_t, normed_t).astype(BF16)
    grad_project_t = feed.tick("in_t", grad_project_t)
    hook = lambda *sums: feed.tick("dx_t", *sums)
    part, g_t, b_t = norm_backward(start, gains32[0], nn(grad_project_t, feed.in_t), hook)
    grad_clip = (grad_t + part.astype(BF16).astype(F32)).astype(BF16)
    rows = (grad_projected, grad_branch_t, grad_branch_s, grad_pre, grad_low)
    grad_clip, *rows = feed.tick("grad_clip", grad_clip, *rows)
    sums = [g_t, g_s, g_m, b_t, b_s, b_m]
    return (output,) + feed.total(sums, rows, leave(grad_clip.reshape(shape)))


def shards(clips_in, cotangent, clip_live, weights_in, weights_out, norm_gain, shift_rows, dense_shift):
    both = ("dp", "seq")
    group = lax.axis_size("seq")
    count, _, patches, width = clips_in.shape
    own = count // group
    rows = -(-patches // SUB) * SUB
    gain_count = norm_gain.shape[0]
    shift_count = shift_rows.shape[0]
    staged = lax.axis_size(both) == 32 and group == 4 and weights_in.shape[0] == 240 and weights_out.shape[0] == 168

    def exchange(x):
        return lax.all_to_all(x, "seq", split_axis=0, concat_axis=1, tiled=True)

    def widen(x):
        return jnp.pad(x, ((0, 0), (0, 0), (0, rows - patches), (0, 0)))

    def leave(x):
        x = x[:, :, :patches]
        return lax.all_to_all(x, "seq", split_axis=1, concat_axis=0, tiled=True)

    packed = jnp.concatenate([norm_gain, shift_rows, dense_shift[None, :]], axis=0)
    feed = (Staged if staged else Whole)(both, weights_in, weights_out, packed, width, exchange(clips_in))
    clip = widen(feed.clip)
    if staged:
        clip = feed.begin(clip)
    live = lax.dynamic_slice(clip_live, (lax.axis_index("seq") * own,), (own,)).astype(BF16)

    def target(after):
        gradient = cotangent * 1
        if staged:
            gradient = tie(gradient, after)[0]
        return widen(exchange(gradient)) * live[:, None, None, None]

    output, grad_clip, summed_in, summed_out, owned = block(clip, target, leave, feed, gain_count, patches)
    return (
        output,
        grad_clip,
        summed_in,
        summed_out,
        owned[:gain_count],
        owned[gain_count : gain_count + shift_count],
        owned[-1],
    )


def solution(mesh):
    clip = P("dp", "seq", None, None)
    row = P(("dp", "seq"), None)
    col = P(None, ("dp", "seq"))
    flat = P(("dp", "seq"))
    return jax.shard_map(
        shards,
        mesh=mesh,
        in_specs=(clip, clip, P("dp"), row, row, col, col, flat),
        out_specs=(clip, clip, row, row, col, col, flat),
        check_vma=False,
    )
```

```python
from functools import partial

import jax
import jax.numpy as jnp
from jax import lax
from jax.experimental import pallas as pl
from jax.experimental.pallas import tpu as pltpu
from jax.sharding import PartitionSpec as P

HEADS = 12
HEAD_DIM = 64
EPSILON = 1e-06
PAIRS = HEADS // 2
LANES = 2 * HEAD_DIM
SUB = 16
NEG = -1e30
COPY_VMEM = 60 << 20
F32 = jnp.float32
BF16 = jnp.bfloat16


def nt(left, right):
    return lax.dot_general(left, right, (((1,), (1,)), ((), ())), preferred_element_type=F32)


def nn(left, right):
    return lax.dot_general(left, right, (((1,), (0,)), ((), ())), preferred_element_type=F32)


def tn(left, right):
    return lax.dot_general(left, right, (((0,), (0,)), ((), ())), preferred_element_type=F32)


def split_heads(pair):
    first = lax.broadcasted_iota(jnp.int32, pair.shape, 1) < HEAD_DIM
    zero = jnp.zeros_like(pair)
    return jnp.concatenate([jnp.where(first, pair, zero), jnp.where(first, zero, pair)], axis=0)


def join_heads(stacked):
    rows = stacked.shape[0] // 2
    first = lax.broadcasted_iota(jnp.int32, (rows, LANES), 1) < HEAD_DIM
    return jnp.where(first, stacked[:rows], stacked[rows:])


def pair_forward(queries, keys, values, keep):
    stacked = split_heads(queries * jnp.asarray(HEAD_DIM**-0.5, BF16))
    scores = jnp.where(keep, nt(keys, stacked), NEG)
    top = jnp.max(scores, axis=0, keepdims=True)
    weights = jnp.exp(scores - top)
    total = jnp.sum(weights, axis=0, keepdims=True)
    probs = (weights * (1.0 / total)).astype(BF16)
    return join_heads(tn(probs, values)).astype(BF16)


def pair_backward(queries, keys, values, grad, keep):
    scaling = HEAD_DIM**-0.5
    stacked = split_heads(queries * jnp.asarray(scaling, BF16))
    grads = split_heads(grad)
    scores = jnp.where(keep, nt(keys, stacked), NEG)
    top = jnp.max(scores, axis=0, keepdims=True)
    weights = jnp.exp(scores - top)
    total = jnp.sum(weights, axis=0, keepdims=True)
    probs = weights * (1.0 / total)
    grad_probs = nt(values, grads)
    mean = jnp.sum(probs * grad_probs, axis=0, keepdims=True)
    grad_scores = (probs * (grad_probs - mean)).astype(BF16)
    grad_values = nn(probs.astype(BF16), grads)
    grad_keys = nn(grad_scores, stacked)
    grad_queries = join_heads(tn(grad_scores, keys)) * scaling
    return (grad_queries.astype(BF16), grad_keys.astype(BF16), grad_values.astype(BF16))


def columns(kind, pair):
    start = (kind * PAIRS + pair) * LANES
    return slice(start, start + LANES)


def find(refs, kind, pair):
    cols = columns(kind, pair)
    for ref in refs:
        size = ref.shape[-1]
        if cols.start < size:
            return (ref, cols)
        cols = slice(cols.start - size, cols.stop - size)


def load(refs, kind, pair):
    ref, cols = find(refs, kind, pair)
    return ref[..., cols].reshape(-1, LANES)


def store(refs, kind, pair, block):
    ref, cols = find(refs, kind, pair)
    ref[..., cols] = block.reshape(ref.shape[:-1] + (LANES,))


def keep_mask(shape, key_axis, group, patches):
    key = lax.broadcasted_iota(jnp.int32, shape, key_axis)
    if group is None:
        return key < patches
    query = lax.broadcasted_iota(jnp.int32, shape, 1 - key_axis)
    return (key % group) == (query % group)


def forward_kernel(group, patches, count, *refs):
    project, mixed = (refs[:count], refs[count:])
    rows = project[0].size // project[0].shape[-1]
    keep = keep_mask((rows, 2 * rows), 0, group, patches)
    for pair in range(PAIRS):
        block = pair_forward(*[load(project, kind, pair) for kind in range(3)], keep)
        store(mixed, 0, pair, block)


def backward_kernel(group, patches, count, *refs):
    project, grad, outs = (refs[:count], refs[count : count + 1], refs[count + 1 :])
    rows = project[0].size // project[0].shape[-1]
    keep = keep_mask((rows, 2 * rows), 0, group, patches)
    for pair in range(PAIRS):
        results = pair_backward(*[load(project, kind, pair) for kind in range(3)], load(grad, 0, pair), keep)
        for kind, result in enumerate(results):
            store(outs, kind, pair, result)


def attention_call(kernel, count, arrays, out_cols, temporal, patches):
    clips, frames, rows, _ = arrays[0].shape
    if temporal:
        group, steps, shape = SUB, rows // SUB, (1, frames, SUB)
        index = lambda c, i: (c, 0, i, 0)
    else:
        group, steps, shape = None, frames, (1, 1, rows)
        index = lambda c, i: (c, i, 0, 0)
    tokens = clips * frames * rows
    backward = kernel is backward_kernel
    return pl.pallas_call(
        partial(kernel, group, patches, count),
        grid=(clips, steps),
        in_specs=[pl.BlockSpec(shape + (a.shape[-1],), index) for a in arrays],
        out_specs=[pl.BlockSpec(shape + (cols,), index) for cols in out_cols],
        out_shape=[jax.ShapeDtypeStruct((clips, frames, rows, cols), BF16) for cols in out_cols],
        compiler_params=pltpu.CompilerParams(dimension_semantics=("arbitrary", "arbitrary")),
        cost_estimate=pl.CostEstimate(
            flops=tokens * (14_000_000 if backward else 9_000_000), bytes_accessed=0, transcendentals=0
        ),
    )(*arrays)


def eights(rows):
    return rows.reshape(rows.shape[:-2] + (-1, 8, rows.shape[-1]))


def place_kernel(outs_plan, blocks, groups, dest_ref, *refs):
    pieces, refs = (refs[: groups * blocks], refs[groups * blocks :])
    outs, refs = (refs[: len(outs_plan)], refs[len(outs_plan) :])
    held, in_sem, out_sem = (refs[:-2], refs[-2], refs[-1])
    moves, slot = ([], 0)
    for target, entries in enumerate(outs_plan):
        for entry, (group, row, rows) in enumerate(entries):
            for block in range(blocks):
                buffer = held[target].at[entry, block]
                source = pieces[group * blocks + block].at[pl.ds(row // 8, rows // 8)]
                fetch = pltpu.make_async_copy(source, buffer, in_sem.at[slot])
                fetch.start()
                write = pltpu.make_async_copy(buffer, outs[target].at[entry, dest_ref[block]], out_sem.at[slot])
                moves.append((fetch, write))
                slot += 1
    for fetch, write in moves:
        fetch.wait()
        write.start()
    for _, write in moves:
        write.wait()


def place(groups, outs_plan, dest):
    blocks = len(groups[0])
    width = groups[0][0].shape[1]
    shapes = [(len(entries), blocks, entries[0][2] // 8, 8, width) for entries in outs_plan]
    slots = sum(len(entries) for entries in outs_plan) * blocks
    size = sum(16 * s[0] * s[1] * s[2] * s[4] for s in shapes)
    flat = [eights(piece) for group in groups for piece in group]
    anywhere = pl.BlockSpec(memory_space=pl.ANY)
    outs = pl.pallas_call(
        partial(place_kernel, tuple(tuple(e) for e in outs_plan), blocks, len(groups)),
        in_specs=[pl.BlockSpec(memory_space=pltpu.SMEM)] + [anywhere] * len(flat),
        out_specs=[anywhere] * len(shapes),
        out_shape=[jax.ShapeDtypeStruct(s, BF16) for s in shapes],
        scratch_shapes=[pltpu.VMEM(s, BF16) for s in shapes]
        + [pltpu.SemaphoreType.DMA((slots,)), pltpu.SemaphoreType.DMA((slots,))],
        compiler_params=pltpu.CompilerParams(vmem_limit_bytes=size + (2 << 20)),
        cost_estimate=pl.CostEstimate(flops=0, bytes_accessed=4 * size, transcendentals=0),
    )(dest, *flat)
    return [out.reshape(out.shape[:2] + (-1, width)) for out in outs]


def split_kernel(spans, plane_rows, squares, core_ref, *refs):
    parts, refs = (refs[: len(spans)], refs[len(spans) :])
    keep, send = refs[:2]
    held, in_sem, out_sem = (refs[2:-2], refs[-2], refs[-1])
    core = core_ref[0]
    incoming, count, part, done = ({}, 0, 0, 0)
    for plane, rows in enumerate(plane_rows):
        for slot in range(2 * squares):
            offset, incoming[plane, slot] = (0, [])
            while offset < rows:
                first, length = spans[part]
                size = min(length - done, rows - offset)
                copy = pltpu.make_async_copy(
                    parts[part].at[pl.ds((first + done) // 8, size // 8)],
                    held[plane].at[slot, pl.ds(offset // 8, size // 8)],
                    in_sem.at[count],
                )
                copy.start()
                incoming[plane, slot].append(copy)
                count, offset, done = (count + 1, offset + size, done + size)
                if done == length:
                    part, done = (part + 1, 0)
    outgoing, row = ([], 0)
    for plane, rows in enumerate(plane_rows):
        for square in range(squares):
            for copy in incoming[plane, 2 * square] + incoming[plane, 2 * square + 1]:
                copy.wait()
            for target, side in ((send, 1 - core), (keep, core)):
                copy = pltpu.make_async_copy(
                    held[plane].at[2 * square + side], target.at[square, pl.ds(row // 8, rows // 8)], out_sem.at[len(outgoing)]
                )
                copy.start()
                outgoing.append(copy)
        row += rows
    for copy in outgoing:
        copy.wait()


def split_cores(parts, plane_rows, squares, core):
    spans = tuple((first, length) for _, first, length in parts)
    arrays = [eights(array) for array, _, _ in parts]
    width = arrays[0].shape[-1]
    slots = len(plane_rows) * squares * 2
    size = 2 * squares * sum(plane_rows) * width * 2
    anywhere = pl.BlockSpec(memory_space=pl.ANY)
    half = jax.ShapeDtypeStruct((squares, sum(plane_rows) // 8, 8, width), BF16)
    outs = pl.pallas_call(
        partial(split_kernel, spans, tuple(plane_rows), squares),
        in_specs=[pl.BlockSpec(memory_space=pltpu.SMEM)] + [anywhere] * len(arrays),
        out_specs=[anywhere, anywhere],
        out_shape=[half, half],
        scratch_shapes=[pltpu.VMEM((2 * squares, rows // 8, 8, width), BF16) for rows in plane_rows]
        + [pltpu.SemaphoreType.DMA((slots + len(parts),)), pltpu.SemaphoreType.DMA((slots,))],
        compiler_params=pltpu.CompilerParams(vmem_limit_bytes=size + (2 << 20)),
        cost_estimate=pl.CostEstimate(flops=0, bytes_accessed=size // 8, transcendentals=0),
    )(core, *arrays)
    return [out.reshape(squares, -1, width) for out in outs]


def join_kernel(chunks, *refs):
    parts, (out, held, in_sem, out_sem) = (refs[:-4], refs[-4:])
    moves = []
    for slot, (part, row) in enumerate(chunks):
        size = held.shape[1]
        fetch = pltpu.make_async_copy(parts[part].at[pl.ds(row, size)], held.at[slot], in_sem.at[slot])
        fetch.start()
        moves.append((fetch, pltpu.make_async_copy(held.at[slot], out.at[pl.ds(slot * size, size)], out_sem.at[slot])))
    for fetch, write in moves:
        fetch.wait()
        write.start()
    for _, write in moves:
        write.wait()


def join(parts, rows):
    width = parts[0].shape[1]
    chunks = [(k, row // 8) for k, part in enumerate(parts) for row in range(0, part.shape[0], rows)]
    count = len(chunks)
    anywhere = pl.BlockSpec(memory_space=pl.ANY)
    out = pl.pallas_call(
        partial(join_kernel, tuple(chunks)),
        in_specs=[anywhere] * len(parts),
        out_specs=anywhere,
        out_shape=jax.ShapeDtypeStruct((count * rows // 8, 8, width), BF16),
        scratch_shapes=[
            pltpu.VMEM((count, rows // 8, 8, width), BF16),
            pltpu.SemaphoreType.DMA((count,)),
            pltpu.SemaphoreType.DMA((count,)),
        ],
        compiler_params=pltpu.CompilerParams(vmem_limit_bytes=COPY_VMEM),
        cost_estimate=pl.CostEstimate(flops=0, bytes_accessed=8 * count * rows * width, transcendentals=0),
    )(*[eights(part) for part in parts])
    return out.reshape(-1, width)


def pack_kernel(devices, *refs):
    parts, out_ref, held = (refs[:-2], refs[-2], refs[-1])
    held[...] = jnp.zeros_like(held)
    out_ref[...] = jnp.zeros_like(out_ref)
    row = 0
    for part in parts:
        held[row : row + part.shape[0], :] = part[...]
        row += part.shape[0]
    share = held.shape[1] // devices
    for device in range(devices):
        out_ref[device, :, :share] = held[:, device * share : (device + 1) * share]


def pack(parts, devices):
    rows = -(-sum(part.shape[0] for part in parts) // 8) * 8
    width = parts[0].shape[1]
    return pl.pallas_call(
        partial(pack_kernel, devices),
        out_shape=jax.ShapeDtypeStruct((devices, rows, LANES), F32),
        scratch_shapes=[pltpu.VMEM((rows, width), F32)],
        cost_estimate=pl.CostEstimate(flops=0, bytes_accessed=8 * rows * width, transcendentals=0),
    )(*parts)


def tie(values, others):
    return lax.optimization_barrier((values, others))


class Whole:
    def __init__(self, axes, weights_in, weights_out, packed, width, clip):
        self.axes, self.width, self.clip = (axes, width, clip)
        full_in = lax.all_gather(weights_in, axes, axis=0, tiled=True)
        full_out = lax.all_gather(weights_out, axes, axis=0, tiled=True)
        devices = lax.axis_size(axes)
        slot = lax.dynamic_update_slice(
            jnp.zeros((devices,) + packed.shape, F32), packed.astype(F32)[None], (lax.axis_index(axes), 0, 0)
        )
        self.small = lax.psum(slot, axes).transpose(1, 0, 2).reshape(packed.shape[0], width).astype(BF16)
        self.in_a, self.in_b = (full_in[: 5 * width // 2], full_in[5 * width // 2 : 3 * width])
        self.in_t, self.in_qk = (full_in[: 3 * width], full_in[3 * width : 5 * width])
        self.in_v, self.in_m = (full_in[5 * width : 6 * width], full_in[6 * width :])
        self.out_t, self.out_f = (full_out[:width], full_out[width : 2 * width])
        self.out_s, self.out_m = (full_out[2 * width : 3 * width], full_out[3 * width :])
        self.grads = {}

    def tick(self, name, *values):
        return values[0] if len(values) == 1 else values

    def total(self, sums, arrays, clip):
        g = self.grads
        parts = sums + [column_sum(array) for array in arrays]
        small = jnp.concatenate([part.reshape(-1, self.width) for part in parts], axis=0)
        d_in = jnp.concatenate([g["in_t"], g["in_qk"], g["in_v"], g["in_m"]], axis=0)
        d_out = jnp.concatenate([g["out_t"], g["out_f"], g["out_s"], g["out_m"]], axis=0)
        summed_in = lax.psum_scatter(d_in, self.axes, scatter_dimension=0, tiled=True).astype(F32)
        summed_out = lax.psum_scatter(d_out, self.axes, scatter_dimension=0, tiled=True).astype(F32)
        share = self.width // lax.axis_size(self.axes)
        at = (0, lax.axis_index(self.axes) * share)
        clip = clip.astype(F32)
        return (clip, summed_in, summed_out, lax.dynamic_slice(lax.psum(small, self.axes), at, (small.shape[0], share)))


class Staged:
    def __init__(self, axes, weights_in, weights_out, packed, width, clip):
        self.axes, self.width = (axes, width)
        me = lax.axis_index(axes)
        self.plane, self.spot, self.square, self.core = (me // 8, me % 8, me % 8 // 2, me % 2)
        self.spots = jnp.bitwise_xor(jnp.arange(8, dtype=jnp.int32), self.spot)
        self.planes = (self.plane + 4 - jnp.arange(4, dtype=jnp.int32)) % 4
        self.core_ref = self.core.astype(jnp.int32).reshape(1)
        self.rows_in, self.count = (weights_in.shape[0], packed.shape[0])
        self.grads = {}
        flat = packed.reshape(1, -1)
        tail = jnp.pad(flat, ((0, 7), (0, width - flat.shape[1])))
        pieces = self.shifted(jnp.concatenate([weights_in, tail], axis=0))
        pieces, self.clip = tie(pieces, clip)
        full_out = lax.all_gather(weights_out, axes, axis=0, tiled=True)
        self.out_t, self.out_f = (full_out[:width], full_out[width : 2 * width])
        self.out_s, self.out_m = (full_out[2 * width : 3 * width], full_out[3 * width :])
        self.column_in, self.column_small = self.columns(pieces, (self.rows_in, 8))

    def flip(self, x, bits):
        return lax.ppermute(x, self.axes, [(d, d ^ bits) for d in range(32)])

    def shift(self, x, step):
        return lax.ppermute(x, self.axes, [(d, (d + 8 * step) % 32) for d in range(32)])

    def shifted(self, shard):
        return [shard] + [self.shift(shard, step) for step in (1, 2, 3)]

    def columns(self, pieces, sizes):
        plan, row = ([], 0)
        for size in sizes:
            plan.append([(0, row, size)])
            row += size
        return [out[0] for out in place([pieces], plan, self.planes)]

    def over(self, piece):
        return [piece] + [self.flip(piece, bits) for bits in (2, 4, 6)]

    def cores(self, pieces):
        both = []
        for piece in pieces:
            both += [piece, self.flip(piece, 1)]
        return both

    def lay(self, groups, entries):
        out = place(groups, [entries], self.spots)[0]
        return out.reshape(-1, self.width)

    def begin(self, clip):
        rows_in, width = (self.rows_in, self.width)
        smalls = self.column_small.reshape(-1, width)
        first = jnp.concatenate([self.column_in[0], smalls], axis=0)
        self.p1, self.p23 = (self.column_in[1], self.column_in[2:].reshape(-1, width))
        p0 = self.over(first)
        p0, clip = tie(p0, clip)
        self.p0 = self.cores(p0)
        low, small = place([self.p0], [[(0, 0, rows_in)], [(0, rows_in, 32)]], self.spots)
        low, self.p1 = tie(low, self.p1)
        self.p1 = self.over(self.p1)
        self.in_a = low.reshape(-1, width)
        share = width // 32
        small = small.reshape(8, 4, 8, width)[:, :, 0, : self.count * share].reshape(8, 4, self.count, share)
        self.small = small.transpose(2, 1, 0, 3).reshape(self.count, width)
        return clip

    def tick(self, name, *values):
        single = len(values) == 1
        rows_in, width = (self.rows_in, self.width)
        g = self.grads
        whole = lambda key: (g[key], 0, g[key].shape[0])
        if name == "query_t":
            values, (self.p1, self.p23) = tie(values, (self.p1, self.p23))
            self.p23 = self.over(self.p23)
            self.p1 = self.cores(self.p1)
            low = self.lay([self.p0, self.p1], [(0, 0, rows_in), (1, 0, rows_in)])
            self.in_t, self.in_qk = (low[: 3 * width], low[3 * width :])
            self.in_b = self.in_t[5 * width // 2 :]
        elif name == "query_s":
            values, self.p23 = tie(values, self.p23)
            self.p23 = self.cores(self.p23)
            high = self.lay([self.p23], [(0, 0, rows_in), (0, rows_in, rows_in)])
            self.in_v, self.in_m = (high[:width], high[width:])
        elif name in ("hidden", "end"):
            values = lax.optimization_barrier(values)
        elif name == "in_m":
            start = 24 * rows_in - 6 * width
            d_in_m = g["in_m"]
            self.kept, send = self.halve([(d_in_m, start, d_in_m.shape[0] - start)], (rows_in,))
            values, send = tie(values, send)
            self.other = self.flip(send, 1)
        elif name == "grad_mixed_s":
            values, (self.kept, self.other) = tie(values, (self.kept, self.other))
            self.d_p3 = self.across(self.kept, self.other)
        elif name == "grad_s":
            values, self.d_p3 = tie(values, self.d_p3)
            self.d_p3 = self.gathered(self.d_p3)
        elif name == "in_v":
            start = 24 * rows_in - 6 * width
            self.kept, send = self.halve([whole("in_v"), (g["in_m"], 0, start)], (rows_in,))
            values, send = tie(values, send)
            self.other = self.flip(send, 1)
        elif name == "in_qk":
            values, (self.kept, self.other) = tie(values, (self.kept, self.other))
            self.d_p2 = self.across(self.kept, self.other)
        elif name == "grad_t":
            late = jnp.zeros((8 * rows_in - 2 * width, width), BF16)
            self.kept, send = self.halve([(late, 0, late.shape[0]), whole("in_qk")], (rows_in,))
            values, send = tie(values, send)
            self.other = self.flip(send, 1)
        elif name == "out_t":
            values, self.d_p2 = tie(values, self.d_p2)
            self.d_p2 = self.gathered(self.d_p2)
            values, (self.kept, self.other) = tie(values, (self.kept, self.other))
            self.d_p1 = self.across(self.kept, self.other)
            d_out = join([g["out_t"], g["out_f"], g["out_s"], g["out_m"]], width // 2)
            values, d_out = tie(values, d_out)
            self.summed_out = lax.psum_scatter(d_out, self.axes, scatter_dimension=0, tiled=True)
        elif name == "grad_project_t":
            values, self.d_p1 = tie(values, self.d_p1)
            self.d_p1 = self.gathered(self.d_p1)
        elif name == "in_t":
            d_in_t = g["in_t"]
            kept, send = self.halve([whole("in_t")], (rows_in, d_in_t.shape[0] // 8 - rows_in))
            values, send = tie(values, send)
            half = lambda a, x: lax.dynamic_slice_in_dim(a, 2 * x, 2, 0).astype(F32)
            other = self.flip(send, 1)
            x = self.square // 2
            send = (half(kept, 1 - x) + half(other, 1 - x)).astype(BF16)
            own = (half(kept, x) + half(other, x)).astype(BF16)
            values, (own, send) = tie(values, (own, send))
            self.last = (own, self.flip(send, 4))
        elif name == "dx_t":
            values, (own, other) = tie(values, self.last)
            y = self.square % 2
            line = lambda a, y: lax.dynamic_index_in_dim(a, y, 0, keepdims=False).astype(F32)
            send = (line(own, 1 - y) + line(other, 1 - y)).astype(BF16)
            own = (line(own, y) + line(other, y)).astype(BF16)
            self.last = (own, self.flip(send, 2))
        elif name == "grad_clip":
            values, last = tie(values, self.last)
            self.d_last = self.gathered(last)
        return values[0] if single else values

    def halve(self, parts, plane_rows):
        return split_cores(parts, plane_rows, 4, self.core_ref)

    def across(self, keep, other):
        result = []
        for bits in (0, 2, 4, 6):
            at = jnp.bitwise_xor(self.square, bits // 2)
            take = lambda a: lax.dynamic_index_in_dim(a, at, 0, keepdims=False).astype(F32)
            summed = (take(keep) + take(other)).astype(BF16)
            result.append(summed if bits == 0 else self.flip(summed, bits))
        return result

    def gathered(self, arrived):
        return self.added(arrived).astype(BF16)

    def towards(self, block, plane):
        pieces = [block]
        for step in (1, 2, 3):
            pairs = [(d, (d + 8 * step) % 32) for d in range(32) if (d // 8 + step) % 4 == plane]
            pieces.append(lax.ppermute(block, self.axes, pairs))
        return pieces

    def added(self, pieces):
        total = pieces[0].astype(F32)
        for piece in pieces[1:]:
            total = total + piece.astype(F32)
        return total

    def total(self, sums, arrays, clip):
        rows, last = (self.rows_in, self.d_last)
        every = jnp.stack([last[:rows], self.d_p1, self.d_p2, self.d_p3], axis=0)
        blocks = [
            lax.dynamic_index_in_dim(every, (self.plane + step) % 4, 0, keepdims=False) for step in range(4)
        ]
        blocks, extra = tie(blocks, last[rows:])
        terms = blocks[:1] + [self.shift(blocks[step], step) for step in (1, 2, 3)]
        beside, arrays = tie(self.flip(extra, 1), arrays)
        extra = self.towards(jnp.concatenate([extra, beside], axis=0), 1)
        extra = self.added(extra).astype(BF16)
        blocks = [extra]
        for bits in (2, 4, 6):
            blocks.append(lax.ppermute(extra, self.axes, [(8 + bits + core, 8 + core) for core in range(2)]))
        extra = jnp.concatenate(blocks, axis=0).reshape(8, -1, self.width)
        swapped = jnp.stack([extra[4], extra[7], extra[6]], axis=0).reshape(-1, self.width)
        swapped = jnp.pad(swapped, ((0, rows - swapped.shape[0]), (0, 0)))
        extra = jnp.where(self.core == 0, extra.reshape(-1, self.width)[:rows], swapped).astype(F32)
        extra = jnp.where((self.plane == 1) & (self.square == 0), extra, 0.0)
        clip, self.summed_out = tie(clip, self.summed_out)
        summed_in = self.added(terms) + extra
        parts = sums + [column_sum(array) for array in arrays]
        parts, clip = tie([part.reshape(-1, self.width) for part in parts], clip)
        small = lax.all_to_all(pack(parts, 32), self.axes, split_axis=0, concat_axis=0)
        small = jnp.sum(small, axis=0)[: self.count, : self.width // 32]
        return (clip.astype(F32), summed_in, self.summed_out.astype(F32), small)


def norm_parts(values):
    centre = values - jnp.mean(values, axis=-1, keepdims=True)
    spread = jnp.mean(centre * centre, axis=-1, keepdims=True)
    scale = lax.rsqrt(spread + EPSILON)
    return (centre * scale, scale)


def layer_norm(values, gains, shifts):
    return (norm_parts(values)[0] * gains + shifts).astype(BF16)


def norm_backward(values, gains, grad, hook=lambda *sums: sums):
    normed, scale = norm_parts(values)
    scaled = grad * gains
    first = jnp.mean(scaled, axis=-1, keepdims=True)
    second = jnp.mean(scaled * normed, axis=-1, keepdims=True)
    sums = (first, second, jnp.sum(grad * normed, axis=0), jnp.sum(grad, axis=0))
    grad, first, second, d_gain, d_shift = hook(grad, *sums)
    inner = (grad * gains - first - normed * second) * scale
    return (inner, d_gain, d_shift)


def gelu_parts(values):
    cdf = 0.5 * (1.0 + lax.erf(values * (0.5**0.5)))
    density = jnp.exp(-0.5 * values * values) * 0.3989422804014327
    return (values * cdf, cdf + values * density)


def column_sum(rows):
    return jnp.sum(rows.astype(F32), axis=0)


def block(clip, target, leave, feed, gain_count, patches):
    shape = clip.shape
    width = shape[-1]
    grid = shape[:3]
    small32 = feed.small.astype(F32)
    gains32, shifts32, dense32 = (small32[:gain_count], small32[gain_count:-1], small32[-1])
    flat = lambda a: a.reshape(-1, a.shape[-1])
    cube = lambda a: a.reshape(grid + (a.shape[-1],))
    grads = feed.grads
    start = clip.reshape(-1, width).astype(F32)
    normed_t = layer_norm(start, gains32[0], shifts32[0])
    project_a = nt(normed_t, feed.in_a).astype(BF16)
    project_a, normed_t = feed.tick("query_t", project_a, normed_t)
    project_b = nt(normed_t, feed.in_b).astype(BF16)
    project_t = [cube(project_a), cube(project_b)]
    mixed_t = attention_call(forward_kernel, 2, project_t, (width,), True, patches)[0]
    mixed_t = flat(feed.tick("mixed_t", mixed_t))
    projected_t = (nn(mixed_t, feed.out_t) + shifts32[3]).astype(BF16)
    branch_t = (nn(projected_t, feed.out_f) + shifts32[4]).astype(BF16)
    after_t = start + branch_t.astype(F32)
    normed_s = layer_norm(after_t, gains32[1], shifts32[1])
    project_qk = nt(normed_s, feed.in_qk).astype(BF16)
    project_qk, normed_s = feed.tick("query_s", project_qk, normed_s)
    project_v = nt(normed_s, feed.in_v).astype(BF16)
    project_s = [cube(project_qk), cube(project_v)]
    mixed_s = attention_call(forward_kernel, 2, project_s, (width,), False, patches)[0]
    mixed_s = flat(feed.tick("mixed_s", mixed_s))
    grad_low = flat(target(mixed_s))
    after_s = after_t + (nn(mixed_s, feed.out_s) + shifts32[5])
    normed_m = layer_norm(after_s, gains32[2], shifts32[2])
    hidden_pre = nt(normed_m, feed.in_m) + shifts32[6:].reshape(-1)
    hidden32, slope32 = gelu_parts(hidden_pre)
    hidden, slope, grad_low = feed.tick("hidden", hidden32.astype(BF16), slope32.astype(BF16), grad_low)
    output = (after_s + (nn(hidden, feed.out_m) + dense32)).astype(BF16)
    output = leave(output.reshape(shape))

    grad_out = grad_low.astype(F32)
    grads["out_m"] = tn(hidden, grad_low).astype(BF16)
    grad_low = feed.tick("out_m", grad_low)
    grad_pre = (nt(grad_low, feed.out_m) * slope.astype(F32)).astype(BF16)
    grad_pre = feed.tick("grad_pre", grad_pre)
    grads["in_m"] = tn(grad_pre, normed_m).astype(BF16)
    grad_pre = feed.tick("in_m", grad_pre)
    part, g_m, b_m = norm_backward(after_s, gains32[2], nn(grad_pre, feed.in_m))
    grad_s = grad_out + part
    grad_branch_s = grad_s.astype(BF16)
    grads["out_s"] = tn(mixed_s, grad_branch_s).astype(BF16)
    grad_mixed_s = nt(grad_branch_s, feed.out_s).astype(BF16)
    grad_mixed_s, output = feed.tick("grad_mixed_s", grad_mixed_s, output)
    grad_qk, grad_v = attention_call(
        backward_kernel, 2, project_s + [cube(grad_mixed_s)], (2 * width, width), False, patches
    )
    grad_qk, grad_v = feed.tick("grad_s", flat(grad_qk), flat(grad_v))
    grads["in_v"] = tn(grad_v, normed_s).astype(BF16)
    grad_qk, grad_v = feed.tick("in_v", grad_qk, grad_v)
    d_in_qk = tn(grad_qk, normed_s).astype(BF16)
    grads["in_qk"], grad_qk, grad_v = feed.tick("in_qk", d_in_qk, grad_qk, grad_v)
    part, g_s, b_s = norm_backward(after_t, gains32[1], nn(grad_qk, feed.in_qk) + nn(grad_v, feed.in_v))
    grad_t = grad_s + part
    grad_branch_t = feed.tick("grad_t", grad_t.astype(BF16))
    grads["out_f"] = tn(projected_t, grad_branch_t).astype(BF16)
    grad_projected = nt(grad_branch_t, feed.out_f).astype(BF16)
    grads["out_t"] = tn(mixed_t, grad_projected).astype(BF16)
    grad_projected = feed.tick("out_t", grad_projected)
    grad_mixed_t = feed.tick("grad_mixed_t", nt(grad_projected, feed.out_t).astype(BF16))
    grad_project_t = attention_call(
        backward_kernel, 2, project_t + [cube(grad_mixed_t)], (3 * width,), True, patches
    )[0]
    grad_project_t = feed.tick("grad_project_t", flat(grad_project_t))
    grads["in_t"] = tn(grad_project_t, normed_t).astype(BF16)
    grad_project_t = feed.tick("in_t", grad_project_t)
    hook = lambda *sums: feed.tick("dx_t", *sums)
    part, g_t, b_t = norm_backward(start, gains32[0], nn(grad_project_t, feed.in_t), hook)
    grad_clip = (grad_t + part.astype(BF16).astype(F32)).astype(BF16)
    rows = (grad_projected, grad_branch_t, grad_branch_s, grad_pre, grad_low)
    grad_clip, *rows = feed.tick("grad_clip", grad_clip, *rows)
    sums = [g_t, g_s, g_m, b_t, b_s, b_m]
    clip, output = feed.tick("end", leave(grad_clip.reshape(shape)), output)
    return (output,) + feed.total(sums, rows, clip)


def shards(clips_in, cotangent, clip_live, weights_in, weights_out, norm_gain, shift_rows, dense_shift):
    both = ("dp", "seq")
    group = lax.axis_size("seq")
    count, _, patches, width = clips_in.shape
    own = count // group
    rows = -(-patches // SUB) * SUB
    gain_count = norm_gain.shape[0]
    shift_count = shift_rows.shape[0]
    staged = lax.axis_size(both) == 32 and group == 4 and weights_in.shape[0] == 240 and weights_out.shape[0] == 168

    def exchange(x):
        return lax.all_to_all(x, "seq", split_axis=0, concat_axis=1, tiled=True)

    def widen(x):
        return jnp.pad(x, ((0, 0), (0, 0), (0, rows - patches), (0, 0)))

    def leave(x):
        x = x[:, :, :patches]
        return lax.all_to_all(x, "seq", split_axis=1, concat_axis=0, tiled=True)

    packed = jnp.concatenate([norm_gain, shift_rows, dense_shift[None, :]], axis=0)
    feed = (Staged if staged else Whole)(both, weights_in, weights_out, packed, width, exchange(clips_in))
    clip = widen(feed.clip)
    if staged:
        clip = feed.begin(clip)
    live = lax.dynamic_slice(clip_live, (lax.axis_index("seq") * own,), (own,)).astype(BF16)

    def target(after):
        gradient = cotangent * 1
        if staged:
            gradient = tie(gradient, after)[0]
        return widen(exchange(gradient)) * live[:, None, None, None]

    output, grad_clip, summed_in, summed_out, owned = block(clip, target, leave, feed, gain_count, patches)
    return (
        output,
        grad_clip,
        summed_in,
        summed_out,
        owned[:gain_count],
        owned[gain_count : gain_count + shift_count],
        owned[-1],
    )


def solution(mesh):
    clip = P("dp", "seq", None, None)
    row = P(("dp", "seq"), None)
    col = P(None, ("dp", "seq"))
    flat = P(("dp", "seq"))
    return jax.shard_map(
        shards,
        mesh=mesh,
        in_specs=(clip, clip, P("dp"), row, row, col, col, flat),
        out_specs=(clip, clip, row, row, col, col, flat),
        check_vma=False,
    )
```
